32 devices in a mesh: sec: 2 (over y), row: 4 (over x, core), col: 4 (over z).
Axes of the slice: x: 2, y: 2, z: 4, core: 2. Of those that a mesh axis runs over, the one named last changes fastest.
Arguments:
- source: bfloat16 [32, 128, 512], P(None, ('sec', 'row'), 'col'), parts along dimension 1, may hold values from -6 to 6
- target: bfloat16 [32, 128, 512], P(None, ('sec', 'row'), 'col'), parts along dimension 1, may hold values from -6 to 6
- conv_weight: bfloat16 [3, 3, 32, 32], replicated, may hold values from -0.375 to 0.375
- flow_cotangent: float32 [2, 128, 512], P(None, ('sec', 'row'), 'col'), parts along dimension 1, may hold values from -6 to 6
Outputs:
- grad_source: bfloat16 [32, 128, 512], P(None, ('sec', 'row'), 'col'), parts along dimension 1
- grad_target: bfloat16 [32, 128, 512], P(None, ('sec', 'row'), 'col'), parts along dimension 1
- grad_weight: float32 [6, 3, 32, 32], P('sec'), parts along dimension 0
The draws below stay inside these ranges and needn't reach their ends.
There are 2 independent parts, one for each index of `sec`. The reference program is written for one: setup_inputs(seed, part) draws one part's arguments, and reference() takes and returns one part's arrays. A program takes and returns all parts, laid end to end along the dimension named above; an argument that names none is the same for every part. Nothing has to cross between parts.
All inputs are finite; a program needn't handle non-finite values.
Results may differ from the reference program's by a relative error of at most 0.011.
Values may be sent and summed in bfloat16 or wider, within the bound.
No kernel may reach another device: no remote copies, remote signals or barrier semaphores. Data moves between devices by JAX's collectives and lax.ppermute only.
A program may use at most 192 MiB of HBM per device.

```python
import math
import jax
import jax.numpy as jnp
from jax import lax

C = 32
RADIUS = 4
NH = 64
NW = 512


def block_levels(stream_key, shape, split, least, largest):
    factor_of, own = 1.0, jax.random.fold_in(stream_key, 6)
    for position, parts in split:
        heights = jnp.exp(jax.random.uniform(jax.random.fold_in(own, position), (parts,), jnp.float32, least / len(split), largest / len(split)))
        factor_of = factor_of * jnp.repeat(heights, shape[position] // parts).reshape([-1 if axis == position else 1 for axis in range(len(shape))])
    return factor_of


def scatter_about(rng, extent, deviation, limit, cuts=(), kind=jnp.bfloat16):
    drawn = jax.random.normal(rng, extent, jnp.float32) * deviation
    if len(cuts) > 0:
        drawn = block_levels(rng, extent, cuts, -0.22, 0.18) * drawn
    return jnp.clip(drawn, min=-limit, max=limit).astype(kind)


def setup_inputs(seed: int = 0, part: int = 0) -> dict:
    splits = jax.random.split(jax.random.key(seed), 5)
    part_keys = jax.random.split(jax.random.fold_in(splits[4], part), 5)
    source = scatter_about(part_keys[0], (C, NH, NW), 1.0, 6.0, ((1, 4), (2, 4)))
    target = scatter_about(part_keys[1], (C, NH, NW), 1.0, 6.0, ((1, 4), (2, 4)))
    conv_weight = scatter_about(splits[2], (3, 3, C, C), (9 * C) ** -0.5, 0.375)
    flow_cotangent = scatter_about(part_keys[3], (2, NH, NW), 1.0, 6.0, ((1, 4), (2, 4)), jnp.float32)
    return dict(source=source, target=target, conv_weight=conv_weight, flow_cotangent=flow_cotangent)


sharpness = 4.0

def unit_of(field):
    wide = field.astype(jnp.float32)
    recip = lax.rsqrt(lax.optimization_barrier(jnp.mean(wide * wide, axis=0)) + 1.0)
    return wide * recip

def unit_back(field, grad_unit):
    wide = field.astype(jnp.float32)
    recip = lax.rsqrt(lax.optimization_barrier(jnp.mean(wide * wide, axis=0)) + 1.0)
    inner = lax.optimization_barrier(jnp.sum(grad_unit * wide, axis=0))
    return recip * grad_unit - wide * (recip * recip * recip) * inner / field.shape[0]

def conv_valid(padded, kernel):
    result = lax.conv_general_dilated(padded[None], kernel, (1, 1), 'VALID', dimension_numbers=('NCHW', 'HWIO', 'NCHW'), preferred_element_type=jnp.float32)
    return result[0]

def volume_back(src_unit, tgt_ext, cotangent):
    channels, rows, cols = src_unit.shape
    span = 2 * RADIUS + 1
    scale = sharpness / math.sqrt(channels)
    scores = []
    for index in range(span * span):
        shift_a = index // span - RADIUS
        shift_b = index % span - RADIUS
        window = tgt_ext[:, RADIUS + shift_a:RADIUS + shift_a + rows, RADIUS + shift_b:RADIUS + shift_b + cols]
        scores.append(lax.optimization_barrier(jnp.sum(src_unit.astype(jnp.float32) * window.astype(jnp.float32), axis=0)) * scale)
    score = jnp.stack(scores)
    weight = jnp.exp(score)
    prob = weight / lax.optimization_barrier(jnp.sum(weight, axis=0))
    offsets = jnp.arange(span * span)
    off_a = (offsets // span - RADIUS).astype(jnp.float32)
    off_b = (offsets % span - RADIUS).astype(jnp.float32)
    expected = off_a[:, None, None] * cotangent[0] + off_b[:, None, None] * cotangent[1]
    base = lax.optimization_barrier(jnp.sum(prob * expected, axis=0))
    dscore = (prob * (expected - base) * scale).astype(jnp.bfloat16)
    grad_unit = jnp.zeros((channels, rows, cols), jnp.float32)
    for index in range(span * span):
        shift_a = index // span - RADIUS
        shift_b = index % span - RADIUS
        window = tgt_ext[:, RADIUS + shift_a:RADIUS + shift_a + rows, RADIUS + shift_b:RADIUS + shift_b + cols]
        grad_unit = grad_unit + dscore[index].astype(jnp.float32) * window.astype(jnp.float32)
    return (dscore, grad_unit)

def target_back(dscore_ext, unit_ext, rows, cols):
    span = 2 * RADIUS + 1
    grad_unit = jnp.zeros((unit_ext.shape[0], rows, cols), jnp.float32)
    for index in range(span * span):
        shift_a = index // span - RADIUS
        shift_b = index % span - RADIUS
        low_a = RADIUS - shift_a
        low_b = RADIUS - shift_b
        grad_unit = grad_unit + dscore_ext[index, low_a:low_a + rows, low_b:low_b + cols].astype(jnp.float32) * unit_ext[:, low_a:low_a + rows, low_b:low_b + cols].astype(jnp.float32)
    return grad_unit

def kernel_terms(src_pad, grad_feat):
    channels, rows, cols = grad_feat.shape
    flat_grad = grad_feat.reshape(channels, rows * cols)
    lines = []
    for tap_i in range(3):
        line = []
        for tap_j in range(3):
            shifted = src_pad[:, tap_i:tap_i + rows, tap_j:tap_j + cols].reshape(channels, rows * cols)
            line.append(lax.dot_general(shifted, flat_grad, (((1,), (1,)), ((), ())), preferred_element_type=jnp.float32))
        lines.append(jnp.stack(line))
    return jnp.stack(lines)

def reference(source, target, conv_weight, flow_cotangent):
    channels, rows, cols = source.shape
    pad_one = ((0, 0), (1, 1), (1, 1))
    pad_far = ((0, 0), (RADIUS, RADIUS), (RADIUS, RADIUS))
    src_pad = jnp.pad(source, pad_one)
    feat = conv_valid(src_pad, conv_weight).astype(jnp.bfloat16)
    src_unit = unit_of(feat).astype(jnp.bfloat16)
    tgt_unit = unit_of(target).astype(jnp.bfloat16)
    dscore, grad_src_unit = volume_back(src_unit, jnp.pad(tgt_unit, pad_far), flow_cotangent)
    grad_tgt_unit = target_back(jnp.pad(dscore, pad_far), jnp.pad(src_unit, pad_far), rows, cols)
    grad_feat = unit_back(feat, grad_src_unit).astype(jnp.bfloat16)
    grad_target = unit_back(target, grad_tgt_unit).astype(jnp.bfloat16)
    flipped = jnp.transpose(conv_weight[::-1, ::-1], (0, 1, 3, 2))
    grad_source = conv_valid(jnp.pad(grad_feat, pad_one), flipped).astype(jnp.bfloat16)
    grad_weight = kernel_terms(src_pad, grad_feat) / math.sqrt(rows * cols)
    return (grad_source, grad_target, grad_weight)
```

```python
import functools
import math

import jax
import jax.numpy as jnp
from jax import lax
from jax.experimental import pallas as pl
from jax.experimental.pallas import tpu as pltpu
from jax.sharding import PartitionSpec as P

RADIUS = 4
SHARPNESS = 4.0
CH = 32
QUAD = 4
LANES = QUAD * CH
GROUP = 32
HALO = 2 * RADIUS
F32 = jnp.float32
BF16 = jnp.bfloat16


def lane_group(shape):
    return lax.broadcasted_iota(jnp.int32, shape, len(shape) - 1) // CH


def by_group(values):
    lane = lax.broadcasted_iota(jnp.int32, values[0].shape, values[0].ndim - 1)
    low = jnp.where(lane < CH, values[0], values[1])
    high = jnp.where(lane < 3 * CH, values[2], values[3])
    return jnp.where(lane < 2 * CH, low, high)


def roll_groups(value, steps):
    steps = steps % QUAD
    if steps == 0:
        return value
    return pltpu.roll(value, steps * CH, value.ndim - 1)


def group_sum(value, ones):
    high = value.astype(BF16)
    low = (value - high.astype(F32)).astype(BF16)
    both = jnp.concatenate([high, low], axis=1)
    return jnp.dot(both, ones, preferred_element_type=F32)


def group_ones():
    row = lax.broadcasted_iota(jnp.int32, (2 * LANES, LANES), 0) % LANES
    col = lax.broadcasted_iota(jnp.int32, (2 * LANES, LANES), 1)
    return jnp.where(row // CH == col // CH, 1.0, 0.0).astype(BF16)


def even(axis):
    return lax.rem(lax.axis_index(axis), 2) == 0


def pack_kernel(src_ref, tgt_ref, flow_ref, own_ref, fl_ref, sa_ref, sb_ref, wide_ref):
    channels, rows, cols = src_ref.shape
    quads = rows // QUAD
    for base, ref in ((0, tgt_ref), (quads, src_ref)):
        wide_ref[...] = ref[...].astype(F32).reshape(channels * rows, cols)
        for q in range(quads):
            part = jnp.concatenate(
                [wide_ref[pl.ds(q * QUAD + i, channels, stride=rows), :] for i in range(QUAD)],
                axis=0,
            )
            own_ref[base + q] = part.T.astype(BF16)
    pieces = []
    for f in range(2):
        value = flow_ref[f]
        high = value.astype(BF16).astype(F32)
        pieces += [high, value - high]
    fl_ref[...] = jnp.concatenate(pieces, axis=0).astype(BF16)
    is_even = even("row")
    last = quads - HALO // QUAD
    for dst, first in (
        (sa_ref, jnp.where(is_even, last, 0)),
        (sb_ref, jnp.where(is_even, 0, last)),
    ):
        for k in range(HALO // QUAD):
            dst[k * cols : (k + 1) * cols] = own_ref[first + k]
            dst[(2 + k) * cols : (3 + k) * cols] = own_ref[quads + first + k]
    top = jnp.concatenate([p[:HALO] for p in pieces], axis=0)
    low = jnp.concatenate([p[rows - HALO :] for p in pieces], axis=0)
    sa_ref[4 * cols :] = jnp.where(is_even, low, top).astype(BF16)
    sb_ref[4 * cols :] = jnp.where(is_even, top, low).astype(BF16)


def pick(flag, first, second):
    return jnp.where(flag, first.astype(F32), second.astype(F32))


def strip_kernel(own_ref, fl_ref, ra_ref, rb_ref, sc_ref, sd_ref, wide_ref):
    planes, cols, _ = own_ref.shape
    quads = planes // 2
    rows = quads * QUAD
    r_even = even("row")
    c_even = even("col")

    def strips(read):
        return read(0, 2 * HALO)[:HALO], read(cols - 2 * HALO, 2 * HALO)[HALO:]

    for kind in range(2):
        for q in range(quads + 4):
            if 2 <= q < quads + 2:
                plane = kind * quads + q - 2
                left, right = strips(lambda at, n: own_ref[plane, at : at + n].astype(F32))
            else:
                down = q >= quads + 2
                at0 = (2 * kind + (q - quads - 2 if down else q)) * cols
                flag = r_even if down else jnp.logical_not(r_even)
                left, right = strips(
                    lambda at, n: pick(
                        flag, ra_ref[at0 + at : at0 + at + n], rb_ref[at0 + at : at0 + at + n]
                    )
                )
            row = (kind * (quads + 4) + q) * HALO
            wide_ref[0, row : row + HALO] = jnp.where(c_even, right, left)
            wide_ref[1, row : row + HALO] = jnp.where(c_even, left, right)
    count = 2 * (quads + 4) * HALO
    sc_ref[:count] = wide_ref[0].astype(BF16)
    sd_ref[:count] = wide_ref[1].astype(BF16)
    a, b = (ra_ref[4 * cols :], rb_ref[4 * cols :])
    up, down = (pick(r_even, b, a), pick(r_even, a, b))
    flow = []
    own = fl_ref[...].astype(F32)
    for v in range(4):
        flow += [
            up[v * HALO : (v + 1) * HALO],
            own[v * rows : (v + 1) * rows],
            down[v * HALO : (v + 1) * HALO],
        ]
    flow = jnp.concatenate(flow, axis=0).astype(BF16)
    sc_ref[count:] = flow
    sd_ref[count:] = flow


def fill_taps(dst_ref, w_ref):
    zero = jnp.zeros((CH, CH), F32)
    for dx in range(3):
        for block in range(2 * QUAD):
            row = block if block < QUAD else {QUAD: QUAD, 2 * QUAD - 1: -1}.get(block)
            parts = []
            for out in range(QUAD):
                tap = None if row is None else row - out + 1
                ok = tap is not None and 0 <= tap < 3
                parts.append(w_ref[tap, dx].astype(F32) if ok else zero)
            dst_ref[dx, block * CH : (block + 1) * CH, :] = jnp.concatenate(parts, axis=1).astype(
                BF16
            )


def taps_of(ref, quad, start, count):
    main = ref[quad, pl.ds(start, count), :]
    after = ref[quad + 1, pl.ds(start, count), :]
    before = ref[quad - 1, pl.ds(start, count), :]
    lane = lax.broadcasted_iota(jnp.int32, main.shape, 1)
    beside = jnp.where(lane < 2 * CH, after, before)
    return jnp.concatenate([main, beside], axis=1).astype(BF16)


def conv(ref, quad, start, count, w_ref):
    total = jnp.zeros((count, LANES), F32)
    for dx in range(3):
        total += jnp.dot(
            taps_of(ref, quad, start + dx - 1, count), w_ref[dx], preferred_element_type=F32
        )
    return total


def assemble(et_ref, es_ref, own_ref, ra_ref, rb_ref, rc_ref, rd_ref):
    planes, cols, _ = own_ref.shape
    quads = planes // 2
    r_even = even("row")
    c_even = even("col")
    width = et_ref.shape[1]
    for kind, dst in ((0, et_ref), (1, es_ref)):
        for q in range(quads + 4):
            if 2 <= q < quads + 2:
                middle = own_ref[kind * quads + q - 2].astype(F32)
            else:
                down = q >= quads + 2
                at = (2 * kind + (q - quads - 2 if down else q)) * cols
                flag = r_even if down else jnp.logical_not(r_even)
                middle = pick(flag, ra_ref[at : at + cols], rb_ref[at : at + cols])
            dst[q, HALO : HALO + cols] = middle
            dst[q, 2 * HALO + cols :] = jnp.zeros((width - cols - 2 * HALO, LANES), F32)
    for pair in range(quads + 4):
        at = pair * 2 * HALO
        c, d = (rc_ref[at : at + 2 * HALO], rd_ref[at : at + 2 * HALO])
        left, right = (pick(c_even, d, c), pick(c_even, c, d))
        for k in range(2):
            kind, q = divmod(2 * pair + k, quads + 4)
            dst = (et_ref, es_ref)[kind]
            dst[q, :HALO] = left[k * HALO : (k + 1) * HALO]
            dst[q, HALO + cols : 2 * HALO + cols] = right[k * HALO : (k + 1) * HALO]


def flow_rows(p_ref, fl_ref, ra_ref, rb_ref, rc_ref, rd_ref, groups, cols, rows):
    r_even = even("row")
    c_even = even("col")
    ext = rows + 2 * HALO
    a, b = (ra_ref[4 * cols :], rb_ref[4 * cols :])
    up, down = (pick(r_even, b, a), pick(r_even, a, b))
    base = rc_ref.shape[0] - 4 * ext
    c, d = (rc_ref[base:], rd_ref[base:])
    left, right = (pick(c_even, d, c), pick(c_even, c, d))
    own = fl_ref[...].astype(F32)
    lane = lax.broadcasted_iota(jnp.int32, (ext, LANES), 1)
    row = lax.broadcasted_iota(jnp.int32, (ext, LANES), 0)
    for f in range(2):
        mid = jnp.zeros((ext, cols), F32)
        side = [jnp.zeros((ext, cols), F32)] * 2
        for part in range(2):
            v = 2 * f + part
            mid = mid + jnp.concatenate(
                [
                    up[v * HALO : (v + 1) * HALO],
                    own[v * rows : (v + 1) * rows],
                    down[v * HALO : (v + 1) * HALO],
                ],
                axis=0,
            )
            side = [s + x[v * ext : (v + 1) * ext] for s, x in zip(side, (left, right))]
        lf, md, rt = (pltpu.roll(x, RADIUS, 1) for x in (side[0], mid, side[1]))
        tiles = [
            jnp.where(lane < RADIUS, lf, md),
            jnp.where(lane < RADIUS, md, jnp.where(lane < 2 * RADIUS, rt, 0.0)),
        ]
        for g in range(groups):
            tile = tiles[g // QUAD]
            total = jnp.zeros((ext, LANES), F32)
            for i in range(QUAD):
                keep = jnp.logical_and(row % QUAD == i, lane // CH == i)
                total = total + jnp.where(keep, roll_groups(tile, i - g), 0.0)
            p_ref[f, g] = total


def block_mask(m_ref):
    span = 3 * QUAD
    key = lax.broadcasted_iota(jnp.int32, (span, 16, LANES), 0)
    kx = lax.broadcasted_iota(jnp.int32, (span, 16, LANES), 1)
    lane = lax.broadcasted_iota(jnp.int32, (span, 16, LANES), 2)
    dy = key - lane // CH
    dx = kx - lane % 8
    ok = (dy >= 0) & (dy <= 2 * RADIUS) & (dx >= 0) & (dx <= 2 * RADIUS)
    m_ref[...] = jnp.where(ok, 1.0, 0.0)


def softmax_block(score, m_ref, f0, f1, scale):
    span = 3 * QUAD
    lane = lax.broadcasted_iota(jnp.int32, (16, LANES), 1)
    at_y = (lane // CH + RADIUS).astype(F32)
    at_x = (lane % 8 + RADIUS).astype(F32)
    key_x = lax.broadcasted_iota(jnp.int32, (16, LANES), 0).astype(F32)
    f0 = jnp.broadcast_to(f0, (16, LANES))
    f1 = jnp.broadcast_to(f1, (16, LANES))
    side = f1 * (key_x - at_x) - f0 * at_y
    weights = []
    total = jnp.zeros((16, LANES), F32)
    lean = jnp.zeros((16, LANES), F32)
    for y in range(span):
        weight = jnp.exp2(score[16 * y : 16 * (y + 1)] * (scale * math.log2(math.e))) * m_ref[y]
        weights.append(weight)
        total = total + weight
        lean = lean + weight * (f0 * float(y) + side)
    total = jnp.sum(total, axis=0, keepdims=True)
    lean = jnp.sum(lean, axis=0, keepdims=True)
    base = jnp.broadcast_to(lean / total, (16, LANES))
    factor = jnp.broadcast_to(scale / total, (16, LANES))
    step = f0 * factor
    side = (side - base) * factor
    return jnp.concatenate(
        [(weights[y] * (step * float(y) + side)).astype(BF16) for y in range(span)], axis=0
    )


def unit_grad(field, recip, grad, ones):
    inner = group_sum(grad * field, ones)
    return recip * grad - field * (recip * recip * recip) * inner * (1.0 / CH)


def spread(dst_ref, quad, value, channels, rows):
    flipped = value.T
    for i in range(QUAD):
        dst_ref[pl.ds(quad * QUAD + i, channels, stride=rows), :] = flipped[
            i * CH : (i + 1) * CH
        ]


def main_kernel(
    own_ref, fl_ref, ra_ref, rb_ref, rc_ref, rd_ref, w_ref, wt_ref,
    gs_out, gt_out, gw_out,
    et_ref, es_ref, t4_ref, q_ref, ga_ref, rt_ref, fe_ref, rf_ref, gu_ref, p_ref, m_ref,
    taps_ref, back_ref, wide_ref,
):
    channels, rows, cols = gs_out.shape
    quads = rows // QUAD
    ext = quads + 4
    width = et_ref.shape[1]
    asked = quads + 2
    groups = q_ref.shape[1]
    wide = groups * GROUP
    scale = SHARPNESS / math.sqrt(channels)
    ones = group_ones()

    fill_taps(taps_ref, w_ref)
    fill_taps(back_ref, wt_ref)
    block_mask(m_ref)
    assemble(et_ref, es_ref, own_ref, ra_ref, rb_ref, rc_ref, rd_ref)
    flow_rows(p_ref, fl_ref, ra_ref, rb_ref, rc_ref, rd_ref, groups, cols, rows)

    def target_unit(q, carry):
        field = et_ref[q]
        recip = lax.rsqrt(group_sum(field * field, ones) * (1.0 / CH) + 1.0)
        rt_ref[q] = recip
        unit = (field * recip).astype(BF16).astype(F32)
        turned = [roll_groups(unit, k) for k in range(QUAD)]
        for i in range(QUAD):
            for g in range(groups):
                at = g * GROUP
                t4_ref[g, q * QUAD + i] = by_group(
                    [
                        turned[(j - i) % QUAD][at + 8 * j : at + 8 * j + 16]
                        for j in range(QUAD)
                    ]
                ).astype(BF16)
        return carry

    lax.fori_loop(0, ext, target_unit, 0)

    def source_unit(n, carry):
        feat = conv(es_ref, n + 1, RADIUS, wide, taps_ref).astype(BF16).astype(F32)
        fe_ref[n] = feat
        recip = lax.rsqrt(group_sum(feat * feat, ones) * (1.0 / CH) + 1.0)
        rf_ref[n] = recip
        unit = (feat * recip).astype(BF16).astype(F32)
        group = lane_group((8, LANES))
        for g in range(groups):
            octs = [unit[g * GROUP + 8 * j : g * GROUP + 8 * j + 8] for j in range(QUAD)]
            turned = [
                roll_groups(by_group([octs[(i + k) % QUAD] for i in range(QUAD)]), k)
                for k in range(QUAD)
            ]
            parts = [
                jnp.where(group == j, turned[(j - i) % QUAD], 0.0)
                for i in range(QUAD)
                for j in range(QUAD)
            ]
            q_ref[n, g] = jnp.concatenate(parts, axis=0).astype(BF16)
        return carry

    lax.fori_loop(0, asked, source_unit, 0)

    ga_ref[...] = jnp.zeros_like(ga_ref)

    def block(n, carry):
        for g in range(groups):
            queries = q_ref[n, g]
            keys = t4_ref[g, pl.ds(n * QUAD, 3 * QUAD)].reshape(3 * QUAD * 16, LANES)
            score = lax.dot_general(
                keys, queries, (((1,), (1,)), ((), ())), preferred_element_type=F32
            )
            at = pl.ds((n + 1) * QUAD, QUAD)
            f0 = jnp.sum(p_ref[0, g, at, :], axis=0, keepdims=True)
            f1 = jnp.sum(p_ref[1, g, at, :], axis=0, keepdims=True)
            dscore = softmax_block(score, m_ref, f0, f1, scale)
            to_keys = jnp.dot(dscore, queries, preferred_element_type=F32)
            here = (g, pl.ds(n * QUAD, 3 * QUAD))
            ga_ref[here] = ga_ref[here] + to_keys.reshape(3 * QUAD, 16, LANES)
            mine = lax.dot_general(
                dscore, keys, (((0,), (0,)), ((), ())), preferred_element_type=F32
            )

            def piece(i, j):
                at = i * GROUP + 8 * j
                return mine[at : at + 8]

            turned = [
                roll_groups(by_group([piece((j + k) % QUAD, j) for j in range(QUAD)]), k)
                for k in range(QUAD)
            ]
            for j in range(QUAD):
                at = g * GROUP + 8 * j
                gu_ref[n, at : at + 8] = by_group(
                    [turned[(i - j) % QUAD] for i in range(QUAD)]
                )
        return carry

    lax.fori_loop(0, asked, block, 0)

    def feature_grad(n, carry):
        value = unit_grad(fe_ref[n], rf_ref[n], gu_ref[n], ones)
        gu_ref[n] = value.astype(BF16).astype(F32)
        return carry

    lax.fori_loop(0, asked, feature_grad, 0)

    totals = []
    for dx in range(3):
        total = jnp.zeros((LANES, 2 * LANES), F32)
        for q in range(quads):
            grad = gu_ref[q + 1, RADIUS : RADIUS + cols].astype(BF16)
            total += lax.dot_general(
                grad,
                taps_of(es_ref, q + 2, HALO + dx - 1, cols),
                (((0,), (0,)), ((), ())),
                preferred_element_type=F32,
            )
        totals.append(total)
    lane = lax.broadcasted_iota(jnp.int32, (CH, LANES), 1)
    for dx, total in enumerate(totals):
        rows_of = [total[i * CH : (i + 1) * CH] for i in range(QUAD)]
        main = [x[:, :LANES] for x in rows_of]
        beside = [x[:, LANES:] for x in rows_of]
        first = jnp.where(lane < CH, roll_groups(beside[0], 1), roll_groups(main[0], 1))
        last = jnp.where(lane < 2 * CH, roll_groups(main[3], 2), roll_groups(beside[3], 2))
        gw_out[dx * CH : (dx + 1) * CH] = (first + main[1]) + (roll_groups(main[2], 3) + last)

    def source_grad(q, carry):
        spread(wide_ref, q, conv(gu_ref, q + 1, RADIUS, cols, back_ref), channels, rows)
        return carry

    lax.fori_loop(0, quads, source_grad, 0)
    gs_out[...] = wide_ref[...].astype(BF16).reshape(channels, rows, cols)

    def target_grad(q, carry):
        parts = []
        base = (q + 2) * QUAD
        for oct in range(1, cols // 8 + 1):
            g0, j0 = divmod(oct, QUAD)
            g1, j1 = divmod(oct - 1, QUAD)
            group = lane_group((8, LANES))
            total = None
            for k in range(QUAD):
                one = ga_ref[g0, base + (j0 + k) % QUAD, 0:8, :]
                two = ga_ref[g1, base + (j1 + k) % QUAD, 8:16, :]
                both = jnp.where(group == j0, one, jnp.where(group == j1, two, 0.0))
                both = roll_groups(both, k)
                total = both if total is None else total + both
            parts.append(total)
        grad = jnp.concatenate(parts, axis=0)
        at = slice(HALO, HALO + cols)
        value = unit_grad(et_ref[q + 2, at], rt_ref[q + 2, at], grad, ones)
        spread(wide_ref, q, value, channels, rows)
        return carry

    lax.fori_loop(0, quads, target_grad, 0)
    gt_out[...] = wide_ref[...].astype(BF16).reshape(channels, rows, cols)


def pair_exchange(x, y, axis):
    size = lax.axis_size(axis)
    near = [(i, i ^ 1) for i in range(size)]
    far = []
    for i in range(1, size - 1, 2):
        far += [(i, i + 1), (i + 1, i)]
    return lax.ppermute(x, axis, near), lax.ppermute(y, axis, far)


def sum_over(x, axis):
    size = lax.axis_size(axis)
    step = 1
    while step < size:
        x = x + lax.ppermute(x, axis, [(i, i ^ step) for i in range(size)])
        step *= 2
    return x


def vmem(count):
    return [pl.BlockSpec(memory_space=pltpu.VMEM)] * count


def per_device(source, target, conv_weight, flow_cotangent):
    channels, rows, cols = source.shape
    quads = rows // QUAD
    ext = quads + 4
    groups = -(-(cols + HALO) // GROUP)
    wide = groups * GROUP
    width = wide + HALO
    asked = quads + 2
    flipped = jnp.transpose(conv_weight[::-1, ::-1], (0, 1, 3, 2))
    shape = jax.ShapeDtypeStruct
    side = shape((4 * cols + 4 * HALO, LANES), BF16)
    own, flow, to_a, to_b = pl.pallas_call(
        pack_kernel,
        out_shape=(
            shape((2 * quads, cols, LANES), BF16),
            shape((4 * rows, cols), BF16),
            side,
            side,
        ),
        in_specs=vmem(3),
        out_specs=tuple(vmem(4)),
        scratch_shapes=[pltpu.VMEM((channels * rows, cols), F32)],
        name="pack",
    )(source, target, flow_cotangent)
    ra, rb = pair_exchange(to_a, to_b, "row")
    strip = shape((2 * ext * HALO + 4 * ext * QUAD, LANES), BF16)
    to_c, to_d = pl.pallas_call(
        strip_kernel,
        out_shape=(strip, strip),
        in_specs=vmem(4),
        out_specs=tuple(vmem(2)),
        scratch_shapes=[pltpu.VMEM((2, 2 * ext * HALO, LANES), F32)],
        name="strip",
    )(own, flow, ra, rb)
    rc, rd = pair_exchange(to_c, to_d, "col")
    scratch = lambda *dims, dtype=F32: pltpu.VMEM(dims, dtype)
    grad_source, grad_target, terms = pl.pallas_call(
        main_kernel,
        out_shape=(
            shape(source.shape, BF16),
            shape(target.shape, BF16),
            shape((3 * CH, LANES), F32),
        ),
        in_specs=vmem(8),
        out_specs=tuple(vmem(3)),
        scratch_shapes=[
            scratch(ext, width, LANES),
            scratch(ext, width, LANES),
            scratch(groups, ext * QUAD, 16, LANES, dtype=BF16),
            scratch(asked, groups, LANES, LANES, dtype=BF16),
            scratch(groups, ext * QUAD, 16, LANES),
            scratch(ext, width, LANES),
            scratch(asked, wide, LANES),
            scratch(asked, wide, LANES),
            scratch(asked, wide, LANES),
            scratch(2, groups, ext * QUAD, LANES),
            scratch(3 * QUAD, 16, LANES),
            scratch(3, 2 * LANES, LANES, dtype=BF16),
            scratch(3, 2 * LANES, LANES, dtype=BF16),
            scratch(channels * rows, cols),
        ],
        name="main",
    )(own, flow, ra, rb, rc, rd, conv_weight, flipped)
    pixels = rows * cols * lax.axis_size("row") * lax.axis_size("col")
    terms = sum_over(sum_over(terms, "row"), "col") / math.sqrt(pixels)
    terms = terms.reshape(3, CH, QUAD, CH)[:, :, :3]
    return (grad_source, grad_target, jnp.transpose(terms, (2, 0, 3, 1)))


def solution(mesh):
    placed = (
        P(None, ("sec", "row"), "col"),
        P(None, ("sec", "row"), "col"),
        P(),
        P(None, ("sec", "row"), "col"),
    )
    return jax.shard_map(
        per_device,
        mesh=mesh,
        in_specs=placed,
        out_specs=(
            P(None, ("sec", "row"), "col"),
            P(None, ("sec", "row"), "col"),
            P("sec", None, None, None),
        ),
        check_vma=False,
    )
```

```python
import functools
import math

import jax
import jax.numpy as jnp
from jax import lax
from jax.experimental import pallas as pl
from jax.experimental.pallas import tpu as pltpu
from jax.sharding import PartitionSpec as P

RADIUS = 4
SHARPNESS = 4.0
CH = 32
QUAD = 4
LANES = QUAD * CH
GROUP = 32
HALO = 2 * RADIUS
F32 = jnp.float32
BF16 = jnp.bfloat16


def lane_group(shape):
    return lax.broadcasted_iota(jnp.int32, shape, len(shape) - 1) // CH


def by_group(values):
    lane = lax.broadcasted_iota(jnp.int32, values[0].shape, values[0].ndim - 1)
    low = jnp.where(lane < CH, values[0], values[1])
    high = jnp.where(lane < 3 * CH, values[2], values[3])
    return jnp.where(lane < 2 * CH, low, high)


def roll_groups(value, steps):
    steps = steps % QUAD
    if steps == 0:
        return value
    return pltpu.roll(value, steps * CH, value.ndim - 1)


def group_sum(value, ones):
    high = value.astype(BF16)
    low = (value - high.astype(F32)).astype(BF16)
    both = jnp.concatenate([high, low], axis=1)
    return jnp.dot(both, ones, preferred_element_type=F32)


def group_ones():
    row = lax.broadcasted_iota(jnp.int32, (2 * LANES, LANES), 0) % LANES
    col = lax.broadcasted_iota(jnp.int32, (2 * LANES, LANES), 1)
    return jnp.where(row // CH == col // CH, 1.0, 0.0).astype(BF16)


def even(axis):
    return lax.rem(lax.axis_index(axis), 2) == 0


def pack_kernel(src_ref, tgt_ref, flow_ref, own_ref, fl_ref, sa_ref, sb_ref, wide_ref):
    channels, rows, cols = src_ref.shape
    quads = rows // QUAD
    for base, ref in ((0, tgt_ref), (quads, src_ref)):
        wide_ref[...] = ref[...].astype(F32).reshape(channels * rows, cols)
        for q in range(quads):
            part = jnp.concatenate(
                [wide_ref[pl.ds(q * QUAD + i, channels, stride=rows), :] for i in range(QUAD)],
                axis=0,
            )
            own_ref[base + q] = part.T.astype(BF16)
    pieces = []
    for f in range(2):
        value = flow_ref[f]
        high = value.astype(BF16).astype(F32)
        pieces += [high, value - high]
    fl_ref[...] = jnp.concatenate(pieces, axis=0).astype(BF16)
    is_even = even("row")
    last = quads - HALO // QUAD
    for dst, first in (
        (sa_ref, jnp.where(is_even, last, 0)),
        (sb_ref, jnp.where(is_even, 0, last)),
    ):
        for k in range(HALO // QUAD):
            dst[k * cols : (k + 1) * cols] = own_ref[first + k]
            dst[(2 + k) * cols : (3 + k) * cols] = own_ref[quads + first + k]
    top = jnp.concatenate([p[:HALO] for p in pieces], axis=0)
    low = jnp.concatenate([p[rows - HALO :] for p in pieces], axis=0)
    sa_ref[4 * cols :] = jnp.where(is_even, low, top).astype(BF16)
    sb_ref[4 * cols :] = jnp.where(is_even, top, low).astype(BF16)


def pick(flag, first, second):
    return jnp.where(flag, first.astype(F32), second.astype(F32))


def strip_kernel(own_ref, fl_ref, ra_ref, rb_ref, sc_ref, sd_ref, wide_ref):
    planes, cols, _ = own_ref.shape
    quads = planes // 2
    rows = quads * QUAD
    r_even = even("row")
    c_even = even("col")

    def strips(read):
        return read(0, 2 * HALO)[:HALO], read(cols - 2 * HALO, 2 * HALO)[HALO:]

    for kind in range(2):
        for q in range(quads + 4):
            if 2 <= q < quads + 2:
                plane = kind * quads + q - 2
                left, right = strips(lambda at, n: own_ref[plane, at : at + n].astype(F32))
            else:
                down = q >= quads + 2
                at0 = (2 * kind + (q - quads - 2 if down else q)) * cols
                flag = r_even if down else jnp.logical_not(r_even)
                left, right = strips(
                    lambda at, n: pick(
                        flag, ra_ref[at0 + at : at0 + at + n], rb_ref[at0 + at : at0 + at + n]
                    )
                )
            row = (kind * (quads + 4) + q) * HALO
            wide_ref[0, row : row + HALO] = jnp.where(c_even, right, left)
            wide_ref[1, row : row + HALO] = jnp.where(c_even, left, right)
    count = 2 * (quads + 4) * HALO
    sc_ref[:count] = wide_ref[0].astype(BF16)
    sd_ref[:count] = wide_ref[1].astype(BF16)
    a, b = (ra_ref[4 * cols :], rb_ref[4 * cols :])
    up, down = (pick(r_even, b, a), pick(r_even, a, b))
    flow = []
    own = fl_ref[...].astype(F32)
    for v in range(4):
        flow += [
            up[v * HALO : (v + 1) * HALO],
            own[v * rows : (v + 1) * rows],
            down[v * HALO : (v + 1) * HALO],
        ]
    flow = jnp.concatenate(flow, axis=0).astype(BF16)
    sc_ref[count:] = flow
    sd_ref[count:] = flow


def fill_taps(dst_ref, w_ref):
    zero = jnp.zeros((CH, CH), F32)
    for dx in range(3):
        for block in range(2 * QUAD):
            row = block if block < QUAD else {QUAD: QUAD, 2 * QUAD - 1: -1}.get(block)
            parts = []
            for out in range(QUAD):
                tap = None if row is None else row - out + 1
                ok = tap is not None and 0 <= tap < 3
                parts.append(w_ref[tap, dx].astype(F32) if ok else zero)
            dst_ref[dx, block * CH : (block + 1) * CH, :] = jnp.concatenate(parts, axis=1).astype(
                BF16
            )


def taps_of(ref, quad, start, count):
    main = ref[quad, pl.ds(start, count), :]
    after = ref[quad + 1, pl.ds(start, count), :]
    before = ref[quad - 1, pl.ds(start, count), :]
    lane = lax.broadcasted_iota(jnp.int32, main.shape, 1)
    beside = jnp.where(lane < 2 * CH, after, before)
    return jnp.concatenate([main, beside], axis=1).astype(BF16)


def conv(ref, quad, start, count, w_ref):
    total = jnp.zeros((count, LANES), F32)
    for dx in range(3):
        total += jnp.dot(
            taps_of(ref, quad, start + dx - 1, count), w_ref[dx], preferred_element_type=F32
        )
    return total


SPAN = 3 * QUAD
KEYS = 16


def halo_plane(kind, q, own_ref, ra_ref, rb_ref):
    planes, cols, _ = own_ref.shape
    quads = planes // 2
    if 2 <= q < quads + 2:
        return own_ref[kind * quads + q - 2].astype(F32)
    down = q >= quads + 2
    at = (2 * kind + (q - quads - 2 if down else q)) * cols
    flag = even("row") if down else jnp.logical_not(even("row"))
    return pick(flag, ra_ref[at : at + cols], rb_ref[at : at + cols])


def sides_of(rc, rd):
    flag = even("col")
    return pick(flag, rd, rc), pick(flag, rc, rd)


def edge_plane(kind, q, side, own_ref, ra_ref, rb_ref, rc_ref, rd_ref):
    planes, cols, _ = own_ref.shape
    quads = planes // 2
    tile = slice(0, KEYS) if side == 0 else slice(cols - KEYS, cols)
    if 2 <= q < quads + 2:
        mine = own_ref[kind * quads + q - 2, tile].astype(F32)
    else:
        down = q >= quads + 2
        at = (2 * kind + (q - quads - 2 if down else q)) * cols
        tile = slice(at + tile.start, at + tile.stop)
        flag = even("row") if down else jnp.logical_not(even("row"))
        mine = pick(flag, ra_ref[tile], rb_ref[tile])
    index = kind * (quads + 4) + q
    at = index // 2 * 2 * HALO
    fetched = sides_of(rc_ref[at : at + 2 * HALO], rd_ref[at : at + 2 * HALO])[side]
    fetched = fetched[index % 2 * HALO : index % 2 * HALO + HALO]
    parts = [fetched, mine[:HALO]] if side == 0 else [mine[HALO:], fetched]
    return jnp.concatenate(parts, axis=0)


def flow_mid(f, fl_ref, ra_ref, rb_ref):
    cols = fl_ref.shape[1]
    rows = fl_ref.shape[0] // 4
    a, b = (ra_ref[4 * cols :], rb_ref[4 * cols :])
    flag = even("row")
    up, down = (pick(flag, b, a), pick(flag, a, b))
    total = None
    for v in (2 * f, 2 * f + 1):
        part = jnp.concatenate(
            [
                up[v * HALO : (v + 1) * HALO],
                fl_ref[v * rows : (v + 1) * rows].astype(F32),
                down[v * HALO : (v + 1) * HALO],
            ],
            axis=0,
        )
        total = part if total is None else total + part
    return total


def flow_inner(p_ref, fl_ref, ra_ref, rb_ref):
    groups = p_ref.shape[1]
    for f in range(2):
        mid = pltpu.roll(flow_mid(f, fl_ref, ra_ref, rb_ref), LANES - RADIUS, 1)
        lane = lax.broadcasted_iota(jnp.int32, mid.shape, 1)
        row = lax.broadcasted_iota(jnp.int32, mid.shape, 0)
        mid = jnp.where(lane < LANES - 8, mid, 0.0)
        turned = [roll_groups(mid, k) for k in range(QUAD)]
        for g in range(groups):
            total = jnp.zeros(mid.shape, F32)
            for i in range(QUAD):
                keep = jnp.logical_and(row % QUAD == i, lane // CH == i)
                total = jnp.where(keep, turned[(i - g) % QUAD], total)
            p_ref[f, g] = total


def flow_edge(e_ref, fl_ref, ra_ref, rb_ref, rc_ref, rd_ref):
    rows = fl_ref.shape[0] // 4
    ext = rows + 2 * HALO
    base = rc_ref.shape[0] - 4 * ext
    left, right = sides_of(rc_ref[base:], rd_ref[base:])
    for f in range(2):
        mid = flow_mid(f, fl_ref, ra_ref, rb_ref)
        at = 2 * f * ext
        lf = left[at : at + ext] + left[at + ext : at + 2 * ext]
        rt = right[at : at + ext] + right[at + ext : at + 2 * ext]
        lane = lax.broadcasted_iota(jnp.int32, mid.shape, 1)
        row = lax.broadcasted_iota(jnp.int32, mid.shape, 0)
        low = jnp.where(lane < RADIUS, pltpu.roll(lf, RADIUS, 1), pltpu.roll(mid, RADIUS, 1))
        high = jnp.where(
            lane < 3 * RADIUS, pltpu.roll(mid, 3 * RADIUS, 1), pltpu.roll(rt, 3 * RADIUS, 1)
        )
        both = jnp.where(lane < 8, low, high)
        for h in range(2):
            total = jnp.zeros(mid.shape, F32)
            for i in range(QUAD):
                turn = i * CH + h * 16
                keep = jnp.logical_and(row % QUAD == i, lane // 16 == 2 * i + h)
                total = jnp.where(keep, pltpu.roll(both, turn, 1) if turn else both, total)
            e_ref[f, h] = total


def fill_mask(m_ref):
    key = lax.broadcasted_iota(jnp.int32, (SPAN, KEYS, LANES), 0)
    kx = lax.broadcasted_iota(jnp.int32, (SPAN, KEYS, LANES), 1)
    lane = lax.broadcasted_iota(jnp.int32, (SPAN, KEYS, LANES), 2)
    dy = key - lane // CH
    dx = kx - lane % 8
    ok = (dy >= 0) & (dy <= 2 * RADIUS) & (dx >= 0) & (dx <= 2 * RADIUS)
    m_ref[...] = jnp.where(ok, 1.0, 0.0)


def softmax_block(score_ref, m_ref, f0, f1, scale):
    lane = lax.broadcasted_iota(jnp.int32, (KEYS, LANES), 1)
    at_y = (lane // CH + RADIUS).astype(F32)
    at_x = (lane % 8 + RADIUS).astype(F32)
    key_x = lax.broadcasted_iota(jnp.int32, (KEYS, LANES), 0).astype(F32)
    f0 = jnp.broadcast_to(f0, (KEYS, LANES))
    f1 = jnp.broadcast_to(f1, (KEYS, LANES))
    side = f1 * (key_x - at_x) - f0 * at_y
    weights = []
    total = jnp.zeros((KEYS, LANES), F32)
    lean = jnp.zeros((KEYS, LANES), F32)
    for y in range(SPAN):
        weight = score_ref[KEYS * y : KEYS * (y + 1)] * (scale * math.log2(math.e))
        weight = jnp.exp2(weight) * m_ref[y]
        weights.append(weight)
        total = total + weight
        lean = lean + weight * (f0 * float(y) + side)
    total = jnp.sum(total, axis=0, keepdims=True)
    lean = jnp.sum(lean, axis=0, keepdims=True)
    base = jnp.broadcast_to(lean / total, (KEYS, LANES))
    factor = jnp.broadcast_to(scale / total, (KEYS, LANES))
    step = f0 * factor
    side = (side - base) * factor
    return jnp.concatenate(
        [(weights[y] * (step * float(y) + side)).astype(BF16) for y in range(SPAN)], axis=0
    )


def unit_of(field, ones):
    recip = lax.rsqrt(group_sum(field * field, ones) * (1.0 / CH) + 1.0)
    return recip, (field * recip).astype(BF16).astype(F32)


def unit_grad(field, recip, grad, ones):
    inner = group_sum(grad * field, ones)
    return recip * grad - field * (recip * recip * recip) * inner * (1.0 / CH)


def key_rows(t4_ref, q, unit):
    turned = [roll_groups(unit, k) for k in range(QUAD)]
    for i in range(QUAD):
        for g in range(t4_ref.shape[0]):
            t4_ref[g, q * QUAD + i] = by_group(
                [
                    turned[(j - i) % QUAD][g * GROUP + 8 * j : g * GROUP + 8 * j + KEYS]
                    for j in range(QUAD)
                ]
            ).astype(BF16)


def query_block(octs):
    group = lane_group((8, LANES))
    turned = [
        roll_groups(by_group([octs[(i + k) % QUAD] for i in range(QUAD)]), k)
        for k in range(QUAD)
    ]
    parts = [
        jnp.where(group == j, turned[(j - i) % QUAD], 0.0)
        for i in range(QUAD)
        for j in range(QUAD)
    ]
    return jnp.concatenate(parts, axis=0).astype(BF16)


def packed_rows(mine):
    def piece(i, j):
        at = i * GROUP + 8 * j
        return mine[at : at + 8]

    turned = [
        roll_groups(by_group([piece((j + k) % QUAD, j) for j in range(QUAD)]), k)
        for k in range(QUAD)
    ]
    return [by_group([turned[(i - j) % QUAD] for i in range(QUAD)]) for j in range(QUAD)]


def run_blocks(blocks, m_ref, sc_ref, d_ref, scale):
    def score(b):
        sc_ref[b % 2] = lax.dot_general(
            blocks[b][0](), blocks[b][1](), (((1,), (1,)), ((), ())), preferred_element_type=F32
        )

    def collect(b):
        dscore = d_ref[b % 2]
        keys, queries, _, put_keys, put_rows = blocks[b]
        put_keys(jnp.dot(dscore, queries(), preferred_element_type=F32))
        mine = lax.dot_general(
            dscore, keys(), (((0,), (0,)), ((), ())), preferred_element_type=F32
        )
        put_rows(packed_rows(mine))

    score(0)
    for b in range(len(blocks)):
        if b + 1 < len(blocks):
            score(b + 1)
        f0, f1 = blocks[b][2]()
        d_ref[b % 2] = softmax_block(sc_ref.at[b % 2], m_ref, f0, f1, scale)
        if b > 0:
            collect(b - 1)
    collect(len(blocks) - 1)


def conv_from(tap_list, w_ref):
    total = None
    for dx in range(3):
        term = jnp.dot(tap_list[dx], w_ref[dx], preferred_element_type=F32)
        total = term if total is None else total + term
    return total


def inner_block(n, g, t4_ref, q_ref, p_ref, ga_ref, gu_ref):
    at = slice(n * QUAD, n * QUAD + SPAN)
    rows = slice((n + 1) * QUAD, (n + 2) * QUAD)

    def put_keys(value):
        ga_ref[g, at] = ga_ref[g, at] + value.reshape(SPAN, KEYS, LANES)

    def put_rows(octs):
        for j in range(QUAD):
            gu_ref[n, g * GROUP + 8 * j : g * GROUP + 8 * j + 8] = octs[j]

    return (
        lambda: t4_ref[g, at].reshape(SPAN * KEYS, LANES),
        lambda: q_ref[n, g],
        lambda: [jnp.sum(p_ref[f, g, rows, :], axis=0, keepdims=True) for f in range(2)],
        put_keys,
        put_rows,
    )


def inner_queries(n, es_ref, taps_ref, fe_ref, rf_ref, q_ref, ones, keep=None):
    cols = fe_ref.shape[1]
    tap_list = [taps_of(es_ref, n + 1, RADIUS + dx - 1, cols) for dx in range(3)]
    if keep is not None:
        for dx in range(3):
            keep[n, dx] = tap_list[dx]
    feat = conv_from(tap_list, taps_ref).astype(BF16).astype(F32)
    fe_ref[n] = feat
    recip, unit = unit_of(feat, ones)
    rf_ref[n] = recip
    for g in range(cols // GROUP):
        q_ref[n, g] = query_block(
            [unit[g * GROUP + 8 * j : g * GROUP + 8 * j + 8] for j in range(QUAD)]
        )


def fill_plane(dst_ref, q, value):
    cols = value.shape[0]
    dst_ref[q, :cols] = value
    dst_ref[q, cols:] = jnp.zeros((dst_ref.shape[1] - cols, LANES), F32)


def early_kernel(own_ref, w_ref, wt_ref, t4_out, taps_out, back_out, m_out, et_ref):
    planes, cols, _ = own_ref.shape
    ones = group_ones()
    fill_taps(taps_out, w_ref)
    fill_taps(back_out, wt_ref)
    fill_mask(m_out)

    def one(q, carry):
        _, unit = unit_of(own_ref[q].astype(F32), ones)
        et_ref[:cols] = unit
        et_ref[cols:] = jnp.zeros((et_ref.shape[0] - cols, LANES), F32)
        key_rows(t4_out, q, et_ref[...])
        return carry

    lax.fori_loop(0, planes // 2, one, 0)


def middle_kernel(
    own_ref, fl_ref, ra_ref, rb_ref, t4_own, taps_ref, m_ref,
    t4_ref, ga_ref, gf_out, gw_out,
    es_ref, et_ref, q_ref, fe_ref, rf_ref, gu_ref, p_ref, tap_ref, sc_ref, d_ref,
):
    planes, cols, _ = own_ref.shape
    quads = planes // 2
    ext = quads + 4
    groups = cols // GROUP
    scale = SHARPNESS / math.sqrt(CH)
    ones = group_ones()
    for q in range(1, ext - 1):
        fill_plane(es_ref, q, halo_plane(1, q, own_ref, ra_ref, rb_ref))
    flow_inner(p_ref, fl_ref, ra_ref, rb_ref)
    for k, q in enumerate((0, 1, ext - 2, ext - 1)):
        fill_plane(et_ref, k, halo_plane(0, q, own_ref, ra_ref, rb_ref))

    def halo_keys(k, carry):
        _, unit = unit_of(et_ref[k], ones)
        key_rows(t4_ref, jnp.where(k < 2, k, k + quads), unit)
        return carry

    lax.fori_loop(0, 4, halo_keys, 0)
    for g in range(groups):
        t4_ref[g, HALO : HALO + quads * QUAD] = t4_own[g]

    def queries(n, carry):
        inner_queries(n, es_ref, taps_ref, fe_ref, rf_ref, q_ref, ones, tap_ref)
        return carry

    lax.fori_loop(1, quads + 1, queries, 0)
    ga_ref[...] = jnp.zeros_like(ga_ref)
    run_blocks(
        [
            inner_block(n, g, t4_ref, q_ref, p_ref, ga_ref, gu_ref)
            for n in range(1, quads + 1)
            for g in range(groups)
        ],
        m_ref, sc_ref, d_ref, scale,
    )
    gw_out[...] = jnp.zeros_like(gw_out)
    row = lax.broadcasted_iota(jnp.int32, (cols, LANES), 0)

    def grads(n, carry):
        value = unit_grad(fe_ref[n], rf_ref[n], gu_ref[n], ones)
        value = jnp.where(row < cols - 8, value, 0.0).astype(BF16)
        gf_out[n - 1] = value
        for dx in range(3):
            gw_out[dx] = gw_out[dx] + lax.dot_general(
                value, tap_ref[n, dx], (((0,), (0,)), ((), ())), preferred_element_type=F32
            )
        return carry

    lax.fori_loop(1, quads + 1, grads, 0)


def edge_blocks(
    pairs, first, ee_ref, tu_ref, taps_ref, t4_ref, q_ref, ep_ref, ga_ref, ones, keep=None
):
    blocks, stores = [], []
    for e, pair in enumerate(pairs):
        quad_of = [pair[j // 2] for j in range(QUAD)]
        tap_list = [
            jnp.concatenate(
                [
                    taps_of(ee_ref.at[j % 2], quad_of[j] + 1, RADIUS + dx - 1, 8).astype(F32)
                    for j in range(QUAD)
                ],
                axis=0,
            ).astype(BF16)
            for dx in range(3)
        ]
        feat = conv_from(tap_list, taps_ref).astype(BF16).astype(F32)
        recip, unit = unit_of(feat, ones)
        q_ref[e] = query_block([unit[8 * j : 8 * j + 8] for j in range(QUAD)])
        for y in range(SPAN):
            t4_ref[e, y] = by_group(
                [
                    tu_ref[(j - y) % QUAD, j % 2, quad_of[j] + y // QUAD]
                    for j in range(QUAD)
                ]
            ).astype(BF16)
        result = []
        stores.append((tap_list, feat, recip, result))

        def flows(pair=pair):
            total = []
            for f in range(2):
                parts = [
                    jnp.sum(
                        ep_ref[f, h, (pair[h] + 1) * QUAD : (pair[h] + 2) * QUAD, :],
                        axis=0,
                        keepdims=True,
                    )
                    for h in range(2)
                ]
                total.append(parts[0] + parts[1])
            return total

        def put_keys(value, e=e):
            ga_ref[first + e] = value.reshape(SPAN, KEYS, LANES)

        blocks.append(
            (
                lambda e=e: t4_ref[e].reshape(SPAN * KEYS, LANES),
                lambda e=e: q_ref[e],
                flows,
                put_keys,
                result.extend,
            )
        )
    return blocks, stores


def edge_planes(ee_ref, tu_ref, ones, quads_of, keys_of, refs):
    for side in range(2):
        for q in quads_of:
            ee_ref[side, q] = edge_plane(1, q, side, *refs)
        raw = jnp.concatenate([edge_plane(0, q, side, *refs) for q in keys_of], axis=0)
        _, unit = unit_of(raw, ones)
        for k in range(QUAD):
            turned = roll_groups(unit, k)
            for index, q in enumerate(keys_of):
                tu_ref[k, side, q] = turned[index * KEYS : (index + 1) * KEYS]


def edge_grads(stores, ones):
    return [
        unit_grad(feat, recip, jnp.concatenate(result, axis=0), ones).astype(BF16)
        for _, feat, recip, result in stores
    ]


def pairs_of(quads):
    return [(n, n + 1) for n in range(1, quads + 1, 2)]


def edge_kernel(
    own_ref, fl_ref, ra_ref, rb_ref, rc_ref, rd_ref, taps_ref, m_ref, gw_ref,
    ga_ref, gf_out, gw_out,
    ee_ref, tu_ref, t4_ref, q_ref, ep_ref, sc_ref, d_ref,
):
    planes, cols, _ = own_ref.shape
    quads = planes // 2
    ext = quads + 4
    scale = SHARPNESS / math.sqrt(CH)
    ones = group_ones()
    refs = (own_ref, ra_ref, rb_ref, rc_ref, rd_ref)
    edge_planes(ee_ref, tu_ref, ones, range(1, ext - 1), range(1, ext - 1), refs)
    flow_edge(ep_ref, fl_ref, ra_ref, rb_ref, rc_ref, rd_ref)
    blocks, stores = edge_blocks(
        pairs_of(quads), 0, ee_ref, tu_ref, taps_ref, t4_ref, q_ref, ep_ref, ga_ref, ones
    )
    run_blocks(blocks, m_ref, sc_ref, d_ref, scale)
    totals = [gw_ref[dx] for dx in range(3)]
    row = lax.broadcasted_iota(jnp.int32, (GROUP, LANES), 0)
    inside = jnp.logical_xor(row // 8 % 2 == 0, row % 8 < RADIUS)
    for e, grad in enumerate(edge_grads(stores, ones)):
        gf_out[e] = grad
        grad = jnp.where(inside, grad.astype(F32), 0.0).astype(BF16)
        for dx in range(3):
            totals[dx] = totals[dx] + lax.dot_general(
                grad, stores[e][0][dx], (((0,), (0,)), ((), ())), preferred_element_type=F32
            )
    lane = lax.broadcasted_iota(jnp.int32, (CH, LANES), 1)
    for dx, total in enumerate(totals):
        rows_of = [total[i * CH : (i + 1) * CH] for i in range(QUAD)]
        main = [x[:, :LANES] for x in rows_of]
        beside = [x[:, LANES:] for x in rows_of]
        start = jnp.where(lane < CH, roll_groups(beside[0], 1), roll_groups(main[0], 1))
        last = jnp.where(lane < 2 * CH, roll_groups(main[3], 2), roll_groups(beside[3], 2))
        gw_out[dx * CH : (dx + 1) * CH] = (start + main[1]) + (roll_groups(main[2], 3) + last)


def spread(dst_ref, quad, value, channels, rows):
    flipped = value.T
    for i in range(QUAD):
        dst_ref[pl.ds(quad * QUAD + i, channels, stride=rows), :] = flipped[
            i * CH : (i + 1) * CH
        ]


def late_kernel(
    own_ref, fl_ref, ra_ref, rb_ref, rc_ref, rd_ref, taps_ref, back_ref, m_ref,
    t4_ref, gm_ref, gf_ref, gem_ref, gfe_ref,
    gs_out, gt_out,
    es_ref, q_ref, fe_ref, rf_ref, gu_ref, p_ref, ga_ref,
    ee_ref, tu_ref, t4e_ref, qe_ref, ep_ref, ge_ref, full_ref, wide_ref, sc_ref, d_ref,
):
    channels, rows, cols = gs_out.shape
    quads = rows // QUAD
    ext = quads + 4
    groups = cols // GROUP
    scale = SHARPNESS / math.sqrt(CH)
    ones = group_ones()
    outer = (0, quads + 1)
    for q in (0, 1, 2, ext - 3, ext - 2, ext - 1):
        fill_plane(es_ref, q, halo_plane(1, q, own_ref, ra_ref, rb_ref))
    flow_inner(p_ref, fl_ref, ra_ref, rb_ref)
    refs = (own_ref, ra_ref, rb_ref, rc_ref, rd_ref)
    edge_planes(ee_ref, tu_ref, ones, (0, 1, 2, ext - 3, ext - 2, ext - 1), range(ext), refs)
    flow_edge(ep_ref, fl_ref, ra_ref, rb_ref, rc_ref, rd_ref)
    ga_ref[...] = gm_ref[...]
    ge_ref[: quads // 2] = gem_ref[...]
    blocks, stores = edge_blocks(
        [outer], quads // 2, ee_ref, tu_ref, taps_ref, t4e_ref, qe_ref, ep_ref, ge_ref, ones
    )
    for n in outer:
        inner_queries(n, es_ref, taps_ref, fe_ref, rf_ref, q_ref, ones)
        blocks += [
            inner_block(n, g, t4_ref, q_ref, p_ref, ga_ref, gu_ref) for g in range(groups)
        ]
    run_blocks(blocks, m_ref, sc_ref, d_ref, scale)

    for n in range(1, quads + 1):
        full_ref[n, 8 : 8 + cols] = gf_ref[n - 1].astype(F32)
    for n in outer:
        value = unit_grad(fe_ref[n], rf_ref[n], gu_ref[n], ones)
        full_ref[n, 8 : 8 + cols] = value.astype(BF16).astype(F32)
    late = [x.astype(F32) for x in edge_grads(stores, ones)]
    for pair, grad in zip(
        pairs_of(quads) + [outer], [gfe_ref[e].astype(F32) for e in range(quads // 2)] + late
    ):
        for j in range(QUAD):
            at = 0 if j % 2 == 0 else cols
            full_ref[pair[j // 2], at : at + 8] = grad[8 * j : 8 * j + 8]

    def source_grad(q, carry):
        tap_list = [taps_of(full_ref, q + 1, RADIUS + dx - 1, cols) for dx in range(3)]
        spread(wide_ref, q, conv_from(tap_list, back_ref), channels, rows)
        return carry

    lax.fori_loop(0, quads, source_grad, 0)
    gs_out[...] = wide_ref[...].astype(BF16).reshape(channels, rows, cols)

    group = lane_group((8, LANES))
    where_is = {}
    for e, pair in enumerate(pairs_of(quads) + [outer]):
        for j in range(QUAD):
            where_is[pair[j // 2], j % 2] = (e, j)
    last = cols // 8
    for q in range(quads):
        parts = []
        for oct in range(1, last + 1):
            total = None
            for k in range(QUAD):
                both = jnp.zeros((8, LANES), F32)
                for half, which in ((0, oct), (1, oct - 1)):
                    if not 0 < which < last:
                        continue
                    g, j = divmod(which - 1, QUAD)
                    at = (q + 2) * QUAD + (j + k) % QUAD
                    both = jnp.where(group == j, ga_ref[g, at, 8 * half : 8 * half + 8], both)
                both = roll_groups(both, k)
                total = both if total is None else total + both
            side = 0 if oct == 1 else 1 if oct == last else None
            if side is not None:
                half = 1 - side
                for n in range(q, q + 3):
                    e, j = where_is[n, side]
                    for i in range(QUAD):
                        part = ge_ref[e, (q + 2 - n) * QUAD + i, 8 * half : 8 * half + 8]
                        total = total + roll_groups(jnp.where(group == j, part, 0.0), i - j)
            parts.append(total)
        grad = jnp.concatenate(parts, axis=0)
        field = own_ref[q].astype(F32)
        recip = lax.rsqrt(group_sum(field * field, ones) * (1.0 / CH) + 1.0)
        spread(wide_ref, q, unit_grad(field, recip, grad, ones), channels, rows)
    gt_out[...] = wide_ref[...].astype(BF16).reshape(channels, rows, cols)


def pair_exchange(x, y, axis):
    size = lax.axis_size(axis)
    near = [(i, i ^ 1) for i in range(size)]
    far = []
    for i in range(1, size - 1, 2):
        far += [(i, i + 1), (i + 1, i)]
    return lax.ppermute(x, axis, near), lax.ppermute(y, axis, far)


def sum_over(x, axis):
    size = lax.axis_size(axis)
    step = 1
    while step < size:
        x = x + lax.ppermute(x, axis, [(i, i ^ step) for i in range(size)])
        step *= 2
    return x


def vmem(count):
    return [pl.BlockSpec(memory_space=pltpu.VMEM)] * count


def per_device(source, target, conv_weight, flow_cotangent):
    channels, rows, cols = source.shape
    quads = rows // QUAD
    ext = quads + 4
    groups = cols // GROUP
    width = cols + HALO
    asked = quads + 2
    flipped = jnp.transpose(conv_weight[::-1, ::-1], (0, 1, 3, 2))
    shape = jax.ShapeDtypeStruct

    def scratch(*dims, dtype=F32):
        return pltpu.VMEM(dims, dtype)

    def call(kernel, name, outs, scratches, *args, cycles=1000):
        return pl.pallas_call(
            kernel,
            out_shape=tuple(outs),
            in_specs=vmem(len(args)),
            out_specs=tuple(vmem(len(outs))),
            scratch_shapes=scratches,
            cost_estimate=pl.CostEstimate(
                flops=cycles * 250_000, bytes_accessed=cycles * 1000, transcendentals=0
            ),
            name=name,
        )(*args)

    side = shape((4 * cols + 4 * HALO, LANES), BF16)
    own, flow, to_a, to_b = call(
        pack_kernel,
        "pack",
        [shape((2 * quads, cols, LANES), BF16), shape((4 * rows, cols), BF16), side, side],
        [scratch(channels * rows, cols)],
        source,
        target,
        flow_cotangent,
    )
    ra, rb = pair_exchange(to_a, to_b, "row")
    taps = shape((3, 2 * LANES, LANES), BF16)
    keys, forward, back, mask = call(
        early_kernel,
        "early",
        [
            shape((groups, rows, KEYS, LANES), BF16),
            taps,
            taps,
            shape((SPAN, KEYS, LANES), F32),
        ],
        [scratch(width, LANES)],
        own,
        conv_weight,
        flipped,
        cycles=2000,
    )
    strip = shape((2 * ext * HALO + 4 * ext * QUAD, LANES), BF16)
    to_c, to_d = call(
        strip_kernel,
        "strip",
        [strip, strip],
        [scratch(2, 2 * ext * HALO, LANES)],
        own,
        flow,
        ra,
        rb,
    )
    rc, rd = pair_exchange(to_c, to_d, "col")
    stages = [scratch(2, SPAN * KEYS, LANES), scratch(2, SPAN * KEYS, LANES, dtype=BF16)]
    inner = [
        scratch(asked, groups, LANES, LANES, dtype=BF16),
        scratch(asked, cols, LANES),
        scratch(asked, cols, LANES),
        scratch(asked, cols, LANES),
        scratch(2, groups, ext * QUAD, LANES),
    ]
    outer = [scratch(2, ext, KEYS, LANES), scratch(QUAD, 2, ext, KEYS, LANES)]
    keys, grad_keys, grad_feat, terms = call(
        middle_kernel,
        "middle",
        [
            shape((groups, ext * QUAD, KEYS, LANES), BF16),
            shape((groups, ext * QUAD, KEYS, LANES), F32),
            shape((quads, cols, LANES), BF16),
            shape((3, LANES, 2 * LANES), F32),
        ],
        [scratch(ext, width, LANES), scratch(4, width, LANES)]
        + inner
        + [scratch(asked, 3, cols, 2 * LANES, dtype=BF16)]
        + stages,
        own,
        flow,
        ra,
        rb,
        keys,
        forward,
        mask,
        cycles=7000,
    )
    pairs = quads // 2
    edge_keys, edge_feat, terms = call(
        edge_kernel,
        "edge",
        [
            shape((pairs, SPAN, KEYS, LANES), F32),
            shape((pairs, GROUP, LANES), BF16),
            shape((3 * CH, LANES), F32),
        ],
        outer
        + [
            scratch(pairs, SPAN, KEYS, LANES, dtype=BF16),
            scratch(pairs, LANES, LANES, dtype=BF16),
            scratch(2, 2, ext * QUAD, LANES),
        ]
        + stages,
        own,
        flow,
        ra,
        rb,
        rc,
        rd,
        forward,
        mask,
        terms,
    )
    grad_source, grad_target = call(
        late_kernel,
        "late",
        [shape(source.shape, BF16), shape(target.shape, BF16)],
        [scratch(ext, width, LANES)]
        + inner
        + [scratch(groups, ext * QUAD, KEYS, LANES)]
        + outer
        + [
            scratch(1, SPAN, KEYS, LANES, dtype=BF16),
            scratch(1, LANES, LANES, dtype=BF16),
            scratch(2, 2, ext * QUAD, LANES),
            scratch(pairs + 1, SPAN, KEYS, LANES),
            scratch(asked, 8 + cols, LANES),
            scratch(channels * rows, cols),
        ]
        + stages,
        own,
        flow,
        ra,
        rb,
        rc,
        rd,
        forward,
        back,
        mask,
        keys,
        grad_keys,
        grad_feat,
        edge_keys,
        edge_feat,
        cycles=6000,
    )
    pixels = rows * cols * lax.axis_size("row") * lax.axis_size("col")
    terms = sum_over(sum_over(terms, "row"), "col") / math.sqrt(pixels)
    terms = terms.reshape(3, CH, QUAD, CH)[:, :, :3]
    return (grad_source, grad_target, jnp.transpose(terms, (2, 0, 3, 1)))


def solution(mesh):
    placed = (
        P(None, ("sec", "row"), "col"),
        P(None, ("sec", "row"), "col"),
        P(),
        P(None, ("sec", "row"), "col"),
    )
    return jax.shard_map(
        per_device,
        mesh=mesh,
        in_specs=placed,
        out_specs=(
            P(None, ("sec", "row"), "col"),
            P(None, ("sec", "row"), "col"),
            P("sec", None, None, None),
        ),
        check_vma=False,
    )
```

```python
import functools
import math

import jax
import jax.numpy as jnp
from jax import lax
from jax.experimental import pallas as pl
from jax.experimental.pallas import tpu as pltpu
from jax.sharding import PartitionSpec as P

RADIUS = 4
SHARPNESS = 4.0
CH = 32
QUAD = 4
LANES = QUAD * CH
GROUP = 32
HALO = 2 * RADIUS
F32 = jnp.float32
BF16 = jnp.bfloat16


def lane_group(shape):
    return lax.broadcasted_iota(jnp.int32, shape, len(shape) - 1) // CH


def by_group(values):
    lane = lax.broadcasted_iota(jnp.int32, values[0].shape, values[0].ndim - 1)
    low = jnp.where(lane < CH, values[0], values[1])
    high = jnp.where(lane < 3 * CH, values[2], values[3])
    return jnp.where(lane < 2 * CH, low, high)


def roll_groups(value, steps):
    steps = steps % QUAD
    if steps == 0:
        return value
    return pltpu.roll(value, steps * CH, value.ndim - 1)


def group_sum(value, ones):
    high = value.astype(BF16)
    low = (value - high.astype(F32)).astype(BF16)
    both = jnp.concatenate([high, low], axis=1)
    return jnp.dot(both, ones, preferred_element_type=F32)


def group_ones():
    row = lax.broadcasted_iota(jnp.int32, (2 * LANES, LANES), 0) % LANES
    col = lax.broadcasted_iota(jnp.int32, (2 * LANES, LANES), 1)
    return jnp.where(row // CH == col // CH, 1.0, 0.0).astype(BF16)


def even(axis):
    return lax.rem(lax.axis_index(axis), 2) == 0


def pack_kernel(src_ref, tgt_ref, flow_ref, own_ref, fl_ref, sa_ref, sb_ref, wide_ref):
    channels, rows, cols = src_ref.shape
    quads = rows // QUAD
    for base, ref in ((0, tgt_ref), (quads, src_ref)):
        wide_ref[...] = ref[...].astype(F32).reshape(channels * rows, cols)
        for q in range(quads):
            part = jnp.concatenate(
                [wide_ref[pl.ds(q * QUAD + i, channels, stride=rows), :] for i in range(QUAD)],
                axis=0,
            )
            own_ref[base + q] = part.T.astype(BF16)
    pieces = []
    for f in range(2):
        value = flow_ref[f]
        high = value.astype(BF16).astype(F32)
        pieces += [high, value - high]
    fl_ref[...] = jnp.concatenate(pieces, axis=0).astype(BF16)
    is_even = even("row")
    last = quads - HALO // QUAD
    for dst, first in (
        (sa_ref, jnp.where(is_even, last, 0)),
        (sb_ref, jnp.where(is_even, 0, last)),
    ):
        for k in range(HALO // QUAD):
            dst[k * cols : (k + 1) * cols] = own_ref[first + k]
            dst[(2 + k) * cols : (3 + k) * cols] = own_ref[quads + first + k]
    top = jnp.concatenate([p[:HALO] for p in pieces], axis=0)
    low = jnp.concatenate([p[rows - HALO :] for p in pieces], axis=0)
    sa_ref[4 * cols :] = jnp.where(is_even, low, top).astype(BF16)
    sb_ref[4 * cols :] = jnp.where(is_even, top, low).astype(BF16)


def pick(flag, first, second):
    return jnp.where(flag, first.astype(F32), second.astype(F32))


def strip_kernel(own_ref, fl_ref, ra_ref, rb_ref, sc_ref, sd_ref, wide_ref):
    planes, cols, _ = own_ref.shape
    quads = planes // 2
    rows = quads * QUAD
    r_even = even("row")
    c_even = even("col")

    def strips(read):
        return read(0, 2 * HALO)[:HALO], read(cols - 2 * HALO, 2 * HALO)[HALO:]

    for kind in range(2):
        for q in range(quads + 4):
            if 2 <= q < quads + 2:
                plane = kind * quads + q - 2
                left, right = strips(lambda at, n: own_ref[plane, at : at + n].astype(F32))
            else:
                down = q >= quads + 2
                at0 = (2 * kind + (q - quads - 2 if down else q)) * cols
                flag = r_even if down else jnp.logical_not(r_even)
                left, right = strips(
                    lambda at, n: pick(
                        flag, ra_ref[at0 + at : at0 + at + n], rb_ref[at0 + at : at0 + at + n]
                    )
                )
            row = (kind * (quads + 4) + q) * HALO
            wide_ref[0, row : row + HALO] = jnp.where(c_even, right, left)
            wide_ref[1, row : row + HALO] = jnp.where(c_even, left, right)
    count = 2 * (quads + 4) * HALO
    sc_ref[:count] = wide_ref[0].astype(BF16)
    sd_ref[:count] = wide_ref[1].astype(BF16)
    a, b = (ra_ref[4 * cols :], rb_ref[4 * cols :])
    up, down = (pick(r_even, b, a), pick(r_even, a, b))
    flow = []
    own = fl_ref[...].astype(F32)
    for v in range(4):
        flow += [
            up[v * HALO : (v + 1) * HALO],
            own[v * rows : (v + 1) * rows],
            down[v * HALO : (v + 1) * HALO],
        ]
    flow = jnp.concatenate(flow, axis=0).astype(BF16)
    sc_ref[count:] = flow
    sd_ref[count:] = flow


def fill_taps(dst_ref, w_ref):
    zero = jnp.zeros((CH, CH), F32)
    for dx in range(3):
        for block in range(2 * QUAD):
            row = block if block < QUAD else {QUAD: QUAD, 2 * QUAD - 1: -1}.get(block)
            parts = []
            for out in range(QUAD):
                tap = None if row is None else row - out + 1
                ok = tap is not None and 0 <= tap < 3
                parts.append(w_ref[tap, dx].astype(F32) if ok else zero)
            dst_ref[dx, block * CH : (block + 1) * CH, :] = jnp.concatenate(parts, axis=1).astype(
                BF16
            )


def taps_of(ref, quad, start, count):
    main = ref[quad, pl.ds(start, count), :]
    after = ref[quad + 1, pl.ds(start, count), :]
    before = ref[quad - 1, pl.ds(start, count), :]
    lane = lax.broadcasted_iota(jnp.int32, main.shape, 1)
    beside = jnp.where(lane < 2 * CH, after, before)
    return jnp.concatenate([main, beside], axis=1).astype(BF16)


def conv(ref, quad, start, count, w_ref):
    total = jnp.zeros((count, LANES), F32)
    for dx in range(3):
        total += jnp.dot(
            taps_of(ref, quad, start + dx - 1, count), w_ref[dx], preferred_element_type=F32
        )
    return total


SPAN = 3 * QUAD
KEYS = 16


def halo_plane(kind, q, own_ref, ra_ref, rb_ref):
    planes, cols, _ = own_ref.shape
    quads = planes // 2
    if 2 <= q < quads + 2:
        return own_ref[kind * quads + q - 2].astype(F32)
    down = q >= quads + 2
    at = (2 * kind + (q - quads - 2 if down else q)) * cols
    flag = even("row") if down else jnp.logical_not(even("row"))
    return pick(flag, ra_ref[at : at + cols], rb_ref[at : at + cols])


def sides_of(rc, rd):
    flag = even("col")
    return pick(flag, rd, rc), pick(flag, rc, rd)


def edge_plane(kind, q, side, own_ref, ra_ref, rb_ref, rc_ref, rd_ref):
    planes, cols, _ = own_ref.shape
    quads = planes // 2
    tile = slice(0, KEYS) if side == 0 else slice(cols - KEYS, cols)
    if 2 <= q < quads + 2:
        mine = own_ref[kind * quads + q - 2, tile].astype(F32)
    else:
        down = q >= quads + 2
        at = (2 * kind + (q - quads - 2 if down else q)) * cols
        tile = slice(at + tile.start, at + tile.stop)
        flag = even("row") if down else jnp.logical_not(even("row"))
        mine = pick(flag, ra_ref[tile], rb_ref[tile])
    index = kind * (quads + 4) + q
    at = index // 2 * 2 * HALO
    fetched = sides_of(rc_ref[at : at + 2 * HALO], rd_ref[at : at + 2 * HALO])[side]
    fetched = fetched[index % 2 * HALO : index % 2 * HALO + HALO]
    parts = [fetched, mine[:HALO]] if side == 0 else [mine[HALO:], fetched]
    return jnp.concatenate(parts, axis=0)


def flow_mid(f, fl_ref, ra_ref, rb_ref):
    cols = fl_ref.shape[1]
    rows = fl_ref.shape[0] // 4
    a, b = (ra_ref[4 * cols :], rb_ref[4 * cols :])
    flag = even("row")
    up, down = (pick(flag, b, a), pick(flag, a, b))
    total = None
    for v in (2 * f, 2 * f + 1):
        part = jnp.concatenate(
            [
                up[v * HALO : (v + 1) * HALO],
                fl_ref[v * rows : (v + 1) * rows].astype(F32),
                down[v * HALO : (v + 1) * HALO],
            ],
            axis=0,
        )
        total = part if total is None else total + part
    return total


def flow_inner(p_ref, fl_ref, ra_ref, rb_ref):
    groups = p_ref.shape[1]
    for f in range(2):
        mid = pltpu.roll(flow_mid(f, fl_ref, ra_ref, rb_ref), LANES - RADIUS, 1)
        lane = lax.broadcasted_iota(jnp.int32, mid.shape, 1)
        row = lax.broadcasted_iota(jnp.int32, mid.shape, 0)
        mid = jnp.where(lane < LANES - 8, mid, 0.0)
        turned = [roll_groups(mid, k) for k in range(QUAD)]
        for g in range(groups):
            total = jnp.zeros(mid.shape, F32)
            for i in range(QUAD):
                keep = jnp.logical_and(row % QUAD == i, lane // CH == i)
                total = jnp.where(keep, turned[(i - g) % QUAD], total)
            p_ref[f, g] = total


def flow_edge(e_ref, fl_ref, ra_ref, rb_ref, rc_ref, rd_ref):
    rows = fl_ref.shape[0] // 4
    ext = rows + 2 * HALO
    base = rc_ref.shape[0] - 4 * ext
    left, right = sides_of(rc_ref[base:], rd_ref[base:])
    for f in range(2):
        mid = flow_mid(f, fl_ref, ra_ref, rb_ref)
        at = 2 * f * ext
        lf = left[at : at + ext] + left[at + ext : at + 2 * ext]
        rt = right[at : at + ext] + right[at + ext : at + 2 * ext]
        lane = lax.broadcasted_iota(jnp.int32, mid.shape, 1)
        row = lax.broadcasted_iota(jnp.int32, mid.shape, 0)
        low = jnp.where(lane < RADIUS, pltpu.roll(lf, RADIUS, 1), pltpu.roll(mid, RADIUS, 1))
        high = jnp.where(
            lane < 3 * RADIUS, pltpu.roll(mid, 3 * RADIUS, 1), pltpu.roll(rt, 3 * RADIUS, 1)
        )
        both = jnp.where(lane < 8, low, high)
        for h in range(2):
            total = jnp.zeros(mid.shape, F32)
            for i in range(QUAD):
                turn = i * CH + h * 16
                keep = jnp.logical_and(row % QUAD == i, lane // 16 == 2 * i + h)
                total = jnp.where(keep, pltpu.roll(both, turn, 1) if turn else both, total)
            e_ref[f, h] = total


def fill_mask(m_ref):
    key = lax.broadcasted_iota(jnp.int32, (SPAN, KEYS, LANES), 0)
    kx = lax.broadcasted_iota(jnp.int32, (SPAN, KEYS, LANES), 1)
    lane = lax.broadcasted_iota(jnp.int32, (SPAN, KEYS, LANES), 2)
    dy = key - lane // CH
    dx = kx - lane % 8
    ok = (dy >= 0) & (dy <= 2 * RADIUS) & (dx >= 0) & (dx <= 2 * RADIUS)
    m_ref[...] = jnp.where(ok, 1.0, 0.0)


def softmax_block(score_ref, m_ref, f0, f1, scale):
    lane = lax.broadcasted_iota(jnp.int32, (KEYS, LANES), 1)
    at_y = (lane // CH + RADIUS).astype(F32)
    at_x = (lane % 8 + RADIUS).astype(F32)
    key_x = lax.broadcasted_iota(jnp.int32, (KEYS, LANES), 0).astype(F32)
    f0 = jnp.broadcast_to(f0, (KEYS, LANES))
    f1 = jnp.broadcast_to(f1, (KEYS, LANES))
    side = f1 * (key_x - at_x) - f0 * at_y
    weights = []
    total = jnp.zeros((KEYS, LANES), F32)
    lean = jnp.zeros((KEYS, LANES), F32)
    for y in range(SPAN):
        weight = score_ref[KEYS * y : KEYS * (y + 1)] * (scale * math.log2(math.e))
        weight = jnp.exp2(weight) * m_ref[y]
        weights.append(weight)
        total = total + weight
        lean = lean + weight * (f0 * float(y) + side)
    total = jnp.sum(total, axis=0, keepdims=True)
    lean = jnp.sum(lean, axis=0, keepdims=True)
    base = jnp.broadcast_to(lean / total, (KEYS, LANES))
    factor = jnp.broadcast_to(scale / total, (KEYS, LANES))
    step = f0 * factor
    side = (side - base) * factor
    return jnp.concatenate(
        [(weights[y] * (step * float(y) + side)).astype(BF16) for y in range(SPAN)], axis=0
    )


def unit_of(field, ones):
    recip = lax.rsqrt(group_sum(field * field, ones) * (1.0 / CH) + 1.0)
    return recip, (field * recip).astype(BF16).astype(F32)


def unit_grad(field, recip, grad, ones):
    inner = group_sum(grad * field, ones)
    return recip * grad - field * (recip * recip * recip) * inner * (1.0 / CH)


def key_rows(t4_ref, q, unit):
    turned = [roll_groups(unit, k) for k in range(QUAD)]
    for i in range(QUAD):
        for g in range(t4_ref.shape[0]):
            t4_ref[g, q * QUAD + i] = by_group(
                [
                    turned[(j - i) % QUAD][g * GROUP + 8 * j : g * GROUP + 8 * j + KEYS]
                    for j in range(QUAD)
                ]
            ).astype(BF16)


def query_block(octs):
    group = lane_group((8, LANES))
    turned = [
        roll_groups(by_group([octs[(i + k) % QUAD] for i in range(QUAD)]), k)
        for k in range(QUAD)
    ]
    parts = [
        jnp.where(group == j, turned[(j - i) % QUAD], 0.0)
        for i in range(QUAD)
        for j in range(QUAD)
    ]
    return jnp.concatenate(parts, axis=0).astype(BF16)


def packed_rows(mine):
    def piece(i, j):
        at = i * GROUP + 8 * j
        return mine[at : at + 8]

    turned = [
        roll_groups(by_group([piece((j + k) % QUAD, j) for j in range(QUAD)]), k)
        for k in range(QUAD)
    ]
    return [by_group([turned[(i - j) % QUAD] for i in range(QUAD)]) for j in range(QUAD)]


def run_blocks(blocks, m_ref, sc_ref, d_ref, scale):
    def score(b):
        sc_ref[b % 2] = lax.dot_general(
            blocks[b][0](), blocks[b][1](), (((1,), (1,)), ((), ())), preferred_element_type=F32
        )

    def collect(b):
        dscore = d_ref[b % 2]
        keys, queries, _, put_keys, put_rows = blocks[b]
        put_keys(jnp.dot(dscore, queries(), preferred_element_type=F32))
        mine = lax.dot_general(
            dscore, keys(), (((0,), (0,)), ((), ())), preferred_element_type=F32
        )
        put_rows(packed_rows(mine))

    score(0)
    for b in range(len(blocks)):
        if b + 1 < len(blocks):
            score(b + 1)
        f0, f1 = blocks[b][2]()
        d_ref[b % 2] = softmax_block(sc_ref.at[b % 2], m_ref, f0, f1, scale)
        if b > 0:
            collect(b - 1)
    collect(len(blocks) - 1)


def conv_from(tap_list, w_ref):
    total = None
    for dx in range(3):
        term = jnp.dot(tap_list[dx], w_ref[dx], preferred_element_type=F32)
        total = term if total is None else total + term
    return total


def inner_block(n, g, t4_ref, q_ref, p_ref, ga_ref, gu_ref):
    at = slice(n * QUAD, n * QUAD + SPAN)
    rows = slice((n + 1) * QUAD, (n + 2) * QUAD)

    def put_keys(value):
        ga_ref[g, at] = ga_ref[g, at] + value.reshape(SPAN, KEYS, LANES)

    def put_rows(octs):
        for j in range(QUAD):
            gu_ref[n, g * GROUP + 8 * j : g * GROUP + 8 * j + 8] = octs[j]

    return (
        lambda: t4_ref[g, at].reshape(SPAN * KEYS, LANES),
        lambda: q_ref[n, g],
        lambda: [jnp.sum(p_ref[f, g, rows, :], axis=0, keepdims=True) for f in range(2)],
        put_keys,
        put_rows,
    )


def inner_queries(n, es_ref, taps_ref, fe_ref, rf_ref, q_ref, ones, keep=None):
    cols = fe_ref.shape[1]
    tap_list = [taps_of(es_ref, n + 1, RADIUS + dx - 1, cols) for dx in range(3)]
    if keep is not None:
        for dx in range(3):
            keep[n, dx] = tap_list[dx]
    feat = conv_from(tap_list, taps_ref).astype(BF16).astype(F32)
    fe_ref[n] = feat
    recip, unit = unit_of(feat, ones)
    rf_ref[n] = recip
    for g in range(cols // GROUP):
        q_ref[n, g] = query_block(
            [unit[g * GROUP + 8 * j : g * GROUP + 8 * j + 8] for j in range(QUAD)]
        )


def fill_plane(dst_ref, q, value):
    cols = value.shape[0]
    dst_ref[q, :cols] = value
    dst_ref[q, cols:] = jnp.zeros((dst_ref.shape[1] - cols, LANES), F32)


def early_kernel(own_ref, w_ref, wt_ref, t4_out, taps_out, back_out, m_out, et_ref):
    planes, cols, _ = own_ref.shape
    ones = group_ones()
    fill_taps(taps_out, w_ref)
    fill_taps(back_out, wt_ref)
    fill_mask(m_out)

    def one(q, carry):
        _, unit = unit_of(own_ref[q].astype(F32), ones)
        et_ref[:cols] = unit
        et_ref[cols:] = jnp.zeros((et_ref.shape[0] - cols, LANES), F32)
        key_rows(t4_out, q, et_ref[...])
        return carry

    lax.fori_loop(0, planes // 2, one, 0)


def middle_kernel(
    own_ref, fl_ref, ra_ref, rb_ref, t4_own, taps_ref, m_ref,
    t4_ref, ga_ref, gf_out, gw_out,
    es_ref, et_ref, q_ref, fe_ref, rf_ref, gu_ref, p_ref, tap_ref, sc_ref, d_ref,
):
    planes, cols, _ = own_ref.shape
    quads = planes // 2
    ext = quads + 4
    groups = cols // GROUP
    scale = SHARPNESS / math.sqrt(CH)
    ones = group_ones()
    for q in range(1, ext - 1):
        fill_plane(es_ref, q, halo_plane(1, q, own_ref, ra_ref, rb_ref))
    flow_inner(p_ref, fl_ref, ra_ref, rb_ref)
    for k, q in enumerate((0, 1, ext - 2, ext - 1)):
        fill_plane(et_ref, k, halo_plane(0, q, own_ref, ra_ref, rb_ref))

    def halo_keys(k, carry):
        _, unit = unit_of(et_ref[k], ones)
        key_rows(t4_ref, jnp.where(k < 2, k, k + quads), unit)
        return carry

    lax.fori_loop(0, 4, halo_keys, 0)
    for g in range(groups):
        t4_ref[g, HALO : HALO + quads * QUAD] = t4_own[g]

    def queries(n, carry):
        inner_queries(n, es_ref, taps_ref, fe_ref, rf_ref, q_ref, ones, tap_ref)
        return carry

    lax.fori_loop(1, quads + 1, queries, 0)
    ga_ref[...] = jnp.zeros_like(ga_ref)
    run_blocks(
        [
            inner_block(n, g, t4_ref, q_ref, p_ref, ga_ref, gu_ref)
            for n in range(1, quads + 1)
            for g in range(groups)
        ],
        m_ref, sc_ref, d_ref, scale,
    )
    gw_out[...] = jnp.zeros_like(gw_out)
    row = lax.broadcasted_iota(jnp.int32, (cols, LANES), 0)

    def grads(n, carry):
        value = unit_grad(fe_ref[n], rf_ref[n], gu_ref[n], ones)
        value = jnp.where(row < cols - 8, value, 0.0).astype(BF16)
        gf_out[n - 1] = value
        for dx in range(3):
            gw_out[dx] = gw_out[dx] + lax.dot_general(
                value, tap_ref[n, dx], (((0,), (0,)), ((), ())), preferred_element_type=F32
            )
        return carry

    lax.fori_loop(1, quads + 1, grads, 0)


def edge_blocks(
    pairs, first, ee_ref, tu_ref, taps_ref, t4_ref, q_ref, ep_ref, ga_ref, ones, keep=None
):
    blocks, stores = [], []
    for e, pair in enumerate(pairs):
        quad_of = [pair[j // 2] for j in range(QUAD)]
        tap_list = [
            jnp.concatenate(
                [
                    taps_of(ee_ref.at[j % 2], quad_of[j] + 1, RADIUS + dx - 1, 8).astype(F32)
                    for j in range(QUAD)
                ],
                axis=0,
            ).astype(BF16)
            for dx in range(3)
        ]
        feat = conv_from(tap_list, taps_ref).astype(BF16).astype(F32)
        recip, unit = unit_of(feat, ones)
        q_ref[e] = query_block([unit[8 * j : 8 * j + 8] for j in range(QUAD)])
        for y in range(SPAN):
            t4_ref[e, y] = by_group(
                [
                    tu_ref[(j - y) % QUAD, j % 2, quad_of[j] + y // QUAD]
                    for j in range(QUAD)
                ]
            ).astype(BF16)
        result = []
        stores.append((tap_list, feat, recip, result))

        def flows(pair=pair):
            total = []
            for f in range(2):
                parts = [
                    jnp.sum(
                        ep_ref[f, h, (pair[h] + 1) * QUAD : (pair[h] + 2) * QUAD, :],
                        axis=0,
                        keepdims=True,
                    )
                    for h in range(2)
                ]
                total.append(parts[0] + parts[1])
            return total

        def put_keys(value, e=e):
            ga_ref[first + e] = value.reshape(SPAN, KEYS, LANES)

        blocks.append(
            (
                lambda e=e: t4_ref[e].reshape(SPAN * KEYS, LANES),
                lambda e=e: q_ref[e],
                flows,
                put_keys,
                result.extend,
            )
        )
    return blocks, stores


def edge_planes(ee_ref, tu_ref, ones, quads_of, keys_of, refs):
    for side in range(2):
        for q in quads_of:
            ee_ref[side, q] = edge_plane(1, q, side, *refs)
        raw = jnp.concatenate([edge_plane(0, q, side, *refs) for q in keys_of], axis=0)
        _, unit = unit_of(raw, ones)
        for k in range(QUAD):
            turned = roll_groups(unit, k)
            for index, q in enumerate(keys_of):
                tu_ref[k, side, q] = turned[index * KEYS : (index + 1) * KEYS]


def edge_grads(stores, ones):
    return [
        unit_grad(feat, recip, jnp.concatenate(result, axis=0), ones).astype(BF16)
        for _, feat, recip, result in stores
    ]


def pairs_of(quads):
    return [(n, n + 1) for n in range(1, quads + 1, 2)]


def edge_kernel(
    own_ref, fl_ref, ra_ref, rb_ref, rc_ref, rd_ref, taps_ref, m_ref, gw_ref,
    ga_ref, gf_out, gw_out,
    ee_ref, tu_ref, t4_ref, q_ref, ep_ref, sc_ref, d_ref,
):
    planes, cols, _ = own_ref.shape
    quads = planes // 2
    ext = quads + 4
    scale = SHARPNESS / math.sqrt(CH)
    ones = group_ones()
    refs = (own_ref, ra_ref, rb_ref, rc_ref, rd_ref)
    edge_planes(ee_ref, tu_ref, ones, range(1, ext - 1), range(1, ext - 1), refs)
    flow_edge(ep_ref, fl_ref, ra_ref, rb_ref, rc_ref, rd_ref)
    blocks, stores = edge_blocks(
        pairs_of(quads), 0, ee_ref, tu_ref, taps_ref, t4_ref, q_ref, ep_ref, ga_ref, ones
    )
    run_blocks(blocks, m_ref, sc_ref, d_ref, scale)
    totals = [gw_ref[dx] for dx in range(3)]
    row = lax.broadcasted_iota(jnp.int32, (GROUP, LANES), 0)
    inside = jnp.logical_xor(row // 8 % 2 == 0, row % 8 < RADIUS)
    for e, grad in enumerate(edge_grads(stores, ones)):
        gf_out[e] = grad
        grad = jnp.where(inside, grad.astype(F32), 0.0).astype(BF16)
        for dx in range(3):
            totals[dx] = totals[dx] + lax.dot_general(
                grad, stores[e][0][dx], (((0,), (0,)), ((), ())), preferred_element_type=F32
            )
    lane = lax.broadcasted_iota(jnp.int32, (CH, LANES), 1)
    for dx, total in enumerate(totals):
        rows_of = [total[i * CH : (i + 1) * CH] for i in range(QUAD)]
        main = [x[:, :LANES] for x in rows_of]
        beside = [x[:, LANES:] for x in rows_of]
        start = jnp.where(lane < CH, roll_groups(beside[0], 1), roll_groups(main[0], 1))
        last = jnp.where(lane < 2 * CH, roll_groups(main[3], 2), roll_groups(beside[3], 2))
        gw_out[dx * CH : (dx + 1) * CH] = (start + main[1]) + (roll_groups(main[2], 3) + last)


def spread(dst_ref, quad, value, channels, rows):
    flipped = value.T
    for i in range(QUAD):
        dst_ref[pl.ds(quad * QUAD + i, channels, stride=rows), :] = flipped[
            i * CH : (i + 1) * CH
        ]


def late_kernel(
    own_ref, fl_ref, ra_ref, rb_ref, rc_ref, rd_ref, taps_ref, back_ref, m_ref,
    t4_ref, gm_ref, gf_ref, gem_ref, gfe_ref,
    gs_out, gt_out,
    es_ref, q_ref, fe_ref, rf_ref, gu_ref, p_ref, ga_ref,
    ee_ref, tu_ref, t4e_ref, qe_ref, ep_ref, ge_ref, full_ref, wide_ref, sc_ref, d_ref,
):
    channels, rows, cols = gs_out.shape
    quads = rows // QUAD
    ext = quads + 4
    groups = cols // GROUP
    scale = SHARPNESS / math.sqrt(CH)
    ones = group_ones()
    outer = (0, quads + 1)
    for q in (0, 1, 2, ext - 3, ext - 2, ext - 1):
        fill_plane(es_ref, q, halo_plane(1, q, own_ref, ra_ref, rb_ref))
    flow_inner(p_ref, fl_ref, ra_ref, rb_ref)
    refs = (own_ref, ra_ref, rb_ref, rc_ref, rd_ref)
    edge_planes(ee_ref, tu_ref, ones, (0, 1, 2, ext - 3, ext - 2, ext - 1), range(ext), refs)
    flow_edge(ep_ref, fl_ref, ra_ref, rb_ref, rc_ref, rd_ref)
    ga_ref[...] = gm_ref[...]
    ge_ref[: quads // 2] = gem_ref[...]
    blocks, stores = edge_blocks(
        [outer], quads // 2, ee_ref, tu_ref, taps_ref, t4e_ref, qe_ref, ep_ref, ge_ref, ones
    )
    for n in outer:
        inner_queries(n, es_ref, taps_ref, fe_ref, rf_ref, q_ref, ones)
        blocks += [
            inner_block(n, g, t4_ref, q_ref, p_ref, ga_ref, gu_ref) for g in range(groups)
        ]
    run_blocks(blocks, m_ref, sc_ref, d_ref, scale)

    for n in range(1, quads + 1):
        full_ref[n, 8 : 8 + cols] = gf_ref[n - 1].astype(F32)
    for n in outer:
        value = unit_grad(fe_ref[n], rf_ref[n], gu_ref[n], ones)
        full_ref[n, 8 : 8 + cols] = value.astype(BF16).astype(F32)
    late = [x.astype(F32) for x in edge_grads(stores, ones)]
    for pair, grad in zip(
        pairs_of(quads) + [outer], [gfe_ref[e].astype(F32) for e in range(quads // 2)] + late
    ):
        for j in range(QUAD):
            at = 0 if j % 2 == 0 else cols
            full_ref[pair[j // 2], at : at + 8] = grad[8 * j : 8 * j + 8]

    def source_grad(q, carry):
        tap_list = [taps_of(full_ref, q + 1, RADIUS + dx - 1, cols) for dx in range(3)]
        spread(wide_ref, q, conv_from(tap_list, back_ref), channels, rows)
        return carry

    lax.fori_loop(0, quads, source_grad, 0)
    gs_out[...] = wide_ref[...].astype(BF16).reshape(channels, rows, cols)

    group = lane_group((8, LANES))
    where_is = {}
    for e, pair in enumerate(pairs_of(quads) + [outer]):
        for j in range(QUAD):
            where_is[pair[j // 2], j % 2] = (e, j)
    last = cols // 8
    for q in range(quads):
        parts = []
        for oct in range(1, last + 1):
            total = None
            for k in range(QUAD):
                both = jnp.zeros((8, LANES), F32)
                for half, which in ((0, oct), (1, oct - 1)):
                    if not 0 < which < last:
                        continue
                    g, j = divmod(which - 1, QUAD)
                    at = (q + 2) * QUAD + (j + k) % QUAD
                    both = jnp.where(group == j, ga_ref[g, at, 8 * half : 8 * half + 8], both)
                both = roll_groups(both, k)
                total = both if total is None else total + both
            side = 0 if oct == 1 else 1 if oct == last else None
            if side is not None:
                half = 1 - side
                for n in range(q, q + 3):
                    e, j = where_is[n, side]
                    for i in range(QUAD):
                        part = ge_ref[e, (q + 2 - n) * QUAD + i, 8 * half : 8 * half + 8]
                        total = total + roll_groups(jnp.where(group == j, part, 0.0), i - j)
            parts.append(total)
        grad = jnp.concatenate(parts, axis=0)
        field = own_ref[q].astype(F32)
        recip = lax.rsqrt(group_sum(field * field, ones) * (1.0 / CH) + 1.0)
        spread(wide_ref, q, unit_grad(field, recip, grad, ones), channels, rows)
    gt_out[...] = wide_ref[...].astype(BF16).reshape(channels, rows, cols)


def pair_exchange(x, y, axis):
    size = lax.axis_size(axis)
    near = [(i, i ^ 1) for i in range(size)]
    far = []
    for i in range(1, size - 1, 2):
        far += [(i, i + 1), (i + 1, i)]
    return lax.ppermute(x, axis, near), lax.ppermute(y, axis, far)


def sum_over(x, axis):
    size = lax.axis_size(axis)
    step = 1
    while step < size:
        x = x + lax.ppermute(x, axis, [(i, i ^ step) for i in range(size)])
        step *= 2
    return x


def vmem(count):
    return [pl.BlockSpec(memory_space=pltpu.VMEM)] * count


def per_device(source, target, conv_weight, flow_cotangent):
    channels, rows, cols = source.shape
    quads = rows // QUAD
    ext = quads + 4
    groups = cols // GROUP
    width = cols + HALO
    asked = quads + 2
    flipped = jnp.transpose(conv_weight[::-1, ::-1], (0, 1, 3, 2))
    shape = jax.ShapeDtypeStruct

    def scratch(*dims, dtype=F32):
        return pltpu.VMEM(dims, dtype)

    def call(kernel, name, outs, scratches, *args, cycles=1000):
        return pl.pallas_call(
            kernel,
            out_shape=tuple(outs),
            in_specs=vmem(len(args)),
            out_specs=tuple(vmem(len(outs))),
            scratch_shapes=scratches,
            cost_estimate=pl.CostEstimate(
                flops=cycles * 250_000, bytes_accessed=cycles * 1000, transcendentals=0
            ),
            compiler_params=pltpu.CompilerParams(vmem_limit_bytes=16 << 20),
            name=name,
        )(*args)

    side = shape((4 * cols + 4 * HALO, LANES), BF16)
    own, flow, to_a, to_b = call(
        pack_kernel,
        "pack",
        [shape((2 * quads, cols, LANES), BF16), shape((4 * rows, cols), BF16), side, side],
        [scratch(channels * rows, cols)],
        source,
        target,
        flow_cotangent,
    )
    ra, rb = pair_exchange(to_a, to_b, "row")
    taps = shape((3, 2 * LANES, LANES), BF16)
    keys, forward, back, mask = call(
        early_kernel,
        "early",
        [
            shape((groups, rows, KEYS, LANES), BF16),
            taps,
            taps,
            shape((SPAN, KEYS, LANES), F32),
        ],
        [scratch(width, LANES)],
        own,
        conv_weight,
        flipped,
        cycles=2000,
    )
    strip = shape((2 * ext * HALO + 4 * ext * QUAD, LANES), BF16)
    to_c, to_d = call(
        strip_kernel,
        "strip",
        [strip, strip],
        [scratch(2, 2 * ext * HALO, LANES)],
        own,
        flow,
        ra,
        rb,
    )
    rc, rd = pair_exchange(to_c, to_d, "col")
    stages = [scratch(2, SPAN * KEYS, LANES), scratch(2, SPAN * KEYS, LANES, dtype=BF16)]
    inner = [
        scratch(asked, groups, LANES, LANES, dtype=BF16),
        scratch(asked, cols, LANES),
        scratch(asked, cols, LANES),
        scratch(asked, cols, LANES),
        scratch(2, groups, ext * QUAD, LANES),
    ]
    outer = [scratch(2, ext, KEYS, LANES), scratch(QUAD, 2, ext, KEYS, LANES)]
    keys, grad_keys, grad_feat, terms = call(
        middle_kernel,
        "middle",
        [
            shape((groups, ext * QUAD, KEYS, LANES), BF16),
            shape((groups, ext * QUAD, KEYS, LANES), F32),
            shape((quads, cols, LANES), BF16),
            shape((3, LANES, 2 * LANES), F32),
        ],
        [scratch(ext, width, LANES), scratch(4, width, LANES)]
        + inner
        + [scratch(asked, 3, cols, 2 * LANES, dtype=BF16)]
        + stages,
        own,
        flow,
        ra,
        rb,
        keys,
        forward,
        mask,
        cycles=7000,
    )
    pairs = quads // 2
    edge_keys, edge_feat, terms = call(
        edge_kernel,
        "edge",
        [
            shape((pairs, SPAN, KEYS, LANES), F32),
            shape((pairs, GROUP, LANES), BF16),
            shape((3 * CH, LANES), F32),
        ],
        outer
        + [
            scratch(pairs, SPAN, KEYS, LANES, dtype=BF16),
            scratch(pairs, LANES, LANES, dtype=BF16),
            scratch(2, 2, ext * QUAD, LANES),
        ]
        + stages,
        own,
        flow,
        ra,
        rb,
        rc,
        rd,
        forward,
        mask,
        terms,
    )
    grad_source, grad_target = call(
        late_kernel,
        "late",
        [shape(source.shape, BF16), shape(target.shape, BF16)],
        [scratch(ext, width, LANES)]
        + inner
        + [scratch(groups, ext * QUAD, KEYS, LANES)]
        + outer
        + [
            scratch(1, SPAN, KEYS, LANES, dtype=BF16),
            scratch(1, LANES, LANES, dtype=BF16),
            scratch(2, 2, ext * QUAD, LANES),
            scratch(pairs + 1, SPAN, KEYS, LANES),
            scratch(asked, 8 + cols, LANES),
            scratch(channels * rows, cols),
        ]
        + stages,
        own,
        flow,
        ra,
        rb,
        rc,
        rd,
        forward,
        back,
        mask,
        keys,
        grad_keys,
        grad_feat,
        edge_keys,
        edge_feat,
        cycles=6000,
    )
    pixels = rows * cols * lax.axis_size("row") * lax.axis_size("col")
    terms = sum_over(sum_over(terms, "row"), "col") / math.sqrt(pixels)
    terms = terms.reshape(3, CH, QUAD, CH)[:, :, :3]
    return (grad_source, grad_target, jnp.transpose(terms, (2, 0, 3, 1)))


def solution(mesh):
    placed = (
        P(None, ("sec", "row"), "col"),
        P(None, ("sec", "row"), "col"),
        P(),
        P(None, ("sec", "row"), "col"),
    )
    return jax.shard_map(
        per_device,
        mesh=mesh,
        in_specs=placed,
        out_specs=(
            P(None, ("sec", "row"), "col"),
            P(None, ("sec", "row"), "col"),
            P("sec", None, None, None),
        ),
        check_vma=False,
    )
```

```python
import functools
import math

import jax
import jax.numpy as jnp
from jax import lax
from jax.experimental import pallas as pl
from jax.experimental.pallas import tpu as pltpu
from jax.sharding import PartitionSpec as P

RADIUS = 4
SHARPNESS = 4.0
CH = 32
QUAD = 4
LANES = QUAD * CH
GROUP = 32
HALO = 2 * RADIUS
F32 = jnp.float32
BF16 = jnp.bfloat16


def lane_group(shape):
    return lax.broadcasted_iota(jnp.int32, shape, len(shape) - 1) // CH


def by_group(values):
    lane = lax.broadcasted_iota(jnp.int32, values[0].shape, values[0].ndim - 1)
    low = jnp.where(lane < CH, values[0], values[1])
    high = jnp.where(lane < 3 * CH, values[2], values[3])
    return jnp.where(lane < 2 * CH, low, high)


def roll_groups(value, steps):
    steps = steps % QUAD
    if steps == 0:
        return value
    return pltpu.roll(value, steps * CH, value.ndim - 1)


def group_sum(value, ones):
    high = value.astype(BF16)
    low = (value - high.astype(F32)).astype(BF16)
    both = jnp.concatenate([high, low], axis=1)
    return jnp.dot(both, ones, preferred_element_type=F32)


def group_ones():
    row = lax.broadcasted_iota(jnp.int32, (2 * LANES, LANES), 0) % LANES
    col = lax.broadcasted_iota(jnp.int32, (2 * LANES, LANES), 1)
    return jnp.where(row // CH == col // CH, 1.0, 0.0).astype(BF16)


def even(axis):
    return lax.rem(lax.axis_index(axis), 2) == 0


def pack_kernel(
    src_hbm, tgt_hbm, flow_hbm, own_ref, fl_ref, sa_ref, sb_ref,
    wide_ref, src_ref, tgt_ref, flow_ref, sem_ref,
):
    channels, rows, cols = src_ref.shape
    quads = rows // QUAD
    copies = [
        pltpu.make_async_copy(src, dst, sem_ref.at[index])
        for index, (src, dst) in enumerate(
            ((tgt_hbm, tgt_ref), (src_hbm, src_ref), (flow_hbm, flow_ref))
        )
    ]
    for copy in copies:
        copy.start()
    for base, ref in ((0, tgt_ref), (quads, src_ref)):
        copies[base // quads].wait()
        wide_ref[...] = ref[...].astype(F32).reshape(channels * rows, cols)
        for q in range(quads):
            part = jnp.concatenate(
                [wide_ref[pl.ds(q * QUAD + i, channels, stride=rows), :] for i in range(QUAD)],
                axis=0,
            )
            own_ref[base + q] = part.T.astype(BF16)
    copies[2].wait()
    pieces = []
    for f in range(2):
        value = flow_ref[f]
        high = value.astype(BF16).astype(F32)
        pieces += [high, value - high]
    fl_ref[...] = jnp.concatenate(pieces, axis=0).astype(BF16)
    is_even = even("row")
    last = quads - HALO // QUAD
    for dst, first in (
        (sa_ref, jnp.where(is_even, last, 0)),
        (sb_ref, jnp.where(is_even, 0, last)),
    ):
        for k in range(HALO // QUAD):
            dst[k * cols : (k + 1) * cols] = own_ref[first + k]
            dst[(2 + k) * cols : (3 + k) * cols] = own_ref[quads + first + k]
    top = jnp.concatenate([p[:HALO] for p in pieces], axis=0)
    low = jnp.concatenate([p[rows - HALO :] for p in pieces], axis=0)
    sa_ref[4 * cols :] = jnp.where(is_even, low, top).astype(BF16)
    sb_ref[4 * cols :] = jnp.where(is_even, top, low).astype(BF16)


def pick(flag, first, second):
    return jnp.where(flag, first.astype(F32), second.astype(F32))


def strip_kernel(own_ref, fl_ref, ra_ref, rb_ref, sc_ref, sd_ref, wide_ref):
    planes, cols, _ = own_ref.shape
    quads = planes // 2
    rows = quads * QUAD
    r_even = even("row")
    c_even = even("col")

    def strips(read):
        return read(0, 2 * HALO)[:HALO], read(cols - 2 * HALO, 2 * HALO)[HALO:]

    for kind in range(2):
        for q in range(quads + 4):
            if 2 <= q < quads + 2:
                plane = kind * quads + q - 2
                left, right = strips(lambda at, n: own_ref[plane, at : at + n].astype(F32))
            else:
                down = q >= quads + 2
                at0 = (2 * kind + (q - quads - 2 if down else q)) * cols
                flag = r_even if down else jnp.logical_not(r_even)
                left, right = strips(
                    lambda at, n: pick(
                        flag, ra_ref[at0 + at : at0 + at + n], rb_ref[at0 + at : at0 + at + n]
                    )
                )
            row = (kind * (quads + 4) + q) * HALO
            wide_ref[0, row : row + HALO] = jnp.where(c_even, right, left)
            wide_ref[1, row : row + HALO] = jnp.where(c_even, left, right)
    count = 2 * (quads + 4) * HALO
    sc_ref[:count] = wide_ref[0].astype(BF16)
    sd_ref[:count] = wide_ref[1].astype(BF16)
    a, b = (ra_ref[4 * cols :], rb_ref[4 * cols :])
    up, down = (pick(r_even, b, a), pick(r_even, a, b))
    flow = []
    own = fl_ref[...].astype(F32)
    for v in range(4):
        flow += [
            up[v * HALO : (v + 1) * HALO],
            own[v * rows : (v + 1) * rows],
            down[v * HALO : (v + 1) * HALO],
        ]
    flow = jnp.concatenate(flow, axis=0).astype(BF16)
    sc_ref[count:] = flow
    sd_ref[count:] = flow


def fill_taps(dst_ref, w_ref):
    zero = jnp.zeros((CH, CH), F32)
    for dx in range(3):
        for block in range(2 * QUAD):
            row = block if block < QUAD else {QUAD: QUAD, 2 * QUAD - 1: -1}.get(block)
            parts = []
            for out in range(QUAD):
                tap = None if row is None else row - out + 1
                ok = tap is not None and 0 <= tap < 3
                parts.append(w_ref[tap, dx].astype(F32) if ok else zero)
            dst_ref[dx, block * CH : (block + 1) * CH, :] = jnp.concatenate(parts, axis=1).astype(
                BF16
            )


def taps_of(ref, quad, start, count):
    main = ref[quad, pl.ds(start, count), :]
    after = ref[quad + 1, pl.ds(start, count), :]
    before = ref[quad - 1, pl.ds(start, count), :]
    lane = lax.broadcasted_iota(jnp.int32, main.shape, 1)
    beside = jnp.where(lane < 2 * CH, after, before)
    return jnp.concatenate([main, beside], axis=1).astype(BF16)


def conv(ref, quad, start, count, w_ref):
    total = jnp.zeros((count, LANES), F32)
    for dx in range(3):
        total += jnp.dot(
            taps_of(ref, quad, start + dx - 1, count), w_ref[dx], preferred_element_type=F32
        )
    return total


SPAN = 3 * QUAD
KEYS = 16


def halo_plane(kind, q, own_ref, ra_ref, rb_ref):
    planes, cols, _ = own_ref.shape
    quads = planes // 2
    if 2 <= q < quads + 2:
        return own_ref[kind * quads + q - 2].astype(F32)
    down = q >= quads + 2
    at = (2 * kind + (q - quads - 2 if down else q)) * cols
    flag = even("row") if down else jnp.logical_not(even("row"))
    return pick(flag, ra_ref[at : at + cols], rb_ref[at : at + cols])


def sides_of(rc, rd):
    flag = even("col")
    return pick(flag, rd, rc), pick(flag, rc, rd)


def edge_plane(kind, q, side, own_ref, ra_ref, rb_ref, rc_ref, rd_ref):
    planes, cols, _ = own_ref.shape
    quads = planes // 2
    tile = slice(0, KEYS) if side == 0 else slice(cols - KEYS, cols)
    if 2 <= q < quads + 2:
        mine = own_ref[kind * quads + q - 2, tile].astype(F32)
    else:
        down = q >= quads + 2
        at = (2 * kind + (q - quads - 2 if down else q)) * cols
        tile = slice(at + tile.start, at + tile.stop)
        flag = even("row") if down else jnp.logical_not(even("row"))
        mine = pick(flag, ra_ref[tile], rb_ref[tile])
    index = kind * (quads + 4) + q
    at = index // 2 * 2 * HALO
    fetched = sides_of(rc_ref[at : at + 2 * HALO], rd_ref[at : at + 2 * HALO])[side]
    fetched = fetched[index % 2 * HALO : index % 2 * HALO + HALO]
    parts = [fetched, mine[:HALO]] if side == 0 else [mine[HALO:], fetched]
    return jnp.concatenate(parts, axis=0)


def flow_up_down(ra_ref, rb_ref):
    at = ra_ref.shape[0] - 4 * HALO
    a, b = (ra_ref[at:], rb_ref[at:])
    flag = even("row")
    return pick(flag, b, a), pick(flag, a, b)


def flow_part(f, ref_or_value, rows):
    parts = [ref_or_value[v * rows : (v + 1) * rows].astype(F32) for v in (2 * f, 2 * f + 1)]
    return parts[0] + parts[1]


def flow_mid(f, fl_ref, ra_ref, rb_ref):
    up, down = flow_up_down(ra_ref, rb_ref)
    return jnp.concatenate(
        [
            flow_part(f, up, HALO),
            flow_part(f, fl_ref, fl_ref.shape[0] // 4),
            flow_part(f, down, HALO),
        ],
        axis=0,
    )


def flow_inner(p_ref, values):
    groups = p_ref.shape[1]
    for f in range(2):
        mid = pltpu.roll(values[f], LANES - RADIUS, 1)
        lane = lax.broadcasted_iota(jnp.int32, mid.shape, 1)
        row = lax.broadcasted_iota(jnp.int32, mid.shape, 0)
        mid = jnp.where(lane < LANES - 8, mid, 0.0)
        turned = [roll_groups(mid, k) for k in range(QUAD)]
        for g in range(groups):
            total = jnp.zeros(mid.shape, F32)
            for i in range(QUAD):
                keep = jnp.logical_and(row % QUAD == i, lane // CH == i)
                total = jnp.where(keep, turned[(i - g) % QUAD], total)
            p_ref[f, g] = total


def flow_edge(e_ref, fl_ref, ra_ref, rb_ref, rc_ref, rd_ref):
    rows = fl_ref.shape[0] // 4
    ext = rows + 2 * HALO
    base = rc_ref.shape[0] - 4 * ext
    left, right = sides_of(rc_ref[base:], rd_ref[base:])
    for f in range(2):
        mid = flow_mid(f, fl_ref, ra_ref, rb_ref)
        at = 2 * f * ext
        lf = left[at : at + ext] + left[at + ext : at + 2 * ext]
        rt = right[at : at + ext] + right[at + ext : at + 2 * ext]
        lane = lax.broadcasted_iota(jnp.int32, mid.shape, 1)
        row = lax.broadcasted_iota(jnp.int32, mid.shape, 0)
        low = jnp.where(lane < RADIUS, pltpu.roll(lf, RADIUS, 1), pltpu.roll(mid, RADIUS, 1))
        high = jnp.where(
            lane < 3 * RADIUS, pltpu.roll(mid, 3 * RADIUS, 1), pltpu.roll(rt, 3 * RADIUS, 1)
        )
        both = jnp.where(lane < 8, low, high)
        for h in range(2):
            total = jnp.zeros(mid.shape, F32)
            for i in range(QUAD):
                turn = i * CH + h * 16
                keep = jnp.logical_and(row % QUAD == i, lane // 16 == 2 * i + h)
                total = jnp.where(keep, pltpu.roll(both, turn, 1) if turn else both, total)
            e_ref[f, h] = total


def fill_mask(m_ref):
    key = lax.broadcasted_iota(jnp.int32, (SPAN, KEYS, LANES), 0)
    kx = lax.broadcasted_iota(jnp.int32, (SPAN, KEYS, LANES), 1)
    lane = lax.broadcasted_iota(jnp.int32, (SPAN, KEYS, LANES), 2)
    dy = key - lane // CH
    dx = kx - lane % 8
    ok = (dy >= 0) & (dy <= 2 * RADIUS) & (dx >= 0) & (dx <= 2 * RADIUS)
    m_ref[...] = jnp.where(ok, 1.0, 0.0)


def softmax_block(score_ref, m_ref, f0, f1, scale):
    lane = lax.broadcasted_iota(jnp.int32, (KEYS, LANES), 1)
    at_y = (lane // CH + RADIUS).astype(F32)
    at_x = (lane % 8 + RADIUS).astype(F32)
    key_x = lax.broadcasted_iota(jnp.int32, (KEYS, LANES), 0).astype(F32)
    f0 = jnp.broadcast_to(f0, (KEYS, LANES))
    f1 = jnp.broadcast_to(f1, (KEYS, LANES))
    side = f1 * (key_x - at_x) - f0 * at_y
    weights = []
    total = jnp.zeros((KEYS, LANES), F32)
    lean = jnp.zeros((KEYS, LANES), F32)
    for y in range(SPAN):
        weight = score_ref[KEYS * y : KEYS * (y + 1)] * (scale * math.log2(math.e))
        weight = jnp.exp2(weight) * m_ref[y]
        weights.append(weight)
        total = total + weight
        lean = lean + weight * (f0 * float(y) + side)
    total = jnp.sum(total, axis=0, keepdims=True)
    lean = jnp.sum(lean, axis=0, keepdims=True)
    base = jnp.broadcast_to(lean / total, (KEYS, LANES))
    factor = jnp.broadcast_to(scale / total, (KEYS, LANES))
    step = f0 * factor
    side = (side - base) * factor
    return jnp.concatenate(
        [(weights[y] * (step * float(y) + side)).astype(BF16) for y in range(SPAN)], axis=0
    )


def unit_of(field, ones):
    recip = lax.rsqrt(group_sum(field * field, ones) * (1.0 / CH) + 1.0)
    return recip, (field * recip).astype(BF16).astype(F32)


def unit_grad(field, recip, grad, ones):
    inner = group_sum(grad * field, ones)
    return recip * grad - field * (recip * recip * recip) * inner * (1.0 / CH)


def key_rows(t4_ref, first, unit):
    turned = [roll_groups(unit, k) for k in range(QUAD)]
    for i in range(QUAD):
        for g in range(t4_ref.shape[0]):
            t4_ref[g, first + i] = by_group(
                [
                    turned[(j - i) % QUAD][g * GROUP + 8 * j : g * GROUP + 8 * j + KEYS]
                    for j in range(QUAD)
                ]
            ).astype(BF16)


def query_block(octs):
    group = lane_group((8, LANES))
    turned = [
        roll_groups(by_group([octs[(i + k) % QUAD] for i in range(QUAD)]), k)
        for k in range(QUAD)
    ]
    parts = [
        jnp.where(group == j, turned[(j - i) % QUAD], 0.0)
        for i in range(QUAD)
        for j in range(QUAD)
    ]
    return jnp.concatenate(parts, axis=0).astype(BF16)


def packed_rows(mine):
    def piece(i, j):
        at = i * GROUP + 8 * j
        return mine[at : at + 8]

    turned = [
        roll_groups(by_group([piece((j + k) % QUAD, j) for j in range(QUAD)]), k)
        for k in range(QUAD)
    ]
    return [by_group([turned[(i - j) % QUAD] for i in range(QUAD)]) for j in range(QUAD)]


def run_blocks(blocks, m_ref, sc_ref, d_ref, scale):
    def score(b):
        sc_ref[b % 2] = lax.dot_general(
            blocks[b][0](), blocks[b][1](), (((1,), (1,)), ((), ())), preferred_element_type=F32
        )

    def collect(b):
        dscore = d_ref[b % 2]
        keys, queries, _, wanted, put_keys, put_rows = blocks[b]
        put_keys(jnp.dot(dscore[wanted], queries(), preferred_element_type=F32))
        mine = lax.dot_general(
            dscore, keys(), (((0,), (0,)), ((), ())), preferred_element_type=F32
        )
        put_rows(packed_rows(mine))

    score(0)
    for b in range(len(blocks)):
        if b + 1 < len(blocks):
            score(b + 1)
        f0, f1 = blocks[b][2]()
        d_ref[b % 2] = softmax_block(sc_ref.at[b % 2], m_ref, f0, f1, scale)
        if b > 0:
            collect(b - 1)
    collect(len(blocks) - 1)


def conv_from(tap_list, w_ref):
    total = None
    for dx in range(3):
        term = jnp.dot(tap_list[dx], w_ref[dx], preferred_element_type=F32)
        total = term if total is None else total + term
    return total


def inner_block(n, g, keys, q_ref, p_ref, p_quad, ga_ref, gu_ref):
    rows = slice(p_quad * QUAD, (p_quad + 1) * QUAD)
    own = ga_ref.shape[1]
    first = n * QUAD - HALO
    low, high = max(first, 0), min(first + SPAN, own)
    wanted = slice((low - first) * KEYS, (high - first) * KEYS)

    def put_keys(value):
        ga_ref[g, low:high] = ga_ref[g, low:high] + value.reshape(high - low, KEYS, LANES)

    def put_rows(octs):
        for j in range(QUAD):
            gu_ref[n, g * GROUP + 8 * j : g * GROUP + 8 * j + 8] = octs[j]

    return (
        lambda: keys(n, g),
        lambda: q_ref[n, g],
        lambda: [jnp.sum(p_ref[f, g, rows, :], axis=0, keepdims=True) for f in range(2)],
        wanted,
        put_keys,
        put_rows,
    )


def inner_queries(n, es_ref, taps_ref, fe_ref, rf_ref, q_ref, ones, keep=None):
    cols = fe_ref.shape[1]
    tap_list = [taps_of(es_ref, n + 1, RADIUS + dx - 1, cols) for dx in range(3)]
    if keep is not None:
        for dx in range(3):
            keep[n, dx] = tap_list[dx]
    feat = conv_from(tap_list, taps_ref).astype(BF16).astype(F32)
    fe_ref[n] = feat
    recip, unit = unit_of(feat, ones)
    rf_ref[n] = recip
    for g in range(cols // GROUP):
        q_ref[n, g] = query_block(
            [unit[g * GROUP + 8 * j : g * GROUP + 8 * j + 8] for j in range(QUAD)]
        )


def fill_plane(dst_ref, q, value):
    cols = value.shape[0]
    dst_ref[q, :cols] = value
    dst_ref[q, cols:] = jnp.zeros((dst_ref.shape[1] - cols, LANES), F32)


def own_rows(
    quads_of, keys, es_ref, taps_ref, m_ref, p_ref, ga_ref, gf_out, gw_out,
    q_ref, fe_ref, rf_ref, gu_ref, tap_ref, sc_ref, d_ref, ones,
):
    cols = fe_ref.shape[1]
    for n in quads_of:
        inner_queries(n, es_ref, taps_ref, fe_ref, rf_ref, q_ref, ones, tap_ref)
    run_blocks(
        [
            inner_block(n, g, keys, q_ref, p_ref, n - 1, ga_ref, gu_ref)
            for n in quads_of
            for g in range(cols // GROUP)
        ],
        m_ref, sc_ref, d_ref, SHARPNESS / math.sqrt(CH),
    )
    row = lax.broadcasted_iota(jnp.int32, (cols, LANES), 0)
    values = []
    for index, n in enumerate(quads_of):
        value = unit_grad(fe_ref[n], rf_ref[n], gu_ref[n], ones)
        value = jnp.where(row < cols - 8, value, 0.0).astype(BF16)
        gf_out[index] = value
        values.append(value)
    value = jnp.concatenate(values, axis=0)
    for dx in range(3):
        others = jnp.concatenate([tap_ref[n, dx] for n in quads_of], axis=0)
        gw_out[dx] = gw_out[dx] + lax.dot_general(
            value, others, (((0,), (0,)), ((), ())), preferred_element_type=F32
        )


def early_kernel(
    own_ref, fl_ref, w_ref, wt_ref,
    t4_out, taps_out, back_out, m_out, p_out, ga_out, gf_out, gw_out,
    es_ref, q_ref, fe_ref, rf_ref, gu_ref, tap_ref, sc_ref, d_ref,
):
    planes, cols, _ = own_ref.shape
    quads = planes // 2
    width = es_ref.shape[1]
    ones = group_ones()
    fill_taps(taps_out, w_ref)
    fill_taps(back_out, wt_ref)
    fill_mask(m_out)
    flow_inner(p_out, [flow_part(f, fl_ref, quads * QUAD) for f in range(2)])
    for q in range(quads):
        fill_plane(es_ref, q + 2, own_ref[quads + q].astype(F32))
        _, unit = unit_of(own_ref[q].astype(F32), ones)
        pad = jnp.zeros((width - cols, LANES), F32)
        key_rows(t4_out, q * QUAD, jnp.concatenate([unit, pad], axis=0))
    ga_out[...] = jnp.zeros_like(ga_out)
    gw_out[...] = jnp.zeros_like(gw_out)

    def keys(n, g):
        at = (n - 2) * QUAD
        return t4_out[g, at : at + SPAN].reshape(SPAN * KEYS, LANES)

    own_rows(
        range(2, quads), keys, es_ref, taps_out, m_out, p_out, ga_out, gf_out, gw_out,
        q_ref, fe_ref, rf_ref, gu_ref, tap_ref, sc_ref, d_ref, ones,
    )


def middle_kernel(
    own_ref, ra_ref, rb_ref, t4_ref, taps_ref, m_ref, p_ref, ga_in, gw_in,
    t4_out, ga_out, gf_out, gw_out,
    es_ref, q_ref, fe_ref, rf_ref, gu_ref, tap_ref, sc_ref, d_ref,
):
    planes, cols, _ = own_ref.shape
    quads = planes // 2
    width = es_ref.shape[1]
    ones = group_ones()
    for q in (1, 2, 3, quads, quads + 1, quads + 2):
        fill_plane(es_ref, q, halo_plane(1, q, own_ref, ra_ref, rb_ref))
    pad = jnp.zeros((width - cols, LANES), F32)
    for k, q in enumerate((1, quads + 2)):
        _, unit = unit_of(halo_plane(0, q, own_ref, ra_ref, rb_ref), ones)
        key_rows(t4_out, k * QUAD, jnp.concatenate([unit, pad], axis=0))

    def keys(n, g):
        if n == 1:
            parts = [t4_out[g, :QUAD], t4_ref[g, : 2 * QUAD]]
        else:
            parts = [t4_ref[g, (quads - 2) * QUAD :], t4_out[g, QUAD:]]
        return jnp.concatenate(parts, axis=0).reshape(SPAN * KEYS, LANES)

    own_rows(
        (1, quads), keys, es_ref, taps_ref, m_ref, p_ref, ga_out, gf_out, gw_out,
        q_ref, fe_ref, rf_ref, gu_ref, tap_ref, sc_ref, d_ref, ones,
    )


def edge_blocks(
    pairs, first, ee_ref, tu_ref, taps_ref, t4_ref, q_ref, ep_ref, ga_ref, ones, keep=None
):
    blocks, stores = [], []
    for e, pair in enumerate(pairs):
        quad_of = [pair[j // 2] for j in range(QUAD)]
        tap_list = [
            jnp.concatenate(
                [
                    taps_of(ee_ref.at[j % 2], quad_of[j] + 1, RADIUS + dx - 1, 8).astype(F32)
                    for j in range(QUAD)
                ],
                axis=0,
            ).astype(BF16)
            for dx in range(3)
        ]
        feat = conv_from(tap_list, taps_ref).astype(BF16).astype(F32)
        recip, unit = unit_of(feat, ones)
        q_ref[e] = query_block([unit[8 * j : 8 * j + 8] for j in range(QUAD)])
        for y in range(SPAN):
            t4_ref[e, y] = by_group(
                [
                    tu_ref[(j - y) % QUAD, j % 2, quad_of[j] + y // QUAD]
                    for j in range(QUAD)
                ]
            ).astype(BF16)
        result = []
        stores.append((tap_list, feat, recip, result))

        def flows(pair=pair):
            total = []
            for f in range(2):
                parts = [
                    jnp.sum(
                        ep_ref[f, h, (pair[h] + 1) * QUAD : (pair[h] + 2) * QUAD, :],
                        axis=0,
                        keepdims=True,
                    )
                    for h in range(2)
                ]
                total.append(parts[0] + parts[1])
            return total

        def put_keys(value, e=e):
            ga_ref[first + e] = value.reshape(SPAN, KEYS, LANES)

        blocks.append(
            (
                lambda e=e: t4_ref[e].reshape(SPAN * KEYS, LANES),
                lambda e=e: q_ref[e],
                flows,
                slice(0, SPAN * KEYS),
                put_keys,
                result.extend,
            )
        )
    return blocks, stores


def edge_planes(ee_ref, tu_ref, ones, quads_of, keys_of, refs):
    for side in range(2):
        for q in quads_of:
            ee_ref[side, q] = edge_plane(1, q, side, *refs)
        raw = jnp.concatenate([edge_plane(0, q, side, *refs) for q in keys_of], axis=0)
        _, unit = unit_of(raw, ones)
        for k in range(QUAD):
            turned = roll_groups(unit, k)
            for index, q in enumerate(keys_of):
                tu_ref[k, side, q] = turned[index * KEYS : (index + 1) * KEYS]


def edge_grads(stores, ones):
    return [
        unit_grad(feat, recip, jnp.concatenate(result, axis=0), ones).astype(BF16)
        for _, feat, recip, result in stores
    ]


def pairs_of(quads):
    return [(n, n + 1) for n in range(1, quads + 1, 2)]


def edge_kernel(
    own_ref, fl_ref, ra_ref, rb_ref, rc_ref, rd_ref, taps_ref, m_ref, gw_ref,
    ga_ref, gf_out, gw_out,
    ee_ref, tu_ref, t4_ref, q_ref, ep_ref, sc_ref, d_ref,
):
    planes, cols, _ = own_ref.shape
    quads = planes // 2
    ext = quads + 4
    scale = SHARPNESS / math.sqrt(CH)
    ones = group_ones()
    refs = (own_ref, ra_ref, rb_ref, rc_ref, rd_ref)
    edge_planes(ee_ref, tu_ref, ones, range(1, ext - 1), range(1, ext - 1), refs)
    flow_edge(ep_ref, fl_ref, ra_ref, rb_ref, rc_ref, rd_ref)
    blocks, stores = edge_blocks(
        pairs_of(quads), 0, ee_ref, tu_ref, taps_ref, t4_ref, q_ref, ep_ref, ga_ref, ones
    )
    run_blocks(blocks, m_ref, sc_ref, d_ref, scale)
    totals = [gw_ref[dx] for dx in range(3)]
    row = lax.broadcasted_iota(jnp.int32, (GROUP, LANES), 0)
    inside = jnp.logical_xor(row // 8 % 2 == 0, row % 8 < RADIUS)
    for e, grad in enumerate(edge_grads(stores, ones)):
        gf_out[e] = grad
        grad = jnp.where(inside, grad.astype(F32), 0.0).astype(BF16)
        for dx in range(3):
            totals[dx] = totals[dx] + lax.dot_general(
                grad, stores[e][0][dx], (((0,), (0,)), ((), ())), preferred_element_type=F32
            )
    lane = lax.broadcasted_iota(jnp.int32, (CH, LANES), 1)
    for dx, total in enumerate(totals):
        rows_of = [total[i * CH : (i + 1) * CH] for i in range(QUAD)]
        main = [x[:, :LANES] for x in rows_of]
        beside = [x[:, LANES:] for x in rows_of]
        start = jnp.where(lane < CH, roll_groups(beside[0], 1), roll_groups(main[0], 1))
        last = jnp.where(lane < 2 * CH, roll_groups(main[3], 2), roll_groups(beside[3], 2))
        gw_out[dx * CH : (dx + 1) * CH] = (start + main[1]) + (roll_groups(main[2], 3) + last)


def spread(dst_ref, quad, value, channels, rows):
    flipped = value.T
    for i in range(QUAD):
        dst_ref[pl.ds(quad * QUAD + i, channels, stride=rows), :] = flipped[
            i * CH : (i + 1) * CH
        ]


def outer_kernel(
    lower, own_ref, ra_ref, rb_ref, taps_ref, m_ref, t4_own, t4_halo, ga_in,
    ga_out, gf_out,
    es_ref, t4_ref, q_ref, fe_ref, rf_ref, gu_ref, p_ref, sc_ref, d_ref,
):
    planes, cols, _ = own_ref.shape
    quads = planes // 2
    width = es_ref.shape[1]
    ones = group_ones()
    n = quads + 1 if lower else 0
    for q in (n, n + 1, n + 2):
        fill_plane(es_ref, q, halo_plane(1, q, own_ref, ra_ref, rb_ref))
    flow_inner(
        p_ref, [flow_part(f, flow_up_down(ra_ref, rb_ref)[lower], HALO) for f in range(2)]
    )
    _, unit = unit_of(halo_plane(0, quads + 3 if lower else 0, own_ref, ra_ref, rb_ref), ones)
    pad = jnp.zeros((width - cols, LANES), F32)
    key_rows(t4_ref, 0, jnp.concatenate([unit, pad], axis=0))

    def keys(n, g):
        if lower:
            parts = [t4_own[g, (quads - 1) * QUAD :], t4_halo[g, QUAD:], t4_ref[g]]
        else:
            parts = [t4_ref[g], t4_halo[g, :QUAD], t4_own[g, :QUAD]]
        return jnp.concatenate(parts, axis=0).reshape(SPAN * KEYS, LANES)

    inner_queries(n, es_ref, taps_ref, fe_ref, rf_ref, q_ref, ones)
    run_blocks(
        [
            inner_block(n, g, keys, q_ref, p_ref, 0 if lower else 1, ga_out, gu_ref)
            for g in range(cols // GROUP)
        ],
        m_ref, sc_ref, d_ref, SHARPNESS / math.sqrt(CH),
    )
    gf_out[...] = unit_grad(fe_ref[n], rf_ref[n], gu_ref[n], ones).astype(BF16)


def corner_kernel(
    own_ref, fl_ref, ra_ref, rb_ref, rc_ref, rd_ref, taps_ref, m_ref,
    ge_out, gf_out,
    ee_ref, tu_ref, t4_ref, q_ref, ep_ref, sc_ref, d_ref,
):
    quads = own_ref.shape[0] // 2
    ext = quads + 4
    ones = group_ones()
    refs = (own_ref, ra_ref, rb_ref, rc_ref, rd_ref)
    near = (0, 1, 2, ext - 3, ext - 2, ext - 1)
    edge_planes(ee_ref, tu_ref, ones, near, near, refs)
    flow_edge(ep_ref, fl_ref, ra_ref, rb_ref, rc_ref, rd_ref)
    blocks, stores = edge_blocks(
        [(0, quads + 1)], 0, ee_ref, tu_ref, taps_ref, t4_ref, q_ref, ep_ref, ge_out, ones
    )
    run_blocks(blocks, m_ref, sc_ref, d_ref, SHARPNESS / math.sqrt(CH))
    gf_out[...] = edge_grads(stores, ones)[0]


def image_kernel(
    own_ref, back_ref, ga_ref, gem_ref, gec_ref,
    gf_early, gf_middle, gf_top, gf_low, gfe_ref, gfc_ref,
    gs_out, gt_out,
    full_ref, wide_ref,
):
    channels, rows, cols = gs_out.shape
    quads = rows // QUAD
    ones = group_ones()
    rows_of = {0: gf_top[...], quads + 1: gf_low[...], 1: gf_middle[0], quads: gf_middle[1]}
    for n in range(2, quads):
        rows_of[n] = gf_early[n - 2]
    for n, value in rows_of.items():
        full_ref[n, 8 : 8 + cols] = value.astype(F32)
    edges = [gfe_ref[e] for e in range(quads // 2)] + [gfc_ref[...]]
    where_is = {}
    for e, (pair, grad) in enumerate(zip(pairs_of(quads) + [(0, quads + 1)], edges)):
        grad = grad.astype(F32)
        for j in range(QUAD):
            at = 0 if j % 2 == 0 else cols
            full_ref[pair[j // 2], at : at + 8] = grad[8 * j : 8 * j + 8]
            where_is[pair[j // 2], j % 2] = (e, j)

    for q in range(quads):
        tap_list = [taps_of(full_ref, q + 1, RADIUS + dx - 1, cols) for dx in range(3)]
        spread(wide_ref, q, conv_from(tap_list, back_ref), channels, rows)
    gs_out[...] = wide_ref[...].astype(BF16).reshape(channels, rows, cols)

    group = lane_group((8, LANES))
    last = cols // 8
    for q in range(quads):
        parts = []
        for oct in range(1, last + 1):
            total = None
            for k in range(QUAD):
                both = jnp.zeros((8, LANES), F32)
                for half, which in ((0, oct), (1, oct - 1)):
                    if not 0 < which < last:
                        continue
                    g, j = divmod(which - 1, QUAD)
                    at = q * QUAD + (j + k) % QUAD
                    both = jnp.where(group == j, ga_ref[g, at, 8 * half : 8 * half + 8], both)
                both = roll_groups(both, k)
                total = both if total is None else total + both
            side = 0 if oct == 1 else 1 if oct == last else None
            if side is not None:
                half = 1 - side
                for n in range(q, q + 3):
                    e, j = where_is[n, side]
                    ref = gem_ref.at[e] if e < quads // 2 else gec_ref.at[0]
                    for i in range(QUAD):
                        part = ref[(q + 2 - n) * QUAD + i, 8 * half : 8 * half + 8]
                        total = total + roll_groups(jnp.where(group == j, part, 0.0), i - j)
            parts.append(total)
        grad = jnp.concatenate(parts, axis=0)
        field = own_ref[q].astype(F32)
        recip = lax.rsqrt(group_sum(field * field, ones) * (1.0 / CH) + 1.0)
        spread(wide_ref, q, unit_grad(field, recip, grad, ones), channels, rows)
    gt_out[...] = wide_ref[...].astype(BF16).reshape(channels, rows, cols)


def final_kernel(scale, one_ref, two_ref, out_ref):
    for dx in range(3):
        at = slice(dx * CH, (dx + 1) * CH)
        total = ((one_ref[at] + two_ref[at]) * scale).T
        for tap in range(3):
            out_ref[tap, dx] = total[tap * CH : (tap + 1) * CH]


def pair_exchange(x, y, axis):
    size = lax.axis_size(axis)
    near = [(i, i ^ 1) for i in range(size)]
    far = []
    for i in range(1, size - 1, 2):
        far += [(i, i + 1), (i + 1, i)]
    second = lax.ppermute(y, axis, far)
    first = lax.ppermute(x, axis, near)
    return first, second


def swap(x, axis, step):
    return lax.ppermute(x, axis, [(i, i ^ step) for i in range(lax.axis_size(axis))])


def after(value, *others):
    return lax.optimization_barrier((value, *others))[0]


def vmem(count):
    return [pl.BlockSpec(memory_space=pltpu.VMEM)] * count


def per_device(source, target, conv_weight, flow_cotangent):
    channels, rows, cols = source.shape
    quads = rows // QUAD
    ext = quads + 4
    groups = cols // GROUP
    width = cols + HALO
    asked = quads + 2
    flipped = jnp.transpose(conv_weight[::-1, ::-1], (0, 1, 3, 2))
    shape = jax.ShapeDtypeStruct

    def scratch(*dims, dtype=F32):
        return pltpu.VMEM(dims, dtype)

    def call(kernel, name, outs, scratches, *args, cycles=1000, alias=None, specs=None):
        return pl.pallas_call(
            kernel,
            out_shape=tuple(outs),
            in_specs=specs or vmem(len(args)),
            out_specs=tuple(vmem(len(outs))),
            scratch_shapes=scratches,
            input_output_aliases=alias or {},
            cost_estimate=pl.CostEstimate(
                flops=cycles * 250_000, bytes_accessed=cycles * 1000, transcendentals=0
            ),
            compiler_params=pltpu.CompilerParams(vmem_limit_bytes=16 << 20),
            name=name,
        )(*args)

    side = shape((4 * cols + 4 * HALO, LANES), BF16)
    own, flow, to_a, to_b = call(
        pack_kernel,
        "pack",
        [shape((2 * quads, cols, LANES), BF16), shape((4 * rows, cols), BF16), side, side],
        [
            scratch(channels * rows, cols),
            scratch(*source.shape, dtype=BF16),
            scratch(*target.shape, dtype=BF16),
            scratch(*flow_cotangent.shape),
            pltpu.SemaphoreType.DMA((3,)),
        ],
        source,
        target,
        flow_cotangent,
        specs=[pl.BlockSpec(memory_space=pl.ANY)] * 3,
    )
    ra, rb = pair_exchange(to_a, to_b, "row")
    taps = shape((3, 2 * LANES, LANES), BF16)
    stages = [scratch(2, SPAN * KEYS, LANES), scratch(2, SPAN * KEYS, LANES, dtype=BF16)]
    inner = [
        scratch(asked, groups, LANES, LANES, dtype=BF16),
        scratch(asked, cols, LANES),
        scratch(asked, cols, LANES),
        scratch(asked, cols, LANES),
    ]
    planes = scratch(ext, width, LANES)
    tap_lists = scratch(asked, 3, cols, 2 * LANES, dtype=BF16)
    for_keys = shape((groups, rows, KEYS, LANES), F32)
    for_kernel = shape((3, LANES, 2 * LANES), F32)
    for_feat = shape((2, cols, LANES), BF16)
    keys, forward, back, mask, cotangents, grad_keys, feat_early, terms = call(
        early_kernel,
        "early",
        [
            shape((groups, rows, KEYS, LANES), BF16),
            taps,
            taps,
            shape((SPAN, KEYS, LANES), F32),
            shape((2, groups, rows, LANES), F32),
            for_keys,
            shape((quads - 2, cols, LANES), BF16),
            for_kernel,
        ],
        [planes] + inner + [tap_lists] + stages,
        own,
        flow,
        conv_weight,
        flipped,
        cycles=3000,
    )
    strip = shape((2 * ext * HALO + 4 * ext * QUAD, LANES), BF16)
    to_c, to_d = call(
        strip_kernel,
        "strip",
        [strip, strip],
        [scratch(2, 2 * ext * HALO, LANES)],
        own,
        flow,
        ra,
        rb,
    )
    rc, rd = pair_exchange(to_c, to_d, "col")
    halo_keys, grad_keys, feat_middle, terms = call(
        middle_kernel,
        "middle",
        [shape((groups, 2 * QUAD, KEYS, LANES), BF16), for_keys, for_feat, for_kernel],
        [planes] + inner + [tap_lists] + stages,
        own,
        ra,
        rb,
        keys,
        forward,
        mask,
        cotangents,
        grad_keys,
        terms,
        cycles=3000,
        alias={7: 1, 8: 3},
    )
    pairs = quads // 2
    outer = [scratch(2, ext, KEYS, LANES), scratch(QUAD, 2, ext, KEYS, LANES)]
    fetched = (own, flow, ra, rb, rc, rd, forward, mask)

    def edge_scratch(count):
        return outer + [
            scratch(count, SPAN, KEYS, LANES, dtype=BF16),
            scratch(count, LANES, LANES, dtype=BF16),
            scratch(2, 2, ext * QUAD, LANES),
        ] + stages

    edge_keys, edge_feat, terms = call(
        edge_kernel,
        "edge",
        [
            shape((pairs, SPAN, KEYS, LANES), F32),
            shape((pairs, GROUP, LANES), BF16),
            shape((3 * CH, LANES), F32),
        ],
        edge_scratch(pairs),
        *fetched,
        terms,
    )

    def outer_rows(lower, sums):
        return call(
            functools.partial(outer_kernel, lower),
            "lower" if lower else "upper",
            [for_keys, shape((cols, LANES), BF16)],
            [planes, scratch(groups, QUAD, KEYS, LANES, dtype=BF16)]
            + inner
            + [scratch(2, groups, HALO, LANES)]
            + stages,
            after(own, sums),
            ra,
            rb,
            forward,
            mask,
            keys,
            halo_keys,
            grad_keys,
            alias={7: 0},
            cycles=1500,
        )

    steps = []
    for axis in ("row", "col"):
        step = 1
        while step < lax.axis_size(axis):
            steps.append((axis, step))
            step *= 2
    for index, (axis, step) in enumerate(steps[:-1]):
        arriving = swap(terms, axis, step)
        ahead = len(steps) - 1 - index
        if ahead == 2:
            grad_keys, feat_top = outer_rows(0, terms)
            done = feat_top
        elif ahead == 1:
            grad_keys, feat_low = outer_rows(1, terms)
            corner_keys, corner_feat = call(
                corner_kernel,
                "corner",
                [shape((1, SPAN, KEYS, LANES), F32), shape((GROUP, LANES), BF16)],
                edge_scratch(1),
                after(own, terms),
                *fetched[1:],
            )
            done = (feat_low, corner_feat)
        else:
            done = None
        terms = terms + arriving
        if done is not None:
            terms = after(terms, done)
    arriving = swap(terms, *steps[-1])
    grad_source, grad_target = call(
        image_kernel,
        "image",
        [shape(source.shape, BF16), shape(target.shape, BF16)],
        [scratch(asked, 8 + cols, LANES), scratch(channels * rows, cols)],
        after(own, terms),
        back,
        grad_keys,
        edge_keys,
        corner_keys,
        feat_early,
        feat_middle,
        feat_top,
        feat_low,
        edge_feat,
        corner_feat,
        cycles=2000,
    )
    pixels = rows * cols * lax.axis_size("row") * lax.axis_size("col")
    (grad_weight,) = call(
        functools.partial(final_kernel, 1.0 / math.sqrt(pixels)),
        "final",
        [shape((3, 3, CH, CH), F32)],
        [],
        terms,
        arriving,
        cycles=10,
    )
    return (grad_source, grad_target, grad_weight)


def solution(mesh):
    placed = (
        P(None, ("sec", "row"), "col"),
        P(None, ("sec", "row"), "col"),
        P(),
        P(None, ("sec", "row"), "col"),
    )
    return jax.shard_map(
        per_device,
        mesh=mesh,
        in_specs=placed,
        out_specs=(
            P(None, ("sec", "row"), "col"),
            P(None, ("sec", "row"), "col"),
            P("sec", None, None, None),
        ),
        check_vma=False,
    )
```

```python
import functools
import math

import jax
import jax.numpy as jnp
from jax import lax
from jax.experimental import pallas as pl
from jax.experimental.pallas import tpu as pltpu
from jax.sharding import PartitionSpec as P

RADIUS = 4
SHARPNESS = 4.0
CH = 32
QUAD = 4
LANES = QUAD * CH
GROUP = 32
HALO = 2 * RADIUS
F32 = jnp.float32
BF16 = jnp.bfloat16


def lane_group(shape):
    return lax.broadcasted_iota(jnp.int32, shape, len(shape) - 1) // CH


def by_group(values):
    lane = lax.broadcasted_iota(jnp.int32, values[0].shape, values[0].ndim - 1)
    low = jnp.where(lane < CH, values[0], values[1])
    high = jnp.where(lane < 3 * CH, values[2], values[3])
    return jnp.where(lane < 2 * CH, low, high)


def roll_groups(value, steps):
    steps = steps % QUAD
    if steps == 0:
        return value
    return pltpu.roll(value, steps * CH, value.ndim - 1)


def group_sum(value, ones):
    high = value.astype(BF16)
    low = (value - high.astype(F32)).astype(BF16)
    both = jnp.concatenate([high, low], axis=1)
    return jnp.dot(both, ones, preferred_element_type=F32)


def group_ones():
    row = lax.broadcasted_iota(jnp.int32, (2 * LANES, LANES), 0) % LANES
    col = lax.broadcasted_iota(jnp.int32, (2 * LANES, LANES), 1)
    return jnp.where(row // CH == col // CH, 1.0, 0.0).astype(BF16)


def even(axis):
    return lax.rem(lax.axis_index(axis), 2) == 0


def pack_kernel(
    src_hbm, tgt_hbm, flow_hbm, own_ref, fl_ref, sa_ref, sb_ref,
    wide_ref, src_ref, tgt_ref, flow_ref, sem_ref,
):
    channels, rows, cols = src_ref.shape
    quads = rows // QUAD
    copies = [
        pltpu.make_async_copy(src, dst, sem_ref.at[index])
        for index, (src, dst) in enumerate(
            ((tgt_hbm, tgt_ref), (src_hbm, src_ref), (flow_hbm, flow_ref))
        )
    ]
    for copy in copies:
        copy.start()
    for base, ref in ((0, tgt_ref), (quads, src_ref)):
        copies[base // quads].wait()
        wide_ref[...] = ref[...].astype(F32).reshape(channels * rows, cols)
        for q in range(quads):
            part = jnp.concatenate(
                [wide_ref[pl.ds(q * QUAD + i, channels, stride=rows), :] for i in range(QUAD)],
                axis=0,
            )
            own_ref[base + q] = part.T.astype(BF16)
    copies[2].wait()
    pieces = []
    for f in range(2):
        value = flow_ref[f]
        high = value.astype(BF16).astype(F32)
        pieces += [high, value - high]
    fl_ref[...] = jnp.concatenate(pieces, axis=0).astype(BF16)
    is_even = even("row")
    last = quads - HALO // QUAD
    for dst, first in (
        (sa_ref, jnp.where(is_even, last, 0)),
        (sb_ref, jnp.where(is_even, 0, last)),
    ):
        for k in range(HALO // QUAD):
            dst[k * cols : (k + 1) * cols] = own_ref[first + k]
            dst[(2 + k) * cols : (3 + k) * cols] = own_ref[quads + first + k]
    top = jnp.concatenate([p[:HALO] for p in pieces], axis=0)
    low = jnp.concatenate([p[rows - HALO :] for p in pieces], axis=0)
    sa_ref[4 * cols :] = jnp.where(is_even, low, top).astype(BF16)
    sb_ref[4 * cols :] = jnp.where(is_even, top, low).astype(BF16)


def low_high(axis, near, far):
    index, size = lax.axis_index(axis), lax.axis_size(axis)
    near, far = near.astype(F32), far.astype(F32)
    flag = even(axis)
    outermost = jnp.logical_or(index == 0, index == size - 1)
    far = jnp.where(outermost, 0.0, far)
    return jnp.where(flag, far, near), jnp.where(flag, near, far)


def strip_kernel(own_ref, fl_ref, ra_ref, rb_ref, sc_ref, sd_ref, wide_ref):
    planes, cols, _ = own_ref.shape
    quads = planes // 2
    rows = quads * QUAD
    c_even = even("col")
    for kind in range(2):
        for q in range(quads + 4):
            left = halo_plane(kind, q, own_ref, ra_ref, rb_ref, slice(0, KEYS))[:HALO]
            right = halo_plane(kind, q, own_ref, ra_ref, rb_ref, slice(cols - KEYS, cols))[HALO:]
            row = (kind * (quads + 4) + q) * HALO
            wide_ref[0, row : row + HALO] = jnp.where(c_even, right, left)
            wide_ref[1, row : row + HALO] = jnp.where(c_even, left, right)
    count = 2 * (quads + 4) * HALO
    sc_ref[:count] = wide_ref[0].astype(BF16)
    sd_ref[:count] = wide_ref[1].astype(BF16)
    up, down = flow_up_down(ra_ref, rb_ref)
    flow = []
    own = fl_ref[...].astype(F32)
    for v in range(4):
        flow += [
            up[v * HALO : (v + 1) * HALO],
            own[v * rows : (v + 1) * rows],
            down[v * HALO : (v + 1) * HALO],
        ]
    flow = jnp.concatenate(flow, axis=0).astype(BF16)
    sc_ref[count:] = flow
    sd_ref[count:] = flow


def fill_taps(dst_ref, w_ref):
    zero = jnp.zeros((CH, CH), F32)
    for dx in range(3):
        for block in range(2 * QUAD):
            row = block if block < QUAD else {QUAD: QUAD, 2 * QUAD - 1: -1}.get(block)
            parts = []
            for out in range(QUAD):
                tap = None if row is None else row - out + 1
                ok = tap is not None and 0 <= tap < 3
                parts.append(w_ref[tap, dx].astype(F32) if ok else zero)
            dst_ref[dx, block * CH : (block + 1) * CH, :] = jnp.concatenate(parts, axis=1).astype(
                BF16
            )


def taps_of(ref, quad, start, count):
    main = ref[quad, pl.ds(start, count), :]
    after = ref[quad + 1, pl.ds(start, count), :]
    before = ref[quad - 1, pl.ds(start, count), :]
    lane = lax.broadcasted_iota(jnp.int32, main.shape, 1)
    beside = jnp.where(lane < 2 * CH, after, before)
    return jnp.concatenate([main, beside], axis=1).astype(BF16)


def conv(ref, quad, start, count, w_ref):
    total = jnp.zeros((count, LANES), F32)
    for dx in range(3):
        total += jnp.dot(
            taps_of(ref, quad, start + dx - 1, count), w_ref[dx], preferred_element_type=F32
        )
    return total


SPAN = 3 * QUAD
KEYS = 16


def halo_plane(kind, q, own_ref, ra_ref, rb_ref, part=None):
    planes, cols, _ = own_ref.shape
    quads = planes // 2
    part = part or slice(0, cols)
    if 2 <= q < quads + 2:
        return own_ref[kind * quads + q - 2, part].astype(F32)
    down = q >= quads + 2
    at = (2 * kind + (q - quads - 2 if down else q)) * cols
    part = slice(at + part.start, at + part.stop)
    return low_high("row", ra_ref[part], rb_ref[part])[down]


def edge_plane(kind, q, side, own_ref, ra_ref, rb_ref, rc_ref, rd_ref):
    planes, cols, _ = own_ref.shape
    quads = planes // 2
    tile = slice(0, KEYS) if side == 0 else slice(cols - KEYS, cols)
    mine = halo_plane(kind, q, own_ref, ra_ref, rb_ref, tile)
    index = kind * (quads + 4) + q
    at = index // 2 * 2 * HALO
    fetched = low_high("col", rc_ref[at : at + 2 * HALO], rd_ref[at : at + 2 * HALO])[side]
    fetched = fetched[index % 2 * HALO : index % 2 * HALO + HALO]
    parts = [fetched, mine[:HALO]] if side == 0 else [mine[HALO:], fetched]
    return jnp.concatenate(parts, axis=0)


def flow_up_down(ra_ref, rb_ref):
    at = ra_ref.shape[0] - 4 * HALO
    return low_high("row", ra_ref[at:], rb_ref[at:])


def flow_part(f, ref_or_value, rows):
    parts = [ref_or_value[v * rows : (v + 1) * rows].astype(F32) for v in (2 * f, 2 * f + 1)]
    return parts[0] + parts[1]


def flow_mid(f, fl_ref, ra_ref, rb_ref):
    up, down = flow_up_down(ra_ref, rb_ref)
    return jnp.concatenate(
        [
            flow_part(f, up, HALO),
            flow_part(f, fl_ref, fl_ref.shape[0] // 4),
            flow_part(f, down, HALO),
        ],
        axis=0,
    )


def flow_inner(p_ref, values):
    groups = p_ref.shape[1]
    for f in range(2):
        mid = pltpu.roll(values[f], LANES - RADIUS, 1)
        lane = lax.broadcasted_iota(jnp.int32, mid.shape, 1)
        row = lax.broadcasted_iota(jnp.int32, mid.shape, 0)
        mid = jnp.where(lane < LANES - 8, mid, 0.0)
        turned = [roll_groups(mid, k) for k in range(QUAD)]
        for g in range(groups):
            total = jnp.zeros(mid.shape, F32)
            for i in range(QUAD):
                keep = jnp.logical_and(row % QUAD == i, lane // CH == i)
                total = jnp.where(keep, turned[(i - g) % QUAD], total)
            p_ref[f, g] = total


def flow_edge(e_ref, fl_ref, ra_ref, rb_ref, rc_ref, rd_ref):
    rows = fl_ref.shape[0] // 4
    ext = rows + 2 * HALO
    base = rc_ref.shape[0] - 4 * ext
    left, right = low_high("col", rc_ref[base:], rd_ref[base:])
    for f in range(2):
        mid = flow_mid(f, fl_ref, ra_ref, rb_ref)
        at = 2 * f * ext
        lf = left[at : at + ext] + left[at + ext : at + 2 * ext]
        rt = right[at : at + ext] + right[at + ext : at + 2 * ext]
        lane = lax.broadcasted_iota(jnp.int32, mid.shape, 1)
        row = lax.broadcasted_iota(jnp.int32, mid.shape, 0)
        low = jnp.where(lane < RADIUS, pltpu.roll(lf, RADIUS, 1), pltpu.roll(mid, RADIUS, 1))
        high = jnp.where(
            lane < 3 * RADIUS, pltpu.roll(mid, 3 * RADIUS, 1), pltpu.roll(rt, 3 * RADIUS, 1)
        )
        both = jnp.where(lane < 8, low, high)
        for h in range(2):
            total = jnp.zeros(mid.shape, F32)
            for i in range(QUAD):
                turn = i * CH + h * 16
                keep = jnp.logical_and(row % QUAD == i, lane // 16 == 2 * i + h)
                total = jnp.where(keep, pltpu.roll(both, turn, 1) if turn else both, total)
            e_ref[f, h] = total


def fill_mask(m_ref):
    key = lax.broadcasted_iota(jnp.int32, (SPAN, KEYS, LANES), 0)
    kx = lax.broadcasted_iota(jnp.int32, (SPAN, KEYS, LANES), 1)
    lane = lax.broadcasted_iota(jnp.int32, (SPAN, KEYS, LANES), 2)
    dy = key - lane // CH
    dx = kx - lane % 8
    ok = (dy >= 0) & (dy <= 2 * RADIUS) & (dx >= 0) & (dx <= 2 * RADIUS)
    m_ref[...] = jnp.where(ok, 1.0, 0.0)


def softmax_block(score_ref, m_ref, f0, f1, scale):
    lane = lax.broadcasted_iota(jnp.int32, (KEYS, LANES), 1)
    at_y = (lane // CH + RADIUS).astype(F32)
    at_x = (lane % 8 + RADIUS).astype(F32)
    key_x = lax.broadcasted_iota(jnp.int32, (KEYS, LANES), 0).astype(F32)
    f0 = jnp.broadcast_to(f0, (KEYS, LANES))
    f1 = jnp.broadcast_to(f1, (KEYS, LANES))
    side = f1 * (key_x - at_x) - f0 * at_y
    weights = []
    total = jnp.zeros((KEYS, LANES), F32)
    lean = jnp.zeros((KEYS, LANES), F32)
    for y in range(SPAN):
        weight = score_ref[KEYS * y : KEYS * (y + 1)] * (scale * math.log2(math.e))
        weight = jnp.exp2(weight) * m_ref[y]
        weights.append(weight)
        total = total + weight
        lean = lean + weight * (f0 * float(y) + side)
    total = jnp.sum(total, axis=0, keepdims=True)
    lean = jnp.sum(lean, axis=0, keepdims=True)
    base = jnp.broadcast_to(lean / total, (KEYS, LANES))
    factor = jnp.broadcast_to(scale / total, (KEYS, LANES))
    step = f0 * factor
    side = (side - base) * factor
    return jnp.concatenate(
        [(weights[y] * (step * float(y) + side)).astype(BF16) for y in range(SPAN)], axis=0
    )


def unit_of(field, ones):
    recip = lax.rsqrt(group_sum(field * field, ones) * (1.0 / CH) + 1.0)
    return recip, (field * recip).astype(BF16).astype(F32)


def unit_grad(field, recip, grad, ones):
    inner = group_sum(grad * field, ones)
    return recip * grad - field * (recip * recip * recip) * inner * (1.0 / CH)


def key_rows(t4_ref, first, unit):
    turned = [roll_groups(unit, k) for k in range(QUAD)]
    for i in range(QUAD):
        for g in range(t4_ref.shape[0]):
            t4_ref[g, first + i] = by_group(
                [
                    turned[(j - i) % QUAD][g * GROUP + 8 * j : g * GROUP + 8 * j + KEYS]
                    for j in range(QUAD)
                ]
            ).astype(BF16)


def query_block(octs):
    group = lane_group((8, LANES))
    turned = [
        roll_groups(by_group([octs[(i + k) % QUAD] for i in range(QUAD)]), k)
        for k in range(QUAD)
    ]
    parts = [
        jnp.where(group == j, turned[(j - i) % QUAD], 0.0)
        for i in range(QUAD)
        for j in range(QUAD)
    ]
    return jnp.concatenate(parts, axis=0).astype(BF16)


def packed_rows(mine):
    def piece(i, j):
        at = i * GROUP + 8 * j
        return mine[at : at + 8]

    turned = [
        roll_groups(by_group([piece((j + k) % QUAD, j) for j in range(QUAD)]), k)
        for k in range(QUAD)
    ]
    return [by_group([turned[(i - j) % QUAD] for i in range(QUAD)]) for j in range(QUAD)]


def run_blocks(blocks, m_ref, sc_ref, d_ref, scale):
    def score(b):
        sc_ref[b % 2] = lax.dot_general(
            blocks[b][0](), blocks[b][1](), (((1,), (1,)), ((), ())), preferred_element_type=F32
        )

    def collect(b):
        dscore = d_ref[b % 2]
        keys, queries, _, wanted, put_keys, put_rows = blocks[b]
        put_keys(jnp.dot(dscore[wanted], queries(), preferred_element_type=F32))
        mine = lax.dot_general(
            dscore, keys(), (((0,), (0,)), ((), ())), preferred_element_type=F32
        )
        put_rows(packed_rows(mine))

    score(0)
    for b in range(len(blocks)):
        if b + 1 < len(blocks):
            score(b + 1)
        f0, f1 = blocks[b][2]()
        d_ref[b % 2] = softmax_block(sc_ref.at[b % 2], m_ref, f0, f1, scale)
        if b > 0:
            collect(b - 1)
    collect(len(blocks) - 1)


def conv_from(tap_list, w_ref):
    total = None
    for dx in range(3):
        term = jnp.dot(tap_list[dx], w_ref[dx], preferred_element_type=F32)
        total = term if total is None else total + term
    return total


def inner_block(n, g, keys, q_ref, p_ref, p_quad, ga_ref, gu_ref):
    rows = slice(p_quad * QUAD, (p_quad + 1) * QUAD)
    own = ga_ref.shape[1]
    first = n * QUAD - HALO
    low, high = max(first, 0), min(first + SPAN, own)
    wanted = slice((low - first) * KEYS, (high - first) * KEYS)

    def put_keys(value):
        ga_ref[g, low:high] = ga_ref[g, low:high] + value.reshape(high - low, KEYS, LANES)

    def put_rows(octs):
        for j in range(QUAD):
            gu_ref[n, g * GROUP + 8 * j : g * GROUP + 8 * j + 8] = octs[j]

    return (
        lambda: keys(n, g),
        lambda: q_ref[n, g],
        lambda: [jnp.sum(p_ref[f, g, rows, :], axis=0, keepdims=True) for f in range(2)],
        wanted,
        put_keys,
        put_rows,
    )


def inner_queries(n, es_ref, taps_ref, fe_ref, rf_ref, q_ref, ones, keep=None):
    cols = fe_ref.shape[1]
    tap_list = [taps_of(es_ref, n + 1, RADIUS + dx - 1, cols) for dx in range(3)]
    if keep is not None:
        for dx in range(3):
            keep[n, dx] = tap_list[dx]
    feat = conv_from(tap_list, taps_ref).astype(BF16).astype(F32)
    fe_ref[n] = feat
    recip, unit = unit_of(feat, ones)
    rf_ref[n] = recip
    for g in range(cols // GROUP):
        q_ref[n, g] = query_block(
            [unit[g * GROUP + 8 * j : g * GROUP + 8 * j + 8] for j in range(QUAD)]
        )


def fill_plane(dst_ref, q, value):
    cols = value.shape[0]
    dst_ref[q, :cols] = value
    dst_ref[q, cols:] = jnp.zeros((dst_ref.shape[1] - cols, LANES), F32)


def own_rows(
    quads_of, keys, es_ref, taps_ref, m_ref, p_ref, ga_ref, gf_out, gw_out,
    q_ref, fe_ref, rf_ref, gu_ref, tap_ref, sc_ref, d_ref, ones,
):
    cols = fe_ref.shape[1]
    for n in quads_of:
        inner_queries(n, es_ref, taps_ref, fe_ref, rf_ref, q_ref, ones, tap_ref)
    run_blocks(
        [
            inner_block(n, g, keys, q_ref, p_ref, n - 1, ga_ref, gu_ref)
            for n in quads_of
            for g in range(cols // GROUP)
        ],
        m_ref, sc_ref, d_ref, SHARPNESS / math.sqrt(CH),
    )
    row = lax.broadcasted_iota(jnp.int32, (cols, LANES), 0)
    values = []
    for index, n in enumerate(quads_of):
        value = unit_grad(fe_ref[n], rf_ref[n], gu_ref[n], ones)
        value = jnp.where(row < cols - 8, value, 0.0).astype(BF16)
        gf_out[index] = value
        values.append(value)
    value = jnp.concatenate(values, axis=0)
    for dx in range(3):
        others = jnp.concatenate([tap_ref[n, dx] for n in quads_of], axis=0)
        gw_out[dx] = gw_out[dx] + lax.dot_general(
            value, others, (((0,), (0,)), ((), ())), preferred_element_type=F32
        )


def early_kernel(
    own_ref, fl_ref, w_ref, wt_ref,
    t4_out, taps_out, back_out, m_out, p_out, ga_out, gf_out, gw_out,
    es_ref, q_ref, fe_ref, rf_ref, gu_ref, tap_ref, sc_ref, d_ref,
):
    planes, cols, _ = own_ref.shape
    quads = planes // 2
    width = es_ref.shape[1]
    ones = group_ones()
    fill_taps(taps_out, w_ref)
    fill_taps(back_out, wt_ref)
    fill_mask(m_out)
    flow_inner(p_out, [flow_part(f, fl_ref, quads * QUAD) for f in range(2)])
    for q in range(quads):
        fill_plane(es_ref, q + 2, own_ref[quads + q].astype(F32))
        _, unit = unit_of(own_ref[q].astype(F32), ones)
        pad = jnp.zeros((width - cols, LANES), F32)
        key_rows(t4_out, q * QUAD, jnp.concatenate([unit, pad], axis=0))
    ga_out[...] = jnp.zeros_like(ga_out)
    gw_out[...] = jnp.zeros_like(gw_out)

    def keys(n, g):
        at = (n - 2) * QUAD
        return t4_out[g, at : at + SPAN].reshape(SPAN * KEYS, LANES)

    own_rows(
        range(2, quads), keys, es_ref, taps_out, m_out, p_out, ga_out, gf_out, gw_out,
        q_ref, fe_ref, rf_ref, gu_ref, tap_ref, sc_ref, d_ref, ones,
    )


def middle_kernel(
    own_ref, ra_ref, rb_ref, t4_ref, taps_ref, m_ref, p_ref, ga_in, gw_in,
    t4_out, ga_out, gf_out, gw_out,
    es_ref, q_ref, fe_ref, rf_ref, gu_ref, tap_ref, sc_ref, d_ref,
):
    planes, cols, _ = own_ref.shape
    quads = planes // 2
    width = es_ref.shape[1]
    ones = group_ones()
    for q in (1, 2, 3, quads, quads + 1, quads + 2):
        fill_plane(es_ref, q, halo_plane(1, q, own_ref, ra_ref, rb_ref))
    pad = jnp.zeros((width - cols, LANES), F32)
    for k, q in enumerate((1, quads + 2)):
        _, unit = unit_of(halo_plane(0, q, own_ref, ra_ref, rb_ref), ones)
        key_rows(t4_out, k * QUAD, jnp.concatenate([unit, pad], axis=0))

    def keys(n, g):
        if n == 1:
            parts = [t4_out[g, :QUAD], t4_ref[g, : 2 * QUAD]]
        else:
            parts = [t4_ref[g, (quads - 2) * QUAD :], t4_out[g, QUAD:]]
        return jnp.concatenate(parts, axis=0).reshape(SPAN * KEYS, LANES)

    own_rows(
        (1, quads), keys, es_ref, taps_ref, m_ref, p_ref, ga_out, gf_out, gw_out,
        q_ref, fe_ref, rf_ref, gu_ref, tap_ref, sc_ref, d_ref, ones,
    )


def edge_blocks(
    pairs, first, ee_ref, tu_ref, taps_ref, t4_ref, q_ref, ep_ref, ga_ref, ones, keep=None
):
    blocks, stores = [], []
    for e, pair in enumerate(pairs):
        quad_of = [pair[j // 2] for j in range(QUAD)]
        tap_list = [
            jnp.concatenate(
                [
                    taps_of(ee_ref.at[j % 2], quad_of[j] + 1, RADIUS + dx - 1, 8).astype(F32)
                    for j in range(QUAD)
                ],
                axis=0,
            ).astype(BF16)
            for dx in range(3)
        ]
        feat = conv_from(tap_list, taps_ref).astype(BF16).astype(F32)
        recip, unit = unit_of(feat, ones)
        q_ref[e] = query_block([unit[8 * j : 8 * j + 8] for j in range(QUAD)])
        for y in range(SPAN):
            t4_ref[e, y] = by_group(
                [
                    tu_ref[(j - y) % QUAD, j % 2, quad_of[j] + y // QUAD]
                    for j in range(QUAD)
                ]
            ).astype(BF16)
        result = []
        stores.append((tap_list, feat, recip, result))

        def flows(pair=pair):
            total = []
            for f in range(2):
                parts = [
                    jnp.sum(
                        ep_ref[f, h, (pair[h] + 1) * QUAD : (pair[h] + 2) * QUAD, :],
                        axis=0,
                        keepdims=True,
                    )
                    for h in range(2)
                ]
                total.append(parts[0] + parts[1])
            return total

        def put_keys(value, e=e):
            ga_ref[first + e] = value.reshape(SPAN, KEYS, LANES)

        blocks.append(
            (
                lambda e=e: t4_ref[e].reshape(SPAN * KEYS, LANES),
                lambda e=e: q_ref[e],
                flows,
                slice(0, SPAN * KEYS),
                put_keys,
                result.extend,
            )
        )
    return blocks, stores


def edge_planes(ee_ref, tu_ref, ones, quads_of, keys_of, refs):
    for side in range(2):
        for q in quads_of:
            ee_ref[side, q] = edge_plane(1, q, side, *refs)
        raw = jnp.concatenate([edge_plane(0, q, side, *refs) for q in keys_of], axis=0)
        _, unit = unit_of(raw, ones)
        for k in range(QUAD):
            turned = roll_groups(unit, k)
            for index, q in enumerate(keys_of):
                tu_ref[k, side, q] = turned[index * KEYS : (index + 1) * KEYS]


def edge_grads(stores, ones):
    return [
        unit_grad(feat, recip, jnp.concatenate(result, axis=0), ones).astype(BF16)
        for _, feat, recip, result in stores
    ]


def pairs_of(quads):
    return [(n, n + 1) for n in range(1, quads + 1, 2)]


def edge_kernel(
    own_ref, fl_ref, ra_ref, rb_ref, rc_ref, rd_ref, taps_ref, m_ref, gw_ref,
    ga_ref, gf_out, gw_out,
    ee_ref, tu_ref, t4_ref, q_ref, ep_ref, sc_ref, d_ref,
):
    planes, cols, _ = own_ref.shape
    quads = planes // 2
    ext = quads + 4
    scale = SHARPNESS / math.sqrt(CH)
    ones = group_ones()
    refs = (own_ref, ra_ref, rb_ref, rc_ref, rd_ref)
    edge_planes(ee_ref, tu_ref, ones, range(1, ext - 1), range(1, ext - 1), refs)
    flow_edge(ep_ref, fl_ref, ra_ref, rb_ref, rc_ref, rd_ref)
    blocks, stores = edge_blocks(
        pairs_of(quads), 0, ee_ref, tu_ref, taps_ref, t4_ref, q_ref, ep_ref, ga_ref, ones
    )
    run_blocks(blocks, m_ref, sc_ref, d_ref, scale)
    totals = [gw_ref[dx] for dx in range(3)]
    row = lax.broadcasted_iota(jnp.int32, (GROUP, LANES), 0)
    inside = jnp.logical_xor(row // 8 % 2 == 0, row % 8 < RADIUS)
    for e, grad in enumerate(edge_grads(stores, ones)):
        gf_out[e] = grad
        grad = jnp.where(inside, grad.astype(F32), 0.0).astype(BF16)
        for dx in range(3):
            totals[dx] = totals[dx] + lax.dot_general(
                grad, stores[e][0][dx], (((0,), (0,)), ((), ())), preferred_element_type=F32
            )
    lane = lax.broadcasted_iota(jnp.int32, (CH, LANES), 1)
    for dx, total in enumerate(totals):
        rows_of = [total[i * CH : (i + 1) * CH] for i in range(QUAD)]
        main = [x[:, :LANES] for x in rows_of]
        beside = [x[:, LANES:] for x in rows_of]
        start = jnp.where(lane < CH, roll_groups(beside[0], 1), roll_groups(main[0], 1))
        last = jnp.where(lane < 2 * CH, roll_groups(main[3], 2), roll_groups(beside[3], 2))
        gw_out[dx * CH : (dx + 1) * CH] = (start + main[1]) + (roll_groups(main[2], 3) + last)


def spread(dst_ref, quad, value, channels, rows):
    flipped = value.T
    for i in range(QUAD):
        dst_ref[pl.ds(quad * QUAD + i, channels, stride=rows), :] = flipped[
            i * CH : (i + 1) * CH
        ]


def outer_kernel(
    lower, own_ref, ra_ref, rb_ref, taps_ref, m_ref, t4_own, t4_halo, ga_in,
    ga_out, gf_out,
    es_ref, t4_ref, q_ref, fe_ref, rf_ref, gu_ref, p_ref, sc_ref, d_ref,
):
    planes, cols, _ = own_ref.shape
    quads = planes // 2
    width = es_ref.shape[1]
    ones = group_ones()
    n = quads + 1 if lower else 0
    for q in (n, n + 1, n + 2):
        fill_plane(es_ref, q, halo_plane(1, q, own_ref, ra_ref, rb_ref))
    flow_inner(
        p_ref, [flow_part(f, flow_up_down(ra_ref, rb_ref)[lower], HALO) for f in range(2)]
    )
    _, unit = unit_of(halo_plane(0, quads + 3 if lower else 0, own_ref, ra_ref, rb_ref), ones)
    pad = jnp.zeros((width - cols, LANES), F32)
    key_rows(t4_ref, 0, jnp.concatenate([unit, pad], axis=0))

    def keys(n, g):
        if lower:
            parts = [t4_own[g, (quads - 1) * QUAD :], t4_halo[g, QUAD:], t4_ref[g]]
        else:
            parts = [t4_ref[g], t4_halo[g, :QUAD], t4_own[g, :QUAD]]
        return jnp.concatenate(parts, axis=0).reshape(SPAN * KEYS, LANES)

    inner_queries(n, es_ref, taps_ref, fe_ref, rf_ref, q_ref, ones)
    run_blocks(
        [
            inner_block(n, g, keys, q_ref, p_ref, 0 if lower else 1, ga_out, gu_ref)
            for g in range(cols // GROUP)
        ],
        m_ref, sc_ref, d_ref, SHARPNESS / math.sqrt(CH),
    )
    gf_out[...] = unit_grad(fe_ref[n], rf_ref[n], gu_ref[n], ones).astype(BF16)


def corner_kernel(
    own_ref, fl_ref, ra_ref, rb_ref, rc_ref, rd_ref, taps_ref, m_ref,
    ge_out, gf_out,
    ee_ref, tu_ref, t4_ref, q_ref, ep_ref, sc_ref, d_ref,
):
    quads = own_ref.shape[0] // 2
    ext = quads + 4
    ones = group_ones()
    refs = (own_ref, ra_ref, rb_ref, rc_ref, rd_ref)
    near = (0, 1, 2, ext - 3, ext - 2, ext - 1)
    edge_planes(ee_ref, tu_ref, ones, near, near, refs)
    flow_edge(ep_ref, fl_ref, ra_ref, rb_ref, rc_ref, rd_ref)
    blocks, stores = edge_blocks(
        [(0, quads + 1)], 0, ee_ref, tu_ref, taps_ref, t4_ref, q_ref, ep_ref, ge_out, ones
    )
    run_blocks(blocks, m_ref, sc_ref, d_ref, SHARPNESS / math.sqrt(CH))
    gf_out[...] = edge_grads(stores, ones)[0]


def image_kernel(
    own_ref, back_ref, ga_ref, gem_ref, gec_ref,
    gf_early, gf_middle, gf_top, gf_low, gfe_ref, gfc_ref,
    gs_out, gt_out,
    full_ref, wide_ref,
):
    channels, rows, cols = gs_out.shape
    quads = rows // QUAD
    ones = group_ones()
    rows_of = {0: gf_top[...], quads + 1: gf_low[...], 1: gf_middle[0], quads: gf_middle[1]}
    for n in range(2, quads):
        rows_of[n] = gf_early[n - 2]
    for n, value in rows_of.items():
        full_ref[n, 8 : 8 + cols] = value.astype(F32)
    edges = [gfe_ref[e] for e in range(quads // 2)] + [gfc_ref[...]]
    where_is = {}
    for e, (pair, grad) in enumerate(zip(pairs_of(quads) + [(0, quads + 1)], edges)):
        grad = grad.astype(F32)
        for j in range(QUAD):
            at = 0 if j % 2 == 0 else cols
            full_ref[pair[j // 2], at : at + 8] = grad[8 * j : 8 * j + 8]
            where_is[pair[j // 2], j % 2] = (e, j)

    for q in range(quads):
        tap_list = [taps_of(full_ref, q + 1, RADIUS + dx - 1, cols) for dx in range(3)]
        spread(wide_ref, q, conv_from(tap_list, back_ref), channels, rows)
    gs_out[...] = wide_ref[...].astype(BF16).reshape(channels, rows, cols)

    group = lane_group((8, LANES))
    last = cols // 8
    for q in range(quads):
        parts = []
        for oct in range(1, last + 1):
            total = None
            for k in range(QUAD):
                both = jnp.zeros((8, LANES), F32)
                for half, which in ((0, oct), (1, oct - 1)):
                    if not 0 < which < last:
                        continue
                    g, j = divmod(which - 1, QUAD)
                    at = q * QUAD + (j + k) % QUAD
                    both = jnp.where(group == j, ga_ref[g, at, 8 * half : 8 * half + 8], both)
                both = roll_groups(both, k)
                total = both if total is None else total + both
            side = 0 if oct == 1 else 1 if oct == last else None
            if side is not None:
                half = 1 - side
                for n in range(q, q + 3):
                    e, j = where_is[n, side]
                    ref = gem_ref.at[e] if e < quads // 2 else gec_ref.at[0]
                    for i in range(QUAD):
                        part = ref[(q + 2 - n) * QUAD + i, 8 * half : 8 * half + 8]
                        total = total + roll_groups(jnp.where(group == j, part, 0.0), i - j)
            parts.append(total)
        grad = jnp.concatenate(parts, axis=0)
        field = own_ref[q].astype(F32)
        recip = lax.rsqrt(group_sum(field * field, ones) * (1.0 / CH) + 1.0)
        spread(wide_ref, q, unit_grad(field, recip, grad, ones), channels, rows)
    gt_out[...] = wide_ref[...].astype(BF16).reshape(channels, rows, cols)


def final_kernel(scale, one_ref, two_ref, out_ref):
    for dx in range(3):
        at = slice(dx * CH, (dx + 1) * CH)
        total = ((one_ref[at] + two_ref[at]) * scale).T
        for tap in range(3):
            out_ref[tap, dx] = total[tap * CH : (tap + 1) * CH]


def pair_exchange(x, y, axis):
    rows, cols = lax.axis_size("row"), lax.axis_size("col")
    near, far = [], []
    for r in range(rows):
        for c in range(cols):
            index, size = (r, rows) if axis == "row" else (c, cols)
            other = index + 1 if index % 2 else index - 1
            for pairs, to in ((near, index ^ 1), (far, other)):
                if 0 <= to < size:
                    target = (to, c) if axis == "row" else (r, to)
                else:
                    target = (r, c ^ 1) if axis == "row" else (r ^ 1, c)
                pairs.append((r * cols + c, target[0] * cols + target[1]))
    both = ("row", "col")
    return lax.ppermute(x, both, near), lax.ppermute(y, both, far)


def swap(x, axis, step):
    return lax.ppermute(x, axis, [(i, i ^ step) for i in range(lax.axis_size(axis))])


def after(value, *others):
    return lax.optimization_barrier((value, *others))[0]


def vmem(count):
    return [pl.BlockSpec(memory_space=pltpu.VMEM)] * count


def per_device(source, target, conv_weight, flow_cotangent):
    channels, rows, cols = source.shape
    quads = rows // QUAD
    ext = quads + 4
    groups = cols // GROUP
    width = cols + HALO
    asked = quads + 2
    flipped = jnp.transpose(conv_weight[::-1, ::-1], (0, 1, 3, 2))
    shape = jax.ShapeDtypeStruct

    def scratch(*dims, dtype=F32):
        return pltpu.VMEM(dims, dtype)

    def call(kernel, name, outs, scratches, *args, cycles=1000, alias=None, specs=None):
        return pl.pallas_call(
            kernel,
            out_shape=tuple(outs),
            in_specs=specs or vmem(len(args)),
            out_specs=tuple(vmem(len(outs))),
            scratch_shapes=scratches,
            input_output_aliases=alias or {},
            cost_estimate=pl.CostEstimate(
                flops=cycles * 250_000, bytes_accessed=cycles * 1000, transcendentals=0
            ),
            compiler_params=pltpu.CompilerParams(vmem_limit_bytes=16 << 20),
            name=name,
        )(*args)

    side = shape((4 * cols + 4 * HALO, LANES), BF16)
    own, flow, to_a, to_b = call(
        pack_kernel,
        "pack",
        [shape((2 * quads, cols, LANES), BF16), shape((4 * rows, cols), BF16), side, side],
        [
            scratch(channels * rows, cols),
            scratch(*source.shape, dtype=BF16),
            scratch(*target.shape, dtype=BF16),
            scratch(*flow_cotangent.shape),
            pltpu.SemaphoreType.DMA((3,)),
        ],
        *(
            pltpu.with_memory_space_constraint(x, pltpu.HBM)
            for x in (source, target, flow_cotangent)
        ),
        specs=[pl.BlockSpec(memory_space=pltpu.HBM)] * 3,
    )
    ra, rb = pair_exchange(to_a, to_b, "row")
    taps = shape((3, 2 * LANES, LANES), BF16)
    stages = [scratch(2, SPAN * KEYS, LANES), scratch(2, SPAN * KEYS, LANES, dtype=BF16)]
    inner = [
        scratch(asked, groups, LANES, LANES, dtype=BF16),
        scratch(asked, cols, LANES),
        scratch(asked, cols, LANES),
        scratch(asked, cols, LANES),
    ]
    planes = scratch(ext, width, LANES)
    tap_lists = scratch(asked, 3, cols, 2 * LANES, dtype=BF16)
    for_keys = shape((groups, rows, KEYS, LANES), F32)
    for_kernel = shape((3, LANES, 2 * LANES), F32)
    for_feat = shape((2, cols, LANES), BF16)
    keys, forward, back, mask, cotangents, grad_keys, feat_early, terms = call(
        early_kernel,
        "early",
        [
            shape((groups, rows, KEYS, LANES), BF16),
            taps,
            taps,
            shape((SPAN, KEYS, LANES), F32),
            shape((2, groups, rows, LANES), F32),
            for_keys,
            shape((quads - 2, cols, LANES), BF16),
            for_kernel,
        ],
        [planes] + inner + [tap_lists] + stages,
        own,
        flow,
        conv_weight,
        flipped,
        cycles=3000,
    )
    strip = shape((2 * ext * HALO + 4 * ext * QUAD, LANES), BF16)
    to_c, to_d = call(
        strip_kernel,
        "strip",
        [strip, strip],
        [scratch(2, 2 * ext * HALO, LANES)],
        own,
        flow,
        ra,
        rb,
    )
    rc, rd = pair_exchange(to_c, to_d, "col")
    halo_keys, grad_keys, feat_middle, terms = call(
        middle_kernel,
        "middle",
        [shape((groups, 2 * QUAD, KEYS, LANES), BF16), for_keys, for_feat, for_kernel],
        [planes] + inner + [tap_lists] + stages,
        own,
        ra,
        rb,
        keys,
        forward,
        mask,
        cotangents,
        grad_keys,
        terms,
        cycles=3000,
        alias={7: 1, 8: 3},
    )
    pairs = quads // 2
    outer = [scratch(2, ext, KEYS, LANES), scratch(QUAD, 2, ext, KEYS, LANES)]
    fetched = (own, flow, ra, rb, rc, rd, forward, mask)

    def edge_scratch(count):
        return outer + [
            scratch(count, SPAN, KEYS, LANES, dtype=BF16),
            scratch(count, LANES, LANES, dtype=BF16),
            scratch(2, 2, ext * QUAD, LANES),
        ] + stages

    edge_keys, edge_feat, terms = call(
        edge_kernel,
        "edge",
        [
            shape((pairs, SPAN, KEYS, LANES), F32),
            shape((pairs, GROUP, LANES), BF16),
            shape((3 * CH, LANES), F32),
        ],
        edge_scratch(pairs),
        *fetched,
        terms,
    )

    def outer_rows(lower, sums):
        return call(
            functools.partial(outer_kernel, lower),
            "lower" if lower else "upper",
            [for_keys, shape((cols, LANES), BF16)],
            [planes, scratch(groups, QUAD, KEYS, LANES, dtype=BF16)]
            + inner
            + [scratch(2, groups, HALO, LANES)]
            + stages,
            after(own, sums),
            ra,
            rb,
            forward,
            mask,
            keys,
            halo_keys,
            grad_keys,
            alias={7: 0},
            cycles=1500,
        )

    steps = []
    for axis in ("row", "col"):
        step = 1
        while step < lax.axis_size(axis):
            steps.append((axis, step))
            step *= 2
    for index, (axis, step) in enumerate(steps[:-1]):
        arriving = swap(terms, axis, step)
        ahead = len(steps) - 1 - index
        if ahead == 2:
            grad_keys, feat_top = outer_rows(0, terms)
            done = feat_top
        elif ahead == 1:
            grad_keys, feat_low = outer_rows(1, terms)
            corner_keys, corner_feat = call(
                corner_kernel,
                "corner",
                [shape((1, SPAN, KEYS, LANES), F32), shape((GROUP, LANES), BF16)],
                edge_scratch(1),
                after(own, terms),
                *fetched[1:],
            )
            done = (feat_low, corner_feat)
        else:
            done = None
        terms = terms + arriving
        if done is not None:
            terms = after(terms, done)
    arriving = swap(terms, *steps[-1])
    grad_source, grad_target = call(
        image_kernel,
        "image",
        [shape(source.shape, BF16), shape(target.shape, BF16)],
        [scratch(asked, 8 + cols, LANES), scratch(channels * rows, cols)],
        after(own, terms),
        back,
        grad_keys,
        edge_keys,
        corner_keys,
        feat_early,
        feat_middle,
        feat_top,
        feat_low,
        edge_feat,
        corner_feat,
        cycles=2000,
    )
    pixels = rows * cols * lax.axis_size("row") * lax.axis_size("col")
    (grad_weight,) = call(
        functools.partial(final_kernel, 1.0 / math.sqrt(pixels)),
        "final",
        [shape((3, 3, CH, CH), F32)],
        [],
        terms,
        arriving,
        cycles=10,
    )
    return (grad_source, grad_target, grad_weight)


def solution(mesh):
    placed = (
        P(None, ("sec", "row"), "col"),
        P(None, ("sec", "row"), "col"),
        P(),
        P(None, ("sec", "row"), "col"),
    )
    return jax.shard_map(
        per_device,
        mesh=mesh,
        in_specs=placed,
        out_specs=(
            P(None, ("sec", "row"), "col"),
            P(None, ("sec", "row"), "col"),
            P("sec", None, None, None),
        ),
        check_vma=False,
    )
```

```python
import functools
import math

import jax
import jax.numpy as jnp
from jax import lax
from jax.experimental import pallas as pl
from jax.experimental.pallas import tpu as pltpu
from jax.sharding import PartitionSpec as P

RADIUS = 4
SHARPNESS = 4.0
CH = 32
QUAD = 4
LANES = QUAD * CH
GROUP = 32
HALO = 2 * RADIUS
F32 = jnp.float32
BF16 = jnp.bfloat16


def lane_group(shape):
    return lax.broadcasted_iota(jnp.int32, shape, len(shape) - 1) // CH


def by_group(values):
    lane = lax.broadcasted_iota(jnp.int32, values[0].shape, values[0].ndim - 1)
    low = jnp.where(lane < CH, values[0], values[1])
    high = jnp.where(lane < 3 * CH, values[2], values[3])
    return jnp.where(lane < 2 * CH, low, high)


def roll_groups(value, steps):
    steps = steps % QUAD
    if steps == 0:
        return value
    return pltpu.roll(value, steps * CH, value.ndim - 1)


def group_sum(value, ones):
    high = value.astype(BF16)
    low = (value - high.astype(F32)).astype(BF16)
    both = jnp.concatenate([high, low], axis=1)
    return jnp.dot(both, ones, preferred_element_type=F32)


def group_ones():
    row = lax.broadcasted_iota(jnp.int32, (2 * LANES, LANES), 0) % LANES
    col = lax.broadcasted_iota(jnp.int32, (2 * LANES, LANES), 1)
    return jnp.where(row // CH == col // CH, 1.0, 0.0).astype(BF16)


def even(axis):
    return lax.rem(lax.axis_index(axis), 2) == 0


def pack_kernel(
    src_hbm, tgt_hbm, flow_hbm, own_ref, fl_ref, sa_ref, sb_ref,
    wide_ref, src_ref, tgt_ref, flow_ref, sem_ref,
):
    channels, rows, cols = src_ref.shape
    quads = rows // QUAD
    copies = [
        pltpu.make_async_copy(src, dst, sem_ref.at[index])
        for index, (src, dst) in enumerate(
            ((tgt_hbm, tgt_ref), (src_hbm, src_ref), (flow_hbm, flow_ref))
        )
    ]
    for copy in copies:
        copy.start()
    for base, ref in ((0, tgt_ref), (quads, src_ref)):
        copies[base // quads].wait()
        wide_ref[...] = ref[...].astype(F32).reshape(channels * rows, cols)
        for q in range(quads):
            part = jnp.concatenate(
                [wide_ref[pl.ds(q * QUAD + i, channels, stride=rows), :] for i in range(QUAD)],
                axis=0,
            )
            own_ref[base + q] = part.T.astype(BF16)
    copies[2].wait()
    pieces = []
    for f in range(2):
        value = flow_ref[f]
        high = value.astype(BF16).astype(F32)
        pieces += [high, value - high]
    fl_ref[...] = jnp.concatenate(pieces, axis=0).astype(BF16)
    is_even = even("row")
    last = quads - HALO // QUAD
    for dst, first in (
        (sa_ref, jnp.where(is_even, last, 0)),
        (sb_ref, jnp.where(is_even, 0, last)),
    ):
        for k in range(HALO // QUAD):
            dst[k * cols : (k + 1) * cols] = own_ref[first + k]
            dst[(2 + k) * cols : (3 + k) * cols] = own_ref[quads + first + k]
    top = jnp.concatenate([p[:HALO] for p in pieces], axis=0)
    low = jnp.concatenate([p[rows - HALO :] for p in pieces], axis=0)
    sa_ref[4 * cols :] = jnp.where(is_even, low, top).astype(BF16)
    sb_ref[4 * cols :] = jnp.where(is_even, top, low).astype(BF16)


def low_high(axis, near, far):
    index, size = lax.axis_index(axis), lax.axis_size(axis)
    near, far = near.astype(F32), far.astype(F32)
    flag = even(axis)
    outermost = jnp.logical_or(index == 0, index == size - 1)
    far = jnp.where(outermost, 0.0, far)
    return jnp.where(flag, far, near), jnp.where(flag, near, far)


def strip_kernel(own_ref, fl_ref, ra_ref, rb_ref, sc_ref, sd_ref, wide_ref):
    planes, cols, _ = own_ref.shape
    quads = planes // 2
    rows = quads * QUAD
    c_even = even("col")
    for kind in range(2):
        for q in range(quads + 4):
            left = halo_plane(kind, q, own_ref, ra_ref, rb_ref, slice(0, KEYS))[:HALO]
            right = halo_plane(kind, q, own_ref, ra_ref, rb_ref, slice(cols - KEYS, cols))[HALO:]
            row = (kind * (quads + 4) + q) * HALO
            wide_ref[0, row : row + HALO] = jnp.where(c_even, right, left)
            wide_ref[1, row : row + HALO] = jnp.where(c_even, left, right)
    count = 2 * (quads + 4) * HALO
    sc_ref[:count] = wide_ref[0].astype(BF16)
    sd_ref[:count] = wide_ref[1].astype(BF16)
    up, down = flow_up_down(ra_ref, rb_ref)
    flow = []
    own = fl_ref[...].astype(F32)
    for v in range(4):
        flow += [
            up[v * HALO : (v + 1) * HALO],
            own[v * rows : (v + 1) * rows],
            down[v * HALO : (v + 1) * HALO],
        ]
    flow = jnp.concatenate(flow, axis=0).astype(BF16)
    sc_ref[count:] = flow
    sd_ref[count:] = flow


def fill_taps(dst_ref, w_ref):
    zero = jnp.zeros((CH, CH), F32)
    for dx in range(3):
        for block in range(2 * QUAD):
            row = block if block < QUAD else {QUAD: QUAD, 2 * QUAD - 1: -1}.get(block)
            parts = []
            for out in range(QUAD):
                tap = None if row is None else row - out + 1
                ok = tap is not None and 0 <= tap < 3
                parts.append(w_ref[tap, dx].astype(F32) if ok else zero)
            dst_ref[dx, block * CH : (block + 1) * CH, :] = jnp.concatenate(parts, axis=1).astype(
                BF16
            )


def taps_of(ref, quad, start, count):
    main = ref[quad, pl.ds(start, count), :]
    after = ref[quad + 1, pl.ds(start, count), :]
    before = ref[quad - 1, pl.ds(start, count), :]
    lane = lax.broadcasted_iota(jnp.int32, main.shape, 1)
    beside = jnp.where(lane < 2 * CH, after, before)
    return jnp.concatenate([main, beside], axis=1).astype(BF16)


def conv(ref, quad, start, count, w_ref):
    total = jnp.zeros((count, LANES), F32)
    for dx in range(3):
        total += jnp.dot(
            taps_of(ref, quad, start + dx - 1, count), w_ref[dx], preferred_element_type=F32
        )
    return total


SPAN = 3 * QUAD
KEYS = 16


def halo_plane(kind, q, own_ref, ra_ref, rb_ref, part=None):
    planes, cols, _ = own_ref.shape
    quads = planes // 2
    part = part or slice(0, cols)
    if 2 <= q < quads + 2:
        return own_ref[kind * quads + q - 2, part].astype(F32)
    down = q >= quads + 2
    at = (2 * kind + (q - quads - 2 if down else q)) * cols
    part = slice(at + part.start, at + part.stop)
    return low_high("row", ra_ref[part], rb_ref[part])[down]


def edge_plane(kind, q, side, own_ref, ra_ref, rb_ref, rc_ref, rd_ref):
    planes, cols, _ = own_ref.shape
    quads = planes // 2
    tile = slice(0, KEYS) if side == 0 else slice(cols - KEYS, cols)
    mine = halo_plane(kind, q, own_ref, ra_ref, rb_ref, tile)
    index = kind * (quads + 4) + q
    at = index // 2 * 2 * HALO
    fetched = low_high("col", rc_ref[at : at + 2 * HALO], rd_ref[at : at + 2 * HALO])[side]
    fetched = fetched[index % 2 * HALO : index % 2 * HALO + HALO]
    parts = [fetched, mine[:HALO]] if side == 0 else [mine[HALO:], fetched]
    return jnp.concatenate(parts, axis=0)


def flow_up_down(ra_ref, rb_ref):
    at = ra_ref.shape[0] - 4 * HALO
    return low_high("row", ra_ref[at:], rb_ref[at:])


def flow_part(f, ref_or_value, rows):
    parts = [ref_or_value[v * rows : (v + 1) * rows].astype(F32) for v in (2 * f, 2 * f + 1)]
    return parts[0] + parts[1]


def flow_mid(f, fl_ref, ra_ref, rb_ref):
    up, down = flow_up_down(ra_ref, rb_ref)
    return jnp.concatenate(
        [
            flow_part(f, up, HALO),
            flow_part(f, fl_ref, fl_ref.shape[0] // 4),
            flow_part(f, down, HALO),
        ],
        axis=0,
    )


def flow_inner(p_ref, values):
    groups = p_ref.shape[1]
    for f in range(2):
        mid = pltpu.roll(values[f], LANES - RADIUS, 1)
        lane = lax.broadcasted_iota(jnp.int32, mid.shape, 1)
        row = lax.broadcasted_iota(jnp.int32, mid.shape, 0)
        mid = jnp.where(lane < LANES - 8, mid, 0.0)
        turned = [roll_groups(mid, k) for k in range(QUAD)]
        for g in range(groups):
            total = jnp.zeros(mid.shape, F32)
            for i in range(QUAD):
                keep = jnp.logical_and(row % QUAD == i, lane // CH == i)
                total = jnp.where(keep, turned[(i - g) % QUAD], total)
            p_ref[f, g] = total


def flow_edge(e_ref, fl_ref, ra_ref, rb_ref, rc_ref, rd_ref):
    rows = fl_ref.shape[0] // 4
    ext = rows + 2 * HALO
    base = rc_ref.shape[0] - 4 * ext
    left, right = low_high("col", rc_ref[base:], rd_ref[base:])
    for f in range(2):
        mid = flow_mid(f, fl_ref, ra_ref, rb_ref)
        at = 2 * f * ext
        lf = left[at : at + ext] + left[at + ext : at + 2 * ext]
        rt = right[at : at + ext] + right[at + ext : at + 2 * ext]
        lane = lax.broadcasted_iota(jnp.int32, mid.shape, 1)
        row = lax.broadcasted_iota(jnp.int32, mid.shape, 0)
        low = jnp.where(lane < RADIUS, pltpu.roll(lf, RADIUS, 1), pltpu.roll(mid, RADIUS, 1))
        high = jnp.where(
            lane < 3 * RADIUS, pltpu.roll(mid, 3 * RADIUS, 1), pltpu.roll(rt, 3 * RADIUS, 1)
        )
        both = jnp.where(lane < 8, low, high)
        for h in range(2):
            total = jnp.zeros(mid.shape, F32)
            for i in range(QUAD):
                turn = i * CH + h * 16
                keep = jnp.logical_and(row % QUAD == i, lane // 16 == 2 * i + h)
                total = jnp.where(keep, pltpu.roll(both, turn, 1) if turn else both, total)
            e_ref[f, h] = total


def fill_mask(m_ref):
    key = lax.broadcasted_iota(jnp.int32, (SPAN, KEYS, LANES), 0)
    kx = lax.broadcasted_iota(jnp.int32, (SPAN, KEYS, LANES), 1)
    lane = lax.broadcasted_iota(jnp.int32, (SPAN, KEYS, LANES), 2)
    dy = key - lane // CH
    dx = kx - lane % 8
    ok = (dy >= 0) & (dy <= 2 * RADIUS) & (dx >= 0) & (dx <= 2 * RADIUS)
    m_ref[...] = jnp.where(ok, 1.0, 0.0)


def softmax_block(score_ref, m_ref, f0, f1, scale):
    lane = lax.broadcasted_iota(jnp.int32, (KEYS, LANES), 1)
    at_y = (lane // CH + RADIUS).astype(F32)
    at_x = (lane % 8 + RADIUS).astype(F32)
    key_x = lax.broadcasted_iota(jnp.int32, (KEYS, LANES), 0).astype(F32)
    f0 = jnp.broadcast_to(f0, (KEYS, LANES))
    f1 = jnp.broadcast_to(f1, (KEYS, LANES))
    side = f1 * (key_x - at_x) - f0 * at_y
    weights = []
    total = jnp.zeros((KEYS, LANES), F32)
    lean = jnp.zeros((KEYS, LANES), F32)
    for y in range(SPAN):
        weight = score_ref[KEYS * y : KEYS * (y + 1)] * (scale * math.log2(math.e))
        weight = jnp.exp2(weight) * m_ref[y]
        weights.append(weight)
        total = total + weight
        lean = lean + weight * (f0 * float(y) + side)
    total = jnp.sum(total, axis=0, keepdims=True)
    lean = jnp.sum(lean, axis=0, keepdims=True)
    base = jnp.broadcast_to(lean / total, (KEYS, LANES))
    factor = jnp.broadcast_to(scale / total, (KEYS, LANES))
    step = f0 * factor
    side = (side - base) * factor
    return jnp.concatenate(
        [(weights[y] * (step * float(y) + side)).astype(BF16) for y in range(SPAN)], axis=0
    )


def unit_of(field, ones):
    recip = lax.rsqrt(group_sum(field * field, ones) * (1.0 / CH) + 1.0)
    return recip, (field * recip).astype(BF16).astype(F32)


def unit_grad(field, recip, grad, ones):
    inner = group_sum(grad * field, ones)
    return recip * grad - field * (recip * recip * recip) * inner * (1.0 / CH)


def key_rows(t4_ref, first, unit):
    turned = [roll_groups(unit, k) for k in range(QUAD)]
    for i in range(QUAD):
        for g in range(t4_ref.shape[0]):
            t4_ref[g, first + i] = by_group(
                [
                    turned[(j - i) % QUAD][g * GROUP + 8 * j : g * GROUP + 8 * j + KEYS]
                    for j in range(QUAD)
                ]
            ).astype(BF16)


def query_block(octs):
    group = lane_group((8, LANES))
    turned = [
        roll_groups(by_group([octs[(i + k) % QUAD] for i in range(QUAD)]), k)
        for k in range(QUAD)
    ]
    parts = [
        jnp.where(group == j, turned[(j - i) % QUAD], 0.0)
        for i in range(QUAD)
        for j in range(QUAD)
    ]
    return jnp.concatenate(parts, axis=0).astype(BF16)


def packed_rows(mine):
    def piece(i, j):
        at = i * GROUP + 8 * j
        return mine[at : at + 8]

    turned = [
        roll_groups(by_group([piece((j + k) % QUAD, j) for j in range(QUAD)]), k)
        for k in range(QUAD)
    ]
    return [by_group([turned[(i - j) % QUAD] for i in range(QUAD)]) for j in range(QUAD)]


def run_blocks(blocks, m_ref, sc_ref, d_ref, scale):
    def score(b):
        sc_ref[b % 2] = lax.dot_general(
            blocks[b][0](), blocks[b][1](), (((1,), (1,)), ((), ())), preferred_element_type=F32
        )

    def collect(b):
        dscore = d_ref[b % 2]
        keys, queries, _, wanted, put_keys, put_rows = blocks[b]
        put_keys(jnp.dot(dscore[wanted], queries(), preferred_element_type=F32))
        mine = lax.dot_general(
            dscore, keys(), (((0,), (0,)), ((), ())), preferred_element_type=F32
        )
        put_rows(packed_rows(mine))

    score(0)
    for b in range(len(blocks)):
        if b + 1 < len(blocks):
            score(b + 1)
        f0, f1 = blocks[b][2]()
        d_ref[b % 2] = softmax_block(sc_ref.at[b % 2], m_ref, f0, f1, scale)
        if b > 0:
            collect(b - 1)
    collect(len(blocks) - 1)


def conv_from(tap_list, w_ref):
    total = None
    for dx in range(3):
        term = jnp.dot(tap_list[dx], w_ref[dx], preferred_element_type=F32)
        total = term if total is None else total + term
    return total


def inner_block(n, g, keys, q_ref, p_ref, p_quad, ga_ref, gu_ref):
    rows = slice(p_quad * QUAD, (p_quad + 1) * QUAD)
    own = ga_ref.shape[1]
    first = n * QUAD - HALO
    low, high = max(first, 0), min(first + SPAN, own)
    wanted = slice((low - first) * KEYS, (high - first) * KEYS)

    def put_keys(value):
        ga_ref[g, low:high] = ga_ref[g, low:high] + value.reshape(high - low, KEYS, LANES)

    def put_rows(octs):
        for j in range(QUAD):
            gu_ref[n, g * GROUP + 8 * j : g * GROUP + 8 * j + 8] = octs[j]

    return (
        lambda: keys(n, g),
        lambda: q_ref[n, g],
        lambda: [jnp.sum(p_ref[f, g, rows, :], axis=0, keepdims=True) for f in range(2)],
        wanted,
        put_keys,
        put_rows,
    )


def inner_queries(n, es_ref, taps_ref, fe_ref, rf_ref, q_ref, ones, keep=None):
    cols = fe_ref.shape[1]
    tap_list = [taps_of(es_ref, n + 1, RADIUS + dx - 1, cols) for dx in range(3)]
    if keep is not None:
        for dx in range(3):
            keep[n, dx] = tap_list[dx]
    feat = conv_from(tap_list, taps_ref).astype(BF16).astype(F32)
    fe_ref[n] = feat
    recip, unit = unit_of(feat, ones)
    rf_ref[n] = recip
    for g in range(cols // GROUP):
        q_ref[n, g] = query_block(
            [unit[g * GROUP + 8 * j : g * GROUP + 8 * j + 8] for j in range(QUAD)]
        )


def fill_plane(dst_ref, q, value):
    cols = value.shape[0]
    dst_ref[q, :cols] = value
    dst_ref[q, cols:] = jnp.zeros((dst_ref.shape[1] - cols, LANES), F32)


def own_rows(
    quads_of, keys, es_ref, taps_ref, m_ref, p_ref, ga_ref, gf_out, gw_out,
    q_ref, fe_ref, rf_ref, gu_ref, tap_ref, sc_ref, d_ref, ones,
):
    cols = fe_ref.shape[1]
    for n in quads_of:
        inner_queries(n, es_ref, taps_ref, fe_ref, rf_ref, q_ref, ones, tap_ref)
    run_blocks(
        [
            inner_block(n, g, keys, q_ref, p_ref, n - 1, ga_ref, gu_ref)
            for n in quads_of
            for g in range(cols // GROUP)
        ],
        m_ref, sc_ref, d_ref, SHARPNESS / math.sqrt(CH),
    )
    row = lax.broadcasted_iota(jnp.int32, (cols, LANES), 0)
    values = []
    for index, n in enumerate(quads_of):
        value = unit_grad(fe_ref[n], rf_ref[n], gu_ref[n], ones)
        value = jnp.where(row < cols - 8, value, 0.0).astype(BF16)
        gf_out[index] = value
        values.append(value)
    value = jnp.concatenate(values, axis=0)
    for dx in range(3):
        others = jnp.concatenate([tap_ref[n, dx] for n in quads_of], axis=0)
        gw_out[dx] = gw_out[dx] + lax.dot_general(
            value, others, (((0,), (0,)), ((), ())), preferred_element_type=F32
        )


def early_kernel(
    own_ref, fl_ref, w_ref, wt_ref,
    t4_out, taps_out, back_out, m_out, p_out, ga_out, gf_out, gw_out,
    es_ref, q_ref, fe_ref, rf_ref, gu_ref, tap_ref, sc_ref, d_ref,
):
    planes, cols, _ = own_ref.shape
    quads = planes // 2
    width = es_ref.shape[1]
    ones = group_ones()
    fill_taps(taps_out, w_ref)
    fill_taps(back_out, wt_ref)
    fill_mask(m_out)
    flow_inner(p_out, [flow_part(f, fl_ref, quads * QUAD) for f in range(2)])
    for q in range(quads):
        fill_plane(es_ref, q + 2, own_ref[quads + q].astype(F32))
        _, unit = unit_of(own_ref[q].astype(F32), ones)
        pad = jnp.zeros((width - cols, LANES), F32)
        key_rows(t4_out, q * QUAD, jnp.concatenate([unit, pad], axis=0))
    ga_out[...] = jnp.zeros_like(ga_out)
    gw_out[...] = jnp.zeros_like(gw_out)

    def keys(n, g):
        at = (n - 2) * QUAD
        return t4_out[g, at : at + SPAN].reshape(SPAN * KEYS, LANES)

    own_rows(
        range(2, quads), keys, es_ref, taps_out, m_out, p_out, ga_out, gf_out, gw_out,
        q_ref, fe_ref, rf_ref, gu_ref, tap_ref, sc_ref, d_ref, ones,
    )


def middle_kernel(
    own_ref, ra_ref, rb_ref, t4_ref, taps_ref, m_ref, p_ref, ga_in, gw_in,
    t4_out, ga_out, gf_out, gw_out,
    es_ref, q_ref, fe_ref, rf_ref, gu_ref, tap_ref, sc_ref, d_ref,
):
    planes, cols, _ = own_ref.shape
    quads = planes // 2
    width = es_ref.shape[1]
    ones = group_ones()
    for q in (1, 2, 3, quads, quads + 1, quads + 2):
        fill_plane(es_ref, q, halo_plane(1, q, own_ref, ra_ref, rb_ref))
    pad = jnp.zeros((width - cols, LANES), F32)
    for k, q in enumerate((1, quads + 2)):
        _, unit = unit_of(halo_plane(0, q, own_ref, ra_ref, rb_ref), ones)
        key_rows(t4_out, k * QUAD, jnp.concatenate([unit, pad], axis=0))

    def keys(n, g):
        if n == 1:
            parts = [t4_out[g, :QUAD], t4_ref[g, : 2 * QUAD]]
        else:
            parts = [t4_ref[g, (quads - 2) * QUAD :], t4_out[g, QUAD:]]
        return jnp.concatenate(parts, axis=0).reshape(SPAN * KEYS, LANES)

    own_rows(
        (1, quads), keys, es_ref, taps_ref, m_ref, p_ref, ga_out, gf_out, gw_out,
        q_ref, fe_ref, rf_ref, gu_ref, tap_ref, sc_ref, d_ref, ones,
    )


def edge_blocks(
    pairs, first, ee_ref, tu_ref, taps_ref, t4_ref, q_ref, ep_ref, ga_ref, ones, keep=None
):
    blocks, stores = [], []
    for e, pair in enumerate(pairs):
        quad_of = [pair[j // 2] for j in range(QUAD)]
        tap_list = [
            jnp.concatenate(
                [
                    taps_of(ee_ref.at[j % 2], quad_of[j] + 1, RADIUS + dx - 1, 8).astype(F32)
                    for j in range(QUAD)
                ],
                axis=0,
            ).astype(BF16)
            for dx in range(3)
        ]
        feat = conv_from(tap_list, taps_ref).astype(BF16).astype(F32)
        recip, unit = unit_of(feat, ones)
        q_ref[e] = query_block([unit[8 * j : 8 * j + 8] for j in range(QUAD)])
        for y in range(SPAN):
            t4_ref[e, y] = by_group(
                [
                    tu_ref[(j - y) % QUAD, j % 2, quad_of[j] + y // QUAD]
                    for j in range(QUAD)
                ]
            ).astype(BF16)
        result = []
        stores.append((tap_list, feat, recip, result))

        def flows(pair=pair):
            total = []
            for f in range(2):
                parts = [
                    jnp.sum(
                        ep_ref[f, h, (pair[h] + 1) * QUAD : (pair[h] + 2) * QUAD, :],
                        axis=0,
                        keepdims=True,
                    )
                    for h in range(2)
                ]
                total.append(parts[0] + parts[1])
            return total

        def put_keys(value, e=e):
            ga_ref[first + e] = value.reshape(SPAN, KEYS, LANES)

        blocks.append(
            (
                lambda e=e: t4_ref[e].reshape(SPAN * KEYS, LANES),
                lambda e=e: q_ref[e],
                flows,
                slice(0, SPAN * KEYS),
                put_keys,
                result.extend,
            )
        )
    return blocks, stores


def edge_planes(ee_ref, tu_ref, ones, quads_of, keys_of, refs):
    for side in range(2):
        for q in quads_of:
            ee_ref[side, q] = edge_plane(1, q, side, *refs)
        raw = jnp.concatenate([edge_plane(0, q, side, *refs) for q in keys_of], axis=0)
        _, unit = unit_of(raw, ones)
        for k in range(QUAD):
            turned = roll_groups(unit, k)
            for index, q in enumerate(keys_of):
                tu_ref[k, side, q] = turned[index * KEYS : (index + 1) * KEYS]


def edge_grads(stores, ones):
    return [
        unit_grad(feat, recip, jnp.concatenate(result, axis=0), ones).astype(BF16)
        for _, feat, recip, result in stores
    ]


def pairs_of(quads):
    return [(n, n + 1) for n in range(1, quads + 1, 2)]


def edge_kernel(
    own_ref, fl_ref, ra_ref, rb_ref, rc_ref, rd_ref, taps_ref, m_ref, gw_ref,
    ga_ref, gf_out, gw_out,
    ee_ref, tu_ref, t4_ref, q_ref, ep_ref, sc_ref, d_ref,
):
    planes, cols, _ = own_ref.shape
    quads = planes // 2
    ext = quads + 4
    scale = SHARPNESS / math.sqrt(CH)
    ones = group_ones()
    refs = (own_ref, ra_ref, rb_ref, rc_ref, rd_ref)
    edge_planes(ee_ref, tu_ref, ones, range(1, ext - 1), range(1, ext - 1), refs)
    flow_edge(ep_ref, fl_ref, ra_ref, rb_ref, rc_ref, rd_ref)
    blocks, stores = edge_blocks(
        pairs_of(quads), 0, ee_ref, tu_ref, taps_ref, t4_ref, q_ref, ep_ref, ga_ref, ones
    )
    run_blocks(blocks, m_ref, sc_ref, d_ref, scale)
    totals = [gw_ref[dx] for dx in range(3)]
    row = lax.broadcasted_iota(jnp.int32, (GROUP, LANES), 0)
    inside = jnp.logical_xor(row // 8 % 2 == 0, row % 8 < RADIUS)
    for e, grad in enumerate(edge_grads(stores, ones)):
        gf_out[e] = grad
        grad = jnp.where(inside, grad.astype(F32), 0.0).astype(BF16)
        for dx in range(3):
            totals[dx] = totals[dx] + lax.dot_general(
                grad, stores[e][0][dx], (((0,), (0,)), ((), ())), preferred_element_type=F32
            )
    lane = lax.broadcasted_iota(jnp.int32, (CH, LANES), 1)
    for dx, total in enumerate(totals):
        rows_of = [total[i * CH : (i + 1) * CH] for i in range(QUAD)]
        main = [x[:, :LANES] for x in rows_of]
        beside = [x[:, LANES:] for x in rows_of]
        start = jnp.where(lane < CH, roll_groups(beside[0], 1), roll_groups(main[0], 1))
        last = jnp.where(lane < 2 * CH, roll_groups(main[3], 2), roll_groups(beside[3], 2))
        gw_out[dx * CH : (dx + 1) * CH] = (start + main[1]) + (roll_groups(main[2], 3) + last)


def spread(dst_ref, quad, value, channels, rows):
    flipped = value.T
    for i in range(QUAD):
        dst_ref[pl.ds(quad * QUAD + i, channels, stride=rows), :] = flipped[
            i * CH : (i + 1) * CH
        ]


def outer_kernel(
    lower, own_ref, ra_ref, rb_ref, taps_ref, m_ref, t4_own, t4_halo, ga_in,
    ga_out, gf_out,
    es_ref, t4_ref, q_ref, fe_ref, rf_ref, gu_ref, p_ref, sc_ref, d_ref,
):
    planes, cols, _ = own_ref.shape
    quads = planes // 2
    width = es_ref.shape[1]
    ones = group_ones()
    n = quads + 1 if lower else 0
    for q in (n, n + 1, n + 2):
        fill_plane(es_ref, q, halo_plane(1, q, own_ref, ra_ref, rb_ref))
    flow_inner(
        p_ref, [flow_part(f, flow_up_down(ra_ref, rb_ref)[lower], HALO) for f in range(2)]
    )
    _, unit = unit_of(halo_plane(0, quads + 3 if lower else 0, own_ref, ra_ref, rb_ref), ones)
    pad = jnp.zeros((width - cols, LANES), F32)
    key_rows(t4_ref, 0, jnp.concatenate([unit, pad], axis=0))

    def keys(n, g):
        if lower:
            parts = [t4_own[g, (quads - 1) * QUAD :], t4_halo[g, QUAD:], t4_ref[g]]
        else:
            parts = [t4_ref[g], t4_halo[g, :QUAD], t4_own[g, :QUAD]]
        return jnp.concatenate(parts, axis=0).reshape(SPAN * KEYS, LANES)

    inner_queries(n, es_ref, taps_ref, fe_ref, rf_ref, q_ref, ones)
    run_blocks(
        [
            inner_block(n, g, keys, q_ref, p_ref, 0 if lower else 1, ga_out, gu_ref)
            for g in range(cols // GROUP)
        ],
        m_ref, sc_ref, d_ref, SHARPNESS / math.sqrt(CH),
    )
    gf_out[...] = unit_grad(fe_ref[n], rf_ref[n], gu_ref[n], ones).astype(BF16)


def corner_kernel(
    own_ref, fl_ref, ra_ref, rb_ref, rc_ref, rd_ref, taps_ref, m_ref,
    ge_out, gf_out,
    ee_ref, tu_ref, t4_ref, q_ref, ep_ref, sc_ref, d_ref,
):
    quads = own_ref.shape[0] // 2
    ext = quads + 4
    ones = group_ones()
    refs = (own_ref, ra_ref, rb_ref, rc_ref, rd_ref)
    near = (0, 1, 2, ext - 3, ext - 2, ext - 1)
    edge_planes(ee_ref, tu_ref, ones, near, near, refs)
    flow_edge(ep_ref, fl_ref, ra_ref, rb_ref, rc_ref, rd_ref)
    blocks, stores = edge_blocks(
        [(0, quads + 1)], 0, ee_ref, tu_ref, taps_ref, t4_ref, q_ref, ep_ref, ge_out, ones
    )
    run_blocks(blocks, m_ref, sc_ref, d_ref, SHARPNESS / math.sqrt(CH))
    gf_out[...] = edge_grads(stores, ones)[0]


def image_kernel(
    own_ref, back_ref, ga_ref, gem_ref, gec_ref,
    gf_early, gf_middle, gf_top, gf_low, gfe_ref, gfc_ref,
    gs_out, gt_out,
    full_ref, wide_ref,
):
    channels, rows, cols = gs_out.shape
    quads = rows // QUAD
    ones = group_ones()
    rows_of = {0: gf_top[...], quads + 1: gf_low[...], 1: gf_middle[0], quads: gf_middle[1]}
    for n in range(2, quads):
        rows_of[n] = gf_early[n - 2]
    for n, value in rows_of.items():
        full_ref[n, 8 : 8 + cols] = value.astype(F32)
    edges = [gfe_ref[e] for e in range(quads // 2)] + [gfc_ref[...]]
    where_is = {}
    for e, (pair, grad) in enumerate(zip(pairs_of(quads) + [(0, quads + 1)], edges)):
        grad = grad.astype(F32)
        for j in range(QUAD):
            at = 0 if j % 2 == 0 else cols
            full_ref[pair[j // 2], at : at + 8] = grad[8 * j : 8 * j + 8]
            where_is[pair[j // 2], j % 2] = (e, j)

    for q in range(quads):
        tap_list = [taps_of(full_ref, q + 1, RADIUS + dx - 1, cols) for dx in range(3)]
        spread(wide_ref, q, conv_from(tap_list, back_ref), channels, rows)
    gs_out[...] = wide_ref[...].astype(BF16).reshape(channels, rows, cols)

    group = lane_group((8, LANES))
    last = cols // 8
    for q in range(quads):
        parts = []
        for oct in range(1, last + 1):
            total = None
            for k in range(QUAD):
                both = jnp.zeros((8, LANES), F32)
                for half, which in ((0, oct), (1, oct - 1)):
                    if not 0 < which < last:
                        continue
                    g, j = divmod(which - 1, QUAD)
                    at = q * QUAD + (j + k) % QUAD
                    both = jnp.where(group == j, ga_ref[g, at, 8 * half : 8 * half + 8], both)
                both = roll_groups(both, k)
                total = both if total is None else total + both
            side = 0 if oct == 1 else 1 if oct == last else None
            if side is not None:
                half = 1 - side
                for n in range(q, q + 3):
                    e, j = where_is[n, side]
                    ref = gem_ref.at[e] if e < quads // 2 else gec_ref.at[0]
                    for i in range(QUAD):
                        part = ref[(q + 2 - n) * QUAD + i, 8 * half : 8 * half + 8]
                        total = total + roll_groups(jnp.where(group == j, part, 0.0), i - j)
            parts.append(total)
        grad = jnp.concatenate(parts, axis=0)
        field = own_ref[q].astype(F32)
        recip = lax.rsqrt(group_sum(field * field, ones) * (1.0 / CH) + 1.0)
        spread(wide_ref, q, unit_grad(field, recip, grad, ones), channels, rows)
    gt_out[...] = wide_ref[...].astype(BF16).reshape(channels, rows, cols)


def final_kernel(scale, one_ref, two_ref, out_ref):
    for dx in range(3):
        at = slice(dx * CH, (dx + 1) * CH)
        total = ((one_ref[at].astype(F32) + two_ref[at].astype(F32)) * scale).T
        for tap in range(3):
            out_ref[tap, dx] = total[tap * CH : (tap + 1) * CH]


def pair_exchange(x, y, axis):
    rows, cols = lax.axis_size("row"), lax.axis_size("col")
    near, far = [], []
    for r in range(rows):
        for c in range(cols):
            index, size = (r, rows) if axis == "row" else (c, cols)
            other = index + 1 if index % 2 else index - 1
            for pairs, to in ((near, index ^ 1), (far, other)):
                if 0 <= to < size:
                    target = (to, c) if axis == "row" else (r, to)
                else:
                    target = (r, c ^ 1) if axis == "row" else (r ^ 1, c)
                pairs.append((r * cols + c, target[0] * cols + target[1]))
    both = ("row", "col")
    return lax.ppermute(x, both, near), lax.ppermute(y, both, far)


def swap(x, flips):
    rows, cols = lax.axis_size("row"), lax.axis_size("col")
    flip_r, flip_c = flips.get("row", 0), flips.get("col", 0)
    pairs = [
        (r * cols + c, (r ^ flip_r) * cols + (c ^ flip_c)) for r in range(rows) for c in range(cols)
    ]
    return lax.ppermute(x, ("row", "col"), pairs)


def after(value, *others):
    return lax.optimization_barrier((value, *others))[0]


def vmem(count):
    return [pl.BlockSpec(memory_space=pltpu.VMEM)] * count


def per_device(source, target, conv_weight, flow_cotangent):
    channels, rows, cols = source.shape
    quads = rows // QUAD
    ext = quads + 4
    groups = cols // GROUP
    width = cols + HALO
    asked = quads + 2
    flipped = jnp.transpose(conv_weight[::-1, ::-1], (0, 1, 3, 2))
    shape = jax.ShapeDtypeStruct

    def scratch(*dims, dtype=F32):
        return pltpu.VMEM(dims, dtype)

    def call(kernel, name, outs, scratches, *args, cycles=1000, alias=None, specs=None):
        return pl.pallas_call(
            kernel,
            out_shape=tuple(outs),
            in_specs=specs or vmem(len(args)),
            out_specs=tuple(vmem(len(outs))),
            scratch_shapes=scratches,
            input_output_aliases=alias or {},
            cost_estimate=pl.CostEstimate(
                flops=cycles * 250_000, bytes_accessed=cycles * 1000, transcendentals=0
            ),
            compiler_params=pltpu.CompilerParams(vmem_limit_bytes=16 << 20),
            name=name,
        )(*args)

    side = shape((4 * cols + 4 * HALO, LANES), BF16)
    own, flow, to_a, to_b = call(
        pack_kernel,
        "pack",
        [shape((2 * quads, cols, LANES), BF16), shape((4 * rows, cols), BF16), side, side],
        [
            scratch(channels * rows, cols),
            scratch(*source.shape, dtype=BF16),
            scratch(*target.shape, dtype=BF16),
            scratch(*flow_cotangent.shape),
            pltpu.SemaphoreType.DMA((3,)),
        ],
        *(
            pltpu.with_memory_space_constraint(x, pltpu.HBM)
            for x in (source, target, flow_cotangent)
        ),
        specs=[pl.BlockSpec(memory_space=pltpu.HBM)] * 3,
    )
    ra, rb = pair_exchange(to_a, to_b, "row")
    taps = shape((3, 2 * LANES, LANES), BF16)
    stages = [scratch(2, SPAN * KEYS, LANES), scratch(2, SPAN * KEYS, LANES, dtype=BF16)]
    inner = [
        scratch(asked, groups, LANES, LANES, dtype=BF16),
        scratch(asked, cols, LANES),
        scratch(asked, cols, LANES),
        scratch(asked, cols, LANES),
    ]
    planes = scratch(ext, width, LANES)
    tap_lists = scratch(asked, 3, cols, 2 * LANES, dtype=BF16)
    for_keys = shape((groups, rows, KEYS, LANES), F32)
    for_kernel = shape((3, LANES, 2 * LANES), F32)
    for_feat = shape((2, cols, LANES), BF16)
    keys, forward, back, mask, cotangents, grad_keys, feat_early, terms = call(
        early_kernel,
        "early",
        [
            shape((groups, rows, KEYS, LANES), BF16),
            taps,
            taps,
            shape((SPAN, KEYS, LANES), F32),
            shape((2, groups, rows, LANES), F32),
            for_keys,
            shape((quads - 2, cols, LANES), BF16),
            for_kernel,
        ],
        [planes] + inner + [tap_lists] + stages,
        own,
        flow,
        conv_weight,
        flipped,
        cycles=3000,
    )
    strip = shape((2 * ext * HALO + 4 * ext * QUAD, LANES), BF16)
    to_c, to_d = call(
        strip_kernel,
        "strip",
        [strip, strip],
        [scratch(2, 2 * ext * HALO, LANES)],
        own,
        flow,
        ra,
        rb,
    )
    rc, rd = pair_exchange(to_c, to_d, "col")
    halo_keys, grad_keys, feat_middle, terms = call(
        middle_kernel,
        "middle",
        [shape((groups, 2 * QUAD, KEYS, LANES), BF16), for_keys, for_feat, for_kernel],
        [planes] + inner + [tap_lists] + stages,
        own,
        ra,
        rb,
        keys,
        forward,
        mask,
        cotangents,
        grad_keys,
        terms,
        cycles=3000,
        alias={7: 1, 8: 3},
    )
    pairs = quads // 2
    outer = [scratch(2, ext, KEYS, LANES), scratch(QUAD, 2, ext, KEYS, LANES)]
    fetched = (own, flow, ra, rb, rc, rd, forward, mask)

    def edge_scratch(count):
        return outer + [
            scratch(count, SPAN, KEYS, LANES, dtype=BF16),
            scratch(count, LANES, LANES, dtype=BF16),
            scratch(2, 2, ext * QUAD, LANES),
        ] + stages

    edge_keys, edge_feat, terms = call(
        edge_kernel,
        "edge",
        [
            shape((pairs, SPAN, KEYS, LANES), F32),
            shape((pairs, GROUP, LANES), BF16),
            shape((3 * CH, LANES), F32),
        ],
        edge_scratch(pairs),
        *fetched,
        terms,
    )

    def outer_rows(lower, sums):
        return call(
            functools.partial(outer_kernel, lower),
            "lower" if lower else "upper",
            [for_keys, shape((cols, LANES), BF16)],
            [planes, scratch(groups, QUAD, KEYS, LANES, dtype=BF16)]
            + inner
            + [scratch(2, groups, HALO, LANES)]
            + stages,
            after(own, sums),
            ra,
            rb,
            forward,
            mask,
            keys,
            halo_keys,
            grad_keys,
            alias={7: 0},
            cycles=1500,
        )

    bits = {axis: [] for axis in ("row", "col")}
    for axis, found in bits.items():
        step = 1
        while step < lax.axis_size(axis):
            found.append({axis: step})
            step *= 2
    steps = [[bits["row"][0]]]
    down, along = bits["row"][1:], bits["col"]
    while down or along:
        if True and down and along and len(down) + len(along) > 2:
            one, two = down.pop(0), along.pop(0)
            steps.append([one, two, {**one, **two}])
        else:
            steps.append([(down or along).pop(0)])

    def exchange(value, step):
        value = value.astype(F32) if step is not steps[0] else value
        return [value] + [swap(value, flips) for flips in step]

    def total_of(parts):
        parts = [x.astype(F32) for x in parts]
        return parts[0] + parts[1] if len(parts) == 2 else (parts[0] + parts[1]) + (parts[2] + parts[3])

    for index, step in enumerate(steps[:-1]):
        parts = exchange(terms, step)
        if index == len(steps) - 2:
            grad_keys, feat_low = outer_rows(1, terms)
            corner_keys, corner_feat = call(
                corner_kernel,
                "corner",
                [shape((1, SPAN, KEYS, LANES), F32), shape((GROUP, LANES), BF16)],
                edge_scratch(1),
                after(own, terms),
                *fetched[1:],
            )
            done = (feat_low, corner_feat)
            if len(step) > 1:
                grad_keys, feat_top = outer_rows(0, terms)
                done = (*done, feat_top)
        elif index == len(steps) - 3 and len(steps[-2]) == 1:
            grad_keys, feat_top = outer_rows(0, terms)
            done = (feat_top,)
        else:
            done = ()
        terms = total_of(parts)
        if done:
            terms = after(terms, done)
    own_terms, arriving = exchange(terms, steps[-1])
    grad_source, grad_target = call(
        image_kernel,
        "image",
        [shape(source.shape, BF16), shape(target.shape, BF16)],
        [scratch(asked, 8 + cols, LANES), scratch(channels * rows, cols)],
        after(own, terms),
        back,
        grad_keys,
        edge_keys,
        corner_keys,
        feat_early,
        feat_middle,
        feat_top,
        feat_low,
        edge_feat,
        corner_feat,
        cycles=2000,
    )
    pixels = rows * cols * lax.axis_size("row") * lax.axis_size("col")
    (grad_weight,) = call(
        functools.partial(final_kernel, 1.0 / math.sqrt(pixels)),
        "final",
        [shape((3, 3, CH, CH), F32)],
        [],
        own_terms,
        arriving,
        cycles=10,
    )
    return (grad_source, grad_target, grad_weight)


def solution(mesh):
    placed = (
        P(None, ("sec", "row"), "col"),
        P(None, ("sec", "row"), "col"),
        P(),
        P(None, ("sec", "row"), "col"),
    )
    return jax.shard_map(
        per_device,
        mesh=mesh,
        in_specs=placed,
        out_specs=(
            P(None, ("sec", "row"), "col"),
            P(None, ("sec", "row"), "col"),
            P("sec", None, None, None),
        ),
        check_vma=False,
    )
```

```python
import functools
import math

import jax
import jax.numpy as jnp
from jax import lax
from jax.experimental import pallas as pl
from jax.experimental.pallas import tpu as pltpu
from jax.sharding import PartitionSpec as P

RADIUS = 4
SHARPNESS = 4.0
CH = 32
QUAD = 4
LANES = QUAD * CH
GROUP = 32
HALO = 2 * RADIUS
F32 = jnp.float32
BF16 = jnp.bfloat16


def lane_group(shape):
    return lax.broadcasted_iota(jnp.int32, shape, len(shape) - 1) // CH


def by_group(values):
    lane = lax.broadcasted_iota(jnp.int32, values[0].shape, values[0].ndim - 1)
    low = jnp.where(lane < CH, values[0], values[1])
    high = jnp.where(lane < 3 * CH, values[2], values[3])
    return jnp.where(lane < 2 * CH, low, high)


def roll(value, lanes):
    lanes = lanes % value.shape[-1]
    return pltpu.roll(value, lanes, value.ndim - 1) if lanes else value


def roll_groups(value, steps):
    steps = steps % QUAD
    if steps == 0:
        return value
    return pltpu.roll(value, steps * CH, value.ndim - 1)


def group_sum(value, ones):
    high = value.astype(BF16)
    low = (value - high.astype(F32)).astype(BF16)
    both = jnp.concatenate([high, low], axis=1)
    return jnp.dot(both, ones, preferred_element_type=F32)


def group_ones():
    row = lax.broadcasted_iota(jnp.int32, (2 * LANES, LANES), 0) % LANES
    col = lax.broadcasted_iota(jnp.int32, (2 * LANES, LANES), 1)
    return jnp.where(row // CH == col // CH, 1.0, 0.0).astype(BF16)


def even(axis):
    return lax.rem(lax.axis_index(axis), 2) == 0


def one_row(plane, row):
    plane = plane.astype(F32)
    count = plane.shape[0] // QUAD
    return by_group(
        [roll_groups(plane[b * count : (b + 1) * count], b - row) for b in range(QUAD)]
    )


def pack_kernel(
    src_hbm, tgt_hbm, flow_hbm, own_ref, fl_ref, sa_ref, sb_ref,
    wide_ref, src_ref, tgt_ref, flow_ref, sem_ref,
):
    channels, rows, cols = src_ref.shape
    quads = rows // QUAD
    copies = [
        pltpu.make_async_copy(src, dst, sem_ref.at[index])
        for index, (src, dst) in enumerate(
            ((tgt_hbm, tgt_ref), (src_hbm, src_ref), (flow_hbm, flow_ref))
        )
    ]
    for copy in copies:
        copy.start()
    for base, ref in ((0, tgt_ref), (quads, src_ref)):
        copies[base // quads].wait()
        wide_ref[...] = ref[...].astype(F32).reshape(channels * rows, cols)
        for q in range(quads):
            part = jnp.concatenate(
                [wide_ref[pl.ds(q * QUAD + i, channels, stride=rows), :] for i in range(QUAD)],
                axis=0,
            )
            own_ref[base + q] = part.T.astype(BF16)
    copies[2].wait()
    pieces = []
    for f in range(2):
        value = flow_ref[f]
        high = value.astype(BF16).astype(F32)
        pieces += [high, value - high]
    fl_ref[...] = jnp.concatenate(pieces, axis=0).astype(BF16)
    is_even = even("row")
    last = quads - HALO // QUAD
    for dst, first in (
        (sa_ref, jnp.where(is_even, last, 0)),
        (sb_ref, jnp.where(is_even, 0, last)),
    ):
        for k in range(HALO // QUAD):
            dst[k * cols : (k + 1) * cols] = own_ref[first + k]
    top = [own_ref[quads].astype(F32), one_row(own_ref[quads + 1], 0)]
    low = [own_ref[2 * quads - 1].astype(F32), one_row(own_ref[2 * quads - 2], QUAD - 1)]
    top = jnp.concatenate(top + [p[:HALO] for p in pieces], axis=0)
    low = jnp.concatenate(low + [p[rows - HALO :] for p in pieces], axis=0)
    sa_ref[2 * cols :] = jnp.where(is_even, low, top).astype(BF16)
    sb_ref[2 * cols :] = jnp.where(is_even, top, low).astype(BF16)


def low_high(axis, near, far):
    index, size = lax.axis_index(axis), lax.axis_size(axis)
    near, far = near.astype(F32), far.astype(F32)
    flag = even(axis)
    outermost = jnp.logical_or(index == 0, index == size - 1)
    far = jnp.where(outermost, 0.0, far)
    return jnp.where(flag, far, near), jnp.where(flag, near, far)


def strip_kernel(own_ref, fl_ref, ra_ref, rb_ref, sc_ref, sd_ref, wide_ref):
    planes, cols, _ = own_ref.shape
    quads = planes // 2
    rows = quads * QUAD
    c_even = even("col")
    for kind in range(2):
        for q in range(quads + 4):
            left = halo_plane(kind, q, own_ref, ra_ref, rb_ref, slice(0, KEYS))[:HALO]
            right = halo_plane(kind, q, own_ref, ra_ref, rb_ref, slice(cols - KEYS, cols))[HALO:]
            row = (kind * (quads + 4) + q) * HALO
            wide_ref[0, row : row + HALO] = jnp.where(c_even, right, left)
            wide_ref[1, row : row + HALO] = jnp.where(c_even, left, right)
    count = 2 * (quads + 4) * HALO
    sc_ref[:count] = wide_ref[0].astype(BF16)
    sd_ref[:count] = wide_ref[1].astype(BF16)
    up, down = flow_up_down(ra_ref, rb_ref)
    own = fl_ref[...].astype(F32)
    left = right = jnp.zeros((rows + 2 * HALO, cols), F32)
    lane = lax.broadcasted_iota(jnp.int32, left.shape, 1)
    for v in range(4):
        flow = jnp.concatenate(
            [
                up[v * HALO : (v + 1) * HALO],
                own[v * rows : (v + 1) * rows],
                down[v * HALO : (v + 1) * HALO],
            ],
            axis=0,
        )
        here = lane // RADIUS == v
        left = jnp.where(here, roll(flow, v * RADIUS), left)
        right = jnp.where(here, roll(flow, (v + 1) * RADIUS), right)
    sc_ref[count:] = jnp.where(c_even, right, left).astype(BF16)
    sd_ref[count:] = jnp.where(c_even, left, right).astype(BF16)


def fill_taps(dst_ref, w_ref):
    zero = jnp.zeros((CH, CH), F32)
    for dx in range(3):
        for block in range(2 * QUAD):
            row = block if block < QUAD else {QUAD: QUAD, 2 * QUAD - 1: -1}.get(block)
            parts = []
            for out in range(QUAD):
                tap = None if row is None else row - out + 1
                ok = tap is not None and 0 <= tap < 3
                parts.append(w_ref[tap, dx].astype(F32) if ok else zero)
            dst_ref[dx, block * CH : (block + 1) * CH, :] = jnp.concatenate(parts, axis=1).astype(
                BF16
            )


def taps_of(ref, quad, start, count):
    main = ref[quad, pl.ds(start, count), :]
    after = ref[quad + 1, pl.ds(start, count), :]
    before = ref[quad - 1, pl.ds(start, count), :]
    lane = lax.broadcasted_iota(jnp.int32, main.shape, 1)
    beside = jnp.where(lane < 2 * CH, after, before)
    return jnp.concatenate([main, beside], axis=1).astype(BF16)


def conv(ref, quad, start, count, w_ref):
    total = jnp.zeros((count, LANES), F32)
    for dx in range(3):
        total += jnp.dot(
            taps_of(ref, quad, start + dx - 1, count), w_ref[dx], preferred_element_type=F32
        )
    return total


SPAN = 3 * QUAD
KEYS = 16


def halo_plane(kind, q, own_ref, ra_ref, rb_ref, part=None):
    planes, cols, _ = own_ref.shape
    quads = planes // 2
    part = part or slice(0, cols)
    if 2 <= q < quads + 2:
        return own_ref[kind * quads + q - 2, part].astype(F32)
    down = q >= quads + 2
    if kind == 1 and q in (0, quads + 3):
        row, count = (0 if down else QUAD - 1), cols // QUAD
        at = 3 * cols
        packed = low_high("row", ra_ref[at : at + count], rb_ref[at : at + count])[down]
        parts = []
        for b in range(part.start // count, (part.stop - 1) // count + 1):
            first, last = max(part.start - b * count, 0), min(part.stop - b * count, count)
            parts.append(roll_groups(packed, row - b)[first:last])
        return jnp.concatenate(parts, axis=0)
    at = 2 * cols if kind == 1 else (q - quads - 2 if down else q) * cols
    part = slice(at + part.start, at + part.stop)
    return low_high("row", ra_ref[part], rb_ref[part])[down]


def edge_plane(kind, q, side, own_ref, ra_ref, rb_ref, rc_ref, rd_ref):
    planes, cols, _ = own_ref.shape
    quads = planes // 2
    tile = slice(0, KEYS) if side == 0 else slice(cols - KEYS, cols)
    mine = halo_plane(kind, q, own_ref, ra_ref, rb_ref, tile)
    index = kind * (quads + 4) + q
    at = index // 2 * 2 * HALO
    fetched = low_high("col", rc_ref[at : at + 2 * HALO], rd_ref[at : at + 2 * HALO])[side]
    fetched = fetched[index % 2 * HALO : index % 2 * HALO + HALO]
    parts = [fetched, mine[:HALO]] if side == 0 else [mine[HALO:], fetched]
    return jnp.concatenate(parts, axis=0)


def flow_up_down(ra_ref, rb_ref):
    at = ra_ref.shape[0] - 4 * HALO
    return low_high("row", ra_ref[at:], rb_ref[at:])


def flow_part(f, ref_or_value, rows):
    parts = [ref_or_value[v * rows : (v + 1) * rows].astype(F32) for v in (2 * f, 2 * f + 1)]
    return parts[0] + parts[1]


def flow_mid(f, fl_ref, ra_ref, rb_ref):
    up, down = flow_up_down(ra_ref, rb_ref)
    return jnp.concatenate(
        [
            flow_part(f, up, HALO),
            flow_part(f, fl_ref, fl_ref.shape[0] // 4),
            flow_part(f, down, HALO),
        ],
        axis=0,
    )


def flow_inner(p_ref, values):
    groups = p_ref.shape[1]
    for f in range(2):
        mid = pltpu.roll(values[f], LANES - RADIUS, 1)
        lane = lax.broadcasted_iota(jnp.int32, mid.shape, 1)
        row = lax.broadcasted_iota(jnp.int32, mid.shape, 0)
        mid = jnp.where(lane < LANES - 8, mid, 0.0)
        turned = [roll_groups(mid, k) for k in range(QUAD)]
        for g in range(groups):
            total = jnp.zeros(mid.shape, F32)
            for i in range(QUAD):
                keep = jnp.logical_and(row % QUAD == i, lane // CH == i)
                total = jnp.where(keep, turned[(i - g) % QUAD], total)
            p_ref[f, g] = total


def flow_edge(e_ref, fl_ref, ra_ref, rb_ref, rc_ref, rd_ref):
    rows = fl_ref.shape[0] // 4
    ext = rows + 2 * HALO
    base = rc_ref.shape[0] - ext
    left, right = low_high("col", rc_ref[base:], rd_ref[base:])
    for f in range(2):
        mid = flow_mid(f, fl_ref, ra_ref, rb_ref)
        at = 2 * f * RADIUS
        lf = roll(left, -at) + roll(left, -at - RADIUS)
        rt = roll(right, 3 * RADIUS - at) + roll(right, 2 * RADIUS - at)
        lane = lax.broadcasted_iota(jnp.int32, mid.shape, 1)
        row = lax.broadcasted_iota(jnp.int32, mid.shape, 0)
        low = jnp.where(lane < RADIUS, lf, roll(mid, RADIUS))
        high = jnp.where(
            lane < 3 * RADIUS, roll(mid, 3 * RADIUS), rt
        )
        both = jnp.where(lane < 8, low, high)
        for h in range(2):
            total = jnp.zeros(mid.shape, F32)
            for i in range(QUAD):
                turn = i * CH + h * 16
                keep = jnp.logical_and(row % QUAD == i, lane // 16 == 2 * i + h)
                total = jnp.where(keep, pltpu.roll(both, turn, 1) if turn else both, total)
            e_ref[f, h] = total


def fill_mask(m_ref):
    key = lax.broadcasted_iota(jnp.int32, (SPAN, KEYS, LANES), 0)
    kx = lax.broadcasted_iota(jnp.int32, (SPAN, KEYS, LANES), 1)
    lane = lax.broadcasted_iota(jnp.int32, (SPAN, KEYS, LANES), 2)
    dy = key - lane // CH
    dx = kx - lane % 8
    ok = (dy >= 0) & (dy <= 2 * RADIUS) & (dx >= 0) & (dx <= 2 * RADIUS)
    m_ref[...] = jnp.where(ok, 1.0, 0.0)


def softmax_block(score_ref, m_ref, f0, f1, scale):
    lane = lax.broadcasted_iota(jnp.int32, (KEYS, LANES), 1)
    at_y = (lane // CH + RADIUS).astype(F32)
    at_x = (lane % 8 + RADIUS).astype(F32)
    key_x = lax.broadcasted_iota(jnp.int32, (KEYS, LANES), 0).astype(F32)
    f0 = jnp.broadcast_to(f0, (KEYS, LANES))
    f1 = jnp.broadcast_to(f1, (KEYS, LANES))
    side = f1 * (key_x - at_x) - f0 * at_y
    weights = []
    total = jnp.zeros((KEYS, LANES), F32)
    lean = jnp.zeros((KEYS, LANES), F32)
    for y in range(SPAN):
        weight = score_ref[KEYS * y : KEYS * (y + 1)] * (scale * math.log2(math.e))
        weight = jnp.exp2(weight) * m_ref[y]
        weights.append(weight)
        total = total + weight
        lean = lean + weight * (f0 * float(y) + side)
    total = jnp.sum(total, axis=0, keepdims=True)
    lean = jnp.sum(lean, axis=0, keepdims=True)
    base = jnp.broadcast_to(lean / total, (KEYS, LANES))
    factor = jnp.broadcast_to(scale / total, (KEYS, LANES))
    step = f0 * factor
    side = (side - base) * factor
    return jnp.concatenate(
        [(weights[y] * (step * float(y) + side)).astype(BF16) for y in range(SPAN)], axis=0
    )


def unit_of(field, ones):
    recip = lax.rsqrt(group_sum(field * field, ones) * (1.0 / CH) + 1.0)
    return recip, (field * recip).astype(BF16).astype(F32)


def unit_grad(field, recip, grad, ones):
    inner = group_sum(grad * field, ones)
    return recip * grad - field * (recip * recip * recip) * inner * (1.0 / CH)


def key_rows(t4_ref, first, unit):
    turned = [roll_groups(unit, k) for k in range(QUAD)]
    for i in range(QUAD):
        for g in range(t4_ref.shape[0]):
            t4_ref[g, first + i] = by_group(
                [
                    turned[(j - i) % QUAD][g * GROUP + 8 * j : g * GROUP + 8 * j + KEYS]
                    for j in range(QUAD)
                ]
            ).astype(BF16)


def query_block(octs):
    group = lane_group((8, LANES))
    turned = [
        roll_groups(by_group([octs[(i + k) % QUAD] for i in range(QUAD)]), k)
        for k in range(QUAD)
    ]
    parts = [
        jnp.where(group == j, turned[(j - i) % QUAD], 0.0)
        for i in range(QUAD)
        for j in range(QUAD)
    ]
    return jnp.concatenate(parts, axis=0).astype(BF16)


def packed_rows(mine):
    def piece(i, j):
        at = i * GROUP + 8 * j
        return mine[at : at + 8]

    turned = [
        roll_groups(by_group([piece((j + k) % QUAD, j) for j in range(QUAD)]), k)
        for k in range(QUAD)
    ]
    return [by_group([turned[(i - j) % QUAD] for i in range(QUAD)]) for j in range(QUAD)]


def run_blocks(blocks, m_ref, sc_ref, d_ref, scale):
    def score(b):
        sc_ref[b % 2] = lax.dot_general(
            blocks[b][0](), blocks[b][1](), (((1,), (1,)), ((), ())), preferred_element_type=F32
        )

    def collect(b):
        dscore = d_ref[b % 2]
        keys, queries, _, wanted, put_keys, put_rows = blocks[b]
        put_keys(jnp.dot(dscore[wanted], queries(), preferred_element_type=F32))
        mine = lax.dot_general(
            dscore, keys(), (((0,), (0,)), ((), ())), preferred_element_type=F32
        )
        put_rows(packed_rows(mine))

    score(0)
    for b in range(len(blocks)):
        if b + 1 < len(blocks):
            score(b + 1)
        f0, f1 = blocks[b][2]()
        d_ref[b % 2] = softmax_block(sc_ref.at[b % 2], m_ref, f0, f1, scale)
        if b > 0:
            collect(b - 1)
    collect(len(blocks) - 1)


def conv_from(tap_list, w_ref):
    total = None
    for dx in range(3):
        term = jnp.dot(tap_list[dx], w_ref[dx], preferred_element_type=F32)
        total = term if total is None else total + term
    return total


def inner_block(n, g, keys, q_ref, p_ref, p_quad, ga_ref, gu_ref):
    rows = slice(p_quad * QUAD, (p_quad + 1) * QUAD)
    own = ga_ref.shape[1]
    first = n * QUAD - HALO
    low, high = max(first, 0), min(first + SPAN, own)
    wanted = slice((low - first) * KEYS, (high - first) * KEYS)

    def put_keys(value):
        ga_ref[g, low:high] = ga_ref[g, low:high] + value.reshape(high - low, KEYS, LANES)

    def put_rows(octs):
        for j in range(QUAD):
            gu_ref[n, g * GROUP + 8 * j : g * GROUP + 8 * j + 8] = octs[j]

    return (
        lambda: keys(n, g),
        lambda: q_ref[n, g],
        lambda: [jnp.sum(p_ref[f, g, rows, :], axis=0, keepdims=True) for f in range(2)],
        wanted,
        put_keys,
        put_rows,
    )


def inner_queries(n, es_ref, taps_ref, fe_ref, rf_ref, q_ref, ones, keep=None):
    cols = fe_ref.shape[1]
    tap_list = [taps_of(es_ref, n + 1, RADIUS + dx - 1, cols) for dx in range(3)]
    if keep is not None:
        for dx in range(3):
            keep[n, dx] = tap_list[dx]
    feat = conv_from(tap_list, taps_ref).astype(BF16).astype(F32)
    fe_ref[n] = feat
    recip, unit = unit_of(feat, ones)
    rf_ref[n] = recip
    for g in range(cols // GROUP):
        q_ref[n, g] = query_block(
            [unit[g * GROUP + 8 * j : g * GROUP + 8 * j + 8] for j in range(QUAD)]
        )


def fill_plane(dst_ref, q, value):
    cols = value.shape[0]
    dst_ref[q, :cols] = value
    dst_ref[q, cols:] = jnp.zeros((dst_ref.shape[1] - cols, LANES), F32)


def own_rows(
    quads_of, keys, es_ref, taps_ref, m_ref, p_ref, ga_ref, gf_out, gw_out,
    q_ref, fe_ref, rf_ref, gu_ref, tap_ref, sc_ref, d_ref, ones,
):
    cols = fe_ref.shape[1]
    for n in quads_of:
        inner_queries(n, es_ref, taps_ref, fe_ref, rf_ref, q_ref, ones, tap_ref)
    run_blocks(
        [
            inner_block(n, g, keys, q_ref, p_ref, n - 1, ga_ref, gu_ref)
            for n in quads_of
            for g in range(cols // GROUP)
        ],
        m_ref, sc_ref, d_ref, SHARPNESS / math.sqrt(CH),
    )
    row = lax.broadcasted_iota(jnp.int32, (cols, LANES), 0)
    values = []
    for index, n in enumerate(quads_of):
        value = unit_grad(fe_ref[n], rf_ref[n], gu_ref[n], ones)
        value = jnp.where(row < cols - 8, value, 0.0).astype(BF16)
        gf_out[index] = value
        values.append(value)
    value = jnp.concatenate(values, axis=0)
    for dx in range(3):
        others = jnp.concatenate([tap_ref[n, dx] for n in quads_of], axis=0)
        gw_out[dx] = gw_out[dx] + lax.dot_general(
            value, others, (((0,), (0,)), ((), ())), preferred_element_type=F32
        )


def early_kernel(
    own_ref, fl_ref, w_ref, wt_ref,
    t4_out, taps_out, back_out, m_out, p_out, ga_out, gf_out, gw_out,
    es_ref, q_ref, fe_ref, rf_ref, gu_ref, tap_ref, sc_ref, d_ref,
):
    planes, cols, _ = own_ref.shape
    quads = planes // 2
    width = es_ref.shape[1]
    ones = group_ones()
    fill_taps(taps_out, w_ref)
    fill_taps(back_out, wt_ref)
    fill_mask(m_out)
    flow_inner(p_out, [flow_part(f, fl_ref, quads * QUAD) for f in range(2)])
    for q in range(quads):
        fill_plane(es_ref, q + 2, own_ref[quads + q].astype(F32))
        _, unit = unit_of(own_ref[q].astype(F32), ones)
        pad = jnp.zeros((width - cols, LANES), F32)
        key_rows(t4_out, q * QUAD, jnp.concatenate([unit, pad], axis=0))
    ga_out[...] = jnp.zeros_like(ga_out)
    gw_out[...] = jnp.zeros_like(gw_out)

    def keys(n, g):
        at = (n - 2) * QUAD
        return t4_out[g, at : at + SPAN].reshape(SPAN * KEYS, LANES)

    own_rows(
        range(2, quads), keys, es_ref, taps_out, m_out, p_out, ga_out, gf_out, gw_out,
        q_ref, fe_ref, rf_ref, gu_ref, tap_ref, sc_ref, d_ref, ones,
    )


def middle_kernel(
    own_ref, ra_ref, rb_ref, t4_ref, taps_ref, m_ref, p_ref, ga_in, gw_in,
    t4_out, ga_out, gf_out, gw_out,
    es_ref, q_ref, fe_ref, rf_ref, gu_ref, tap_ref, sc_ref, d_ref,
):
    planes, cols, _ = own_ref.shape
    quads = planes // 2
    width = es_ref.shape[1]
    ones = group_ones()
    for q in (1, 2, 3, quads, quads + 1, quads + 2):
        fill_plane(es_ref, q, halo_plane(1, q, own_ref, ra_ref, rb_ref))
    pad = jnp.zeros((width - cols, LANES), F32)
    for k, q in enumerate((1, quads + 2)):
        _, unit = unit_of(halo_plane(0, q, own_ref, ra_ref, rb_ref), ones)
        key_rows(t4_out, k * QUAD, jnp.concatenate([unit, pad], axis=0))

    def keys(n, g):
        if n == 1:
            parts = [t4_out[g, :QUAD], t4_ref[g, : 2 * QUAD]]
        else:
            parts = [t4_ref[g, (quads - 2) * QUAD :], t4_out[g, QUAD:]]
        return jnp.concatenate(parts, axis=0).reshape(SPAN * KEYS, LANES)

    own_rows(
        (1, quads), keys, es_ref, taps_ref, m_ref, p_ref, ga_out, gf_out, gw_out,
        q_ref, fe_ref, rf_ref, gu_ref, tap_ref, sc_ref, d_ref, ones,
    )


def edge_blocks(
    pairs, first, ee_ref, tu_ref, taps_ref, t4_ref, q_ref, ep_ref, ga_ref, ones, keep=None
):
    blocks, stores = [], []
    for e, pair in enumerate(pairs):
        quad_of = [pair[j // 2] for j in range(QUAD)]
        tap_list = [
            jnp.concatenate(
                [
                    taps_of(ee_ref.at[j % 2], quad_of[j] + 1, RADIUS + dx - 1, 8).astype(F32)
                    for j in range(QUAD)
                ],
                axis=0,
            ).astype(BF16)
            for dx in range(3)
        ]
        feat = conv_from(tap_list, taps_ref).astype(BF16).astype(F32)
        recip, unit = unit_of(feat, ones)
        q_ref[e] = query_block([unit[8 * j : 8 * j + 8] for j in range(QUAD)])
        for y in range(SPAN):
            t4_ref[e, y] = by_group(
                [
                    tu_ref[(j - y) % QUAD, j % 2, quad_of[j] + y // QUAD]
                    for j in range(QUAD)
                ]
            ).astype(BF16)
        result = []
        stores.append((tap_list, feat, recip, result))

        def flows(pair=pair):
            total = []
            for f in range(2):
                parts = [
                    jnp.sum(
                        ep_ref[f, h, (pair[h] + 1) * QUAD : (pair[h] + 2) * QUAD, :],
                        axis=0,
                        keepdims=True,
                    )
                    for h in range(2)
                ]
                total.append(parts[0] + parts[1])
            return total

        def put_keys(value, e=e):
            ga_ref[first + e] = value.reshape(SPAN, KEYS, LANES)

        blocks.append(
            (
                lambda e=e: t4_ref[e].reshape(SPAN * KEYS, LANES),
                lambda e=e: q_ref[e],
                flows,
                slice(0, SPAN * KEYS),
                put_keys,
                result.extend,
            )
        )
    return blocks, stores


def edge_planes(ee_ref, tu_ref, ones, quads_of, keys_of, refs):
    for side in range(2):
        for q in quads_of:
            ee_ref[side, q] = edge_plane(1, q, side, *refs)
        raw = jnp.concatenate([edge_plane(0, q, side, *refs) for q in keys_of], axis=0)
        _, unit = unit_of(raw, ones)
        for k in range(QUAD):
            turned = roll_groups(unit, k)
            for index, q in enumerate(keys_of):
                tu_ref[k, side, q] = turned[index * KEYS : (index + 1) * KEYS]


def edge_grads(stores, ones):
    return [
        unit_grad(feat, recip, jnp.concatenate(result, axis=0), ones).astype(BF16)
        for _, feat, recip, result in stores
    ]


def pairs_of(quads):
    return [(n, n + 1) for n in range(1, quads + 1, 2)]


def edge_kernel(
    own_ref, fl_ref, ra_ref, rb_ref, rc_ref, rd_ref, taps_ref, m_ref, gw_ref,
    ga_ref, gf_out, gw_out,
    ee_ref, tu_ref, t4_ref, q_ref, ep_ref, sc_ref, d_ref,
):
    planes, cols, _ = own_ref.shape
    quads = planes // 2
    ext = quads + 4
    scale = SHARPNESS / math.sqrt(CH)
    ones = group_ones()
    refs = (own_ref, ra_ref, rb_ref, rc_ref, rd_ref)
    edge_planes(ee_ref, tu_ref, ones, range(1, ext - 1), range(1, ext - 1), refs)
    flow_edge(ep_ref, fl_ref, ra_ref, rb_ref, rc_ref, rd_ref)
    blocks, stores = edge_blocks(
        pairs_of(quads), 0, ee_ref, tu_ref, taps_ref, t4_ref, q_ref, ep_ref, ga_ref, ones
    )
    run_blocks(blocks, m_ref, sc_ref, d_ref, scale)
    totals = [gw_ref[dx] for dx in range(3)]
    row = lax.broadcasted_iota(jnp.int32, (GROUP, LANES), 0)
    inside = jnp.logical_xor(row // 8 % 2 == 0, row % 8 < RADIUS)
    for e, grad in enumerate(edge_grads(stores, ones)):
        gf_out[e] = grad
        grad = jnp.where(inside, grad.astype(F32), 0.0).astype(BF16)
        for dx in range(3):
            totals[dx] = totals[dx] + lax.dot_general(
                grad, stores[e][0][dx], (((0,), (0,)), ((), ())), preferred_element_type=F32
            )
    lane = lax.broadcasted_iota(jnp.int32, (CH, LANES), 1)
    for dx, total in enumerate(totals):
        rows_of = [total[i * CH : (i + 1) * CH] for i in range(QUAD)]
        main = [x[:, :LANES] for x in rows_of]
        beside = [x[:, LANES:] for x in rows_of]
        start = jnp.where(lane < CH, roll_groups(beside[0], 1), roll_groups(main[0], 1))
        last = jnp.where(lane < 2 * CH, roll_groups(main[3], 2), roll_groups(beside[3], 2))
        totals[dx] = (start + main[1]) + (roll_groups(main[2], 3) + last)
    for dx in range(2):
        gw_out[dx * CH : (dx + 1) * CH] = jnp.where(
            lane < 3 * CH, totals[dx], roll_groups(totals[2], 3 - dx)
        )
    gw_out[2 * CH :] = one_row(totals[2], 2)


def spread(dst_ref, quad, value, channels, rows):
    flipped = value.T
    for i in range(QUAD):
        dst_ref[pl.ds(quad * QUAD + i, channels, stride=rows), :] = flipped[
            i * CH : (i + 1) * CH
        ]


def outer_kernel(
    lower, own_ref, ra_ref, rb_ref, taps_ref, m_ref, t4_own, t4_halo, ga_in,
    ga_out, gf_out,
    es_ref, t4_ref, q_ref, fe_ref, rf_ref, gu_ref, p_ref, sc_ref, d_ref,
):
    planes, cols, _ = own_ref.shape
    quads = planes // 2
    width = es_ref.shape[1]
    ones = group_ones()
    n = quads + 1 if lower else 0
    for q in (n, n + 1, n + 2):
        fill_plane(es_ref, q, halo_plane(1, q, own_ref, ra_ref, rb_ref))
    flow_inner(
        p_ref, [flow_part(f, flow_up_down(ra_ref, rb_ref)[lower], HALO) for f in range(2)]
    )
    _, unit = unit_of(halo_plane(0, quads + 3 if lower else 0, own_ref, ra_ref, rb_ref), ones)
    pad = jnp.zeros((width - cols, LANES), F32)
    key_rows(t4_ref, 0, jnp.concatenate([unit, pad], axis=0))

    def keys(n, g):
        if lower:
            parts = [t4_own[g, (quads - 1) * QUAD :], t4_halo[g, QUAD:], t4_ref[g]]
        else:
            parts = [t4_ref[g], t4_halo[g, :QUAD], t4_own[g, :QUAD]]
        return jnp.concatenate(parts, axis=0).reshape(SPAN * KEYS, LANES)

    inner_queries(n, es_ref, taps_ref, fe_ref, rf_ref, q_ref, ones)
    run_blocks(
        [
            inner_block(n, g, keys, q_ref, p_ref, 0 if lower else 1, ga_out, gu_ref)
            for g in range(cols // GROUP)
        ],
        m_ref, sc_ref, d_ref, SHARPNESS / math.sqrt(CH),
    )
    gf_out[...] = unit_grad(fe_ref[n], rf_ref[n], gu_ref[n], ones).astype(BF16)


def corner_kernel(
    own_ref, fl_ref, ra_ref, rb_ref, rc_ref, rd_ref, taps_ref, m_ref,
    ge_out, gf_out,
    ee_ref, tu_ref, t4_ref, q_ref, ep_ref, sc_ref, d_ref,
):
    quads = own_ref.shape[0] // 2
    ext = quads + 4
    ones = group_ones()
    refs = (own_ref, ra_ref, rb_ref, rc_ref, rd_ref)
    near = (0, 1, 2, ext - 3, ext - 2, ext - 1)
    edge_planes(ee_ref, tu_ref, ones, near, near, refs)
    flow_edge(ep_ref, fl_ref, ra_ref, rb_ref, rc_ref, rd_ref)
    blocks, stores = edge_blocks(
        [(0, quads + 1)], 0, ee_ref, tu_ref, taps_ref, t4_ref, q_ref, ep_ref, ge_out, ones
    )
    run_blocks(blocks, m_ref, sc_ref, d_ref, SHARPNESS / math.sqrt(CH))
    gf_out[...] = edge_grads(stores, ones)[0]


def image_kernel(
    own_ref, back_ref, ga_ref, gem_ref, gec_ref,
    gf_early, gf_middle, gf_top, gf_low, gfe_ref, gfc_ref,
    gs_out, gt_out,
    full_ref, wide_ref,
):
    channels, rows, cols = gs_out.shape
    quads = rows // QUAD
    ones = group_ones()
    rows_of = {0: gf_top[...], quads + 1: gf_low[...], 1: gf_middle[0], quads: gf_middle[1]}
    for n in range(2, quads):
        rows_of[n] = gf_early[n - 2]
    for n, value in rows_of.items():
        full_ref[n, 8 : 8 + cols] = value.astype(F32)
    edges = [gfe_ref[e] for e in range(quads // 2)] + [gfc_ref[...]]
    where_is = {}
    for e, (pair, grad) in enumerate(zip(pairs_of(quads) + [(0, quads + 1)], edges)):
        grad = grad.astype(F32)
        for j in range(QUAD):
            at = 0 if j % 2 == 0 else cols
            full_ref[pair[j // 2], at : at + 8] = grad[8 * j : 8 * j + 8]
            where_is[pair[j // 2], j % 2] = (e, j)

    for q in range(quads):
        tap_list = [taps_of(full_ref, q + 1, RADIUS + dx - 1, cols) for dx in range(3)]
        spread(wide_ref, q, conv_from(tap_list, back_ref), channels, rows)
    gs_out[...] = wide_ref[...].astype(BF16).reshape(channels, rows, cols)

    group = lane_group((8, LANES))
    last = cols // 8
    for q in range(quads):
        parts = []
        for oct in range(1, last + 1):
            total = None
            for k in range(QUAD):
                both = jnp.zeros((8, LANES), F32)
                for half, which in ((0, oct), (1, oct - 1)):
                    if not 0 < which < last:
                        continue
                    g, j = divmod(which - 1, QUAD)
                    at = q * QUAD + (j + k) % QUAD
                    both = jnp.where(group == j, ga_ref[g, at, 8 * half : 8 * half + 8], both)
                both = roll_groups(both, k)
                total = both if total is None else total + both
            side = 0 if oct == 1 else 1 if oct == last else None
            if side is not None:
                half = 1 - side
                for n in range(q, q + 3):
                    e, j = where_is[n, side]
                    ref = gem_ref.at[e] if e < quads // 2 else gec_ref.at[0]
                    for i in range(QUAD):
                        part = ref[(q + 2 - n) * QUAD + i, 8 * half : 8 * half + 8]
                        total = total + roll_groups(jnp.where(group == j, part, 0.0), i - j)
            parts.append(total)
        grad = jnp.concatenate(parts, axis=0)
        field = own_ref[q].astype(F32)
        recip = lax.rsqrt(group_sum(field * field, ones) * (1.0 / CH) + 1.0)
        spread(wide_ref, q, unit_grad(field, recip, grad, ones), channels, rows)
    gt_out[...] = wide_ref[...].astype(BF16).reshape(channels, rows, cols)


def final_kernel(scale, one_ref, two_ref, out_ref):
    total = (one_ref[...].astype(F32) + two_ref[...].astype(F32)) * scale
    first, second, rest = total[:CH], total[CH : 2 * CH], total[2 * CH :]
    rest = jnp.concatenate([roll_groups(rest, 2 - b) for b in range(QUAD)], axis=0)
    third = by_group([roll_groups(first, 1), roll_groups(second, 2), rest, rest])
    for dx, value in enumerate((first, second, third)):
        value = value.T
        for tap in range(3):
            out_ref[tap, dx] = value[tap * CH : (tap + 1) * CH]


def pair_exchange(x, y, axis):
    rows, cols = lax.axis_size("row"), lax.axis_size("col")
    near, far = [], []
    for r in range(rows):
        for c in range(cols):
            index, size = (r, rows) if axis == "row" else (c, cols)
            other = index + 1 if index % 2 else index - 1
            for pairs, to in ((near, index ^ 1), (far, other)):
                if 0 <= to < size:
                    target = (to, c) if axis == "row" else (r, to)
                else:
                    target = (r, c ^ 1) if axis == "row" else (r ^ 1, c)
                pairs.append((r * cols + c, target[0] * cols + target[1]))
    both = ("row", "col")
    return lax.ppermute(x, both, near), lax.ppermute(y, both, far)


def swap(x, flips):
    rows, cols = lax.axis_size("row"), lax.axis_size("col")
    flip_r, flip_c = flips.get("row", 0), flips.get("col", 0)
    pairs = [
        (r * cols + c, (r ^ flip_r) * cols + (c ^ flip_c)) for r in range(rows) for c in range(cols)
    ]
    return lax.ppermute(x, ("row", "col"), pairs)


def after(value, *others):
    return lax.optimization_barrier((value, *others))[0]


def vmem(count):
    return [pl.BlockSpec(memory_space=pltpu.VMEM)] * count


def per_device(source, target, conv_weight, flow_cotangent):
    channels, rows, cols = source.shape
    quads = rows // QUAD
    ext = quads + 4
    groups = cols // GROUP
    width = cols + HALO
    asked = quads + 2
    flipped = jnp.transpose(conv_weight[::-1, ::-1], (0, 1, 3, 2))
    shape = jax.ShapeDtypeStruct

    def scratch(*dims, dtype=F32):
        return pltpu.VMEM(dims, dtype)

    def call(kernel, name, outs, scratches, *args, cycles=1000, alias=None, specs=None):
        return pl.pallas_call(
            kernel,
            out_shape=tuple(outs),
            in_specs=specs or vmem(len(args)),
            out_specs=tuple(vmem(len(outs))),
            scratch_shapes=scratches,
            input_output_aliases=alias or {},
            cost_estimate=pl.CostEstimate(
                flops=cycles * 250_000, bytes_accessed=cycles * 1000, transcendentals=0
            ),
            compiler_params=pltpu.CompilerParams(vmem_limit_bytes=16 << 20),
            name=name,
        )(*args)

    side = shape((3 * cols + cols // QUAD + 4 * HALO, LANES), BF16)
    own, flow, to_a, to_b = call(
        pack_kernel,
        "pack",
        [shape((2 * quads, cols, LANES), BF16), shape((4 * rows, cols), BF16), side, side],
        [
            scratch(channels * rows, cols),
            scratch(*source.shape, dtype=BF16),
            scratch(*target.shape, dtype=BF16),
            scratch(*flow_cotangent.shape),
            pltpu.SemaphoreType.DMA((3,)),
        ],
        *(
            pltpu.with_memory_space_constraint(x, pltpu.HBM)
            for x in (source, target, flow_cotangent)
        ),
        specs=[pl.BlockSpec(memory_space=pltpu.HBM)] * 3,
    )
    ra, rb = pair_exchange(to_a, to_b, "row")
    taps = shape((3, 2 * LANES, LANES), BF16)
    stages = [scratch(2, SPAN * KEYS, LANES), scratch(2, SPAN * KEYS, LANES, dtype=BF16)]
    inner = [
        scratch(asked, groups, LANES, LANES, dtype=BF16),
        scratch(asked, cols, LANES),
        scratch(asked, cols, LANES),
        scratch(asked, cols, LANES),
    ]
    planes = scratch(ext, width, LANES)
    tap_lists = scratch(asked, 3, cols, 2 * LANES, dtype=BF16)
    for_keys = shape((groups, rows, KEYS, LANES), F32)
    for_kernel = shape((3, LANES, 2 * LANES), F32)
    for_feat = shape((2, cols, LANES), BF16)
    keys, forward, back, mask, cotangents, grad_keys, feat_early, terms = call(
        early_kernel,
        "early",
        [
            shape((groups, rows, KEYS, LANES), BF16),
            taps,
            taps,
            shape((SPAN, KEYS, LANES), F32),
            shape((2, groups, rows, LANES), F32),
            for_keys,
            shape((quads - 2, cols, LANES), BF16),
            for_kernel,
        ],
        [planes] + inner + [tap_lists] + stages,
        own,
        flow,
        conv_weight,
        flipped,
        cycles=3000,
    )
    strip = shape((2 * ext * HALO + ext * QUAD, LANES), BF16)
    to_c, to_d = call(
        strip_kernel,
        "strip",
        [strip, strip],
        [scratch(2, 2 * ext * HALO, LANES)],
        own,
        flow,
        ra,
        rb,
    )
    rc, rd = pair_exchange(to_c, to_d, "col")
    halo_keys, grad_keys, feat_middle, terms = call(
        middle_kernel,
        "middle",
        [shape((groups, 2 * QUAD, KEYS, LANES), BF16), for_keys, for_feat, for_kernel],
        [planes] + inner + [tap_lists] + stages,
        own,
        ra,
        rb,
        keys,
        forward,
        mask,
        cotangents,
        grad_keys,
        terms,
        cycles=3000,
        alias={7: 1, 8: 3},
    )
    pairs = quads // 2
    outer = [scratch(2, ext, KEYS, LANES), scratch(QUAD, 2, ext, KEYS, LANES)]
    fetched = (own, flow, ra, rb, rc, rd, forward, mask)

    def edge_scratch(count):
        return outer + [
            scratch(count, SPAN, KEYS, LANES, dtype=BF16),
            scratch(count, LANES, LANES, dtype=BF16),
            scratch(2, 2, ext * QUAD, LANES),
        ] + stages

    edge_keys, edge_feat, terms = call(
        edge_kernel,
        "edge",
        [
            shape((pairs, SPAN, KEYS, LANES), F32),
            shape((pairs, GROUP, LANES), BF16),
            shape((2 * CH + CH // QUAD, LANES), F32),
        ],
        edge_scratch(pairs),
        *fetched,
        terms,
    )

    def outer_rows(lower, sums):
        return call(
            functools.partial(outer_kernel, lower),
            "lower" if lower else "upper",
            [for_keys, shape((cols, LANES), BF16)],
            [planes, scratch(groups, QUAD, KEYS, LANES, dtype=BF16)]
            + inner
            + [scratch(2, groups, HALO, LANES)]
            + stages,
            after(own, sums),
            ra,
            rb,
            forward,
            mask,
            keys,
            halo_keys,
            grad_keys,
            alias={7: 0},
            cycles=1500,
        )

    bits = {axis: [] for axis in ("row", "col")}
    for axis, found in bits.items():
        step = 1
        while step < lax.axis_size(axis):
            found.append({axis: step})
            step *= 2
    steps = [[bits["row"][0]]]
    down, along = bits["row"][1:], bits["col"]
    while down or along:
        if True and down and along and len(down) + len(along) > 2:
            one, two = down.pop(0), along.pop(0)
            steps.append([one, two, {**one, **two}])
        else:
            steps.append([(down or along).pop(0)])

    def exchange(value, step):
        value = value.astype(BF16) if step is not steps[0] else value
        return [value] + [swap(value, flips) for flips in step]

    def total_of(parts):
        parts = [x.astype(F32) for x in parts]
        return parts[0] + parts[1] if len(parts) == 2 else (parts[0] + parts[1]) + (parts[2] + parts[3])

    for index, step in enumerate(steps[:-1]):
        parts = exchange(terms, step)
        done = ()
        if index == 0:
            corner_keys, corner_feat = call(
                corner_kernel,
                "corner",
                [shape((1, SPAN, KEYS, LANES), F32), shape((GROUP, LANES), BF16)],
                edge_scratch(1),
                after(own, terms),
                *fetched[1:],
            )
            done = (corner_feat,)
        if index == len(steps) - 2:
            grad_keys, feat_low = outer_rows(1, terms)
            done = (*done, feat_low)
            if len(step) > 1:
                grad_keys, feat_top = outer_rows(0, terms)
                done = (*done, feat_top)
        elif index == len(steps) - 3 and len(steps[-2]) == 1:
            grad_keys, feat_top = outer_rows(0, terms)
            done = (*done, feat_top)
        terms = total_of(parts)
        if done:
            terms = after(terms, done)
    own_terms, arriving = exchange(terms, steps[-1])
    grad_source, grad_target = call(
        image_kernel,
        "image",
        [shape(source.shape, BF16), shape(target.shape, BF16)],
        [scratch(asked, 8 + cols, LANES), scratch(channels * rows, cols)],
        after(own, terms),
        back,
        grad_keys,
        edge_keys,
        corner_keys,
        feat_early,
        feat_middle,
        feat_top,
        feat_low,
        edge_feat,
        corner_feat,
        cycles=2000,
    )
    pixels = rows * cols * lax.axis_size("row") * lax.axis_size("col")
    (grad_weight,) = call(
        functools.partial(final_kernel, 1.0 / math.sqrt(pixels)),
        "final",
        [shape((3, 3, CH, CH), F32)],
        [],
        own_terms,
        arriving,
        cycles=10,
    )
    return (grad_source, grad_target, grad_weight)


def solution(mesh):
    placed = (
        P(None, ("sec", "row"), "col"),
        P(None, ("sec", "row"), "col"),
        P(),
        P(None, ("sec", "row"), "col"),
    )
    return jax.shard_map(
        per_device,
        mesh=mesh,
        in_specs=placed,
        out_specs=(
            P(None, ("sec", "row"), "col"),
            P(None, ("sec", "row"), "col"),
            P("sec", None, None, None),
        ),
        check_vma=False,
    )
```

```python
import functools
import math

import jax
import jax.numpy as jnp
from jax import lax
from jax.experimental import pallas as pl
from jax.experimental.pallas import tpu as pltpu
from jax.sharding import PartitionSpec as P

RADIUS = 4
SHARPNESS = 4.0
CH = 32
QUAD = 4
LANES = QUAD * CH
GROUP = 32
HALO = 2 * RADIUS
F32 = jnp.float32
BF16 = jnp.bfloat16


def lane_group(shape):
    return lax.broadcasted_iota(jnp.int32, shape, len(shape) - 1) // CH


def by_group(values):
    lane = lax.broadcasted_iota(jnp.int32, values[0].shape, values[0].ndim - 1)
    low = jnp.where(lane < CH, values[0], values[1])
    high = jnp.where(lane < 3 * CH, values[2], values[3])
    return jnp.where(lane < 2 * CH, low, high)


def roll(value, lanes):
    lanes = lanes % value.shape[-1]
    return pltpu.roll(value, lanes, value.ndim - 1) if lanes else value


def roll_groups(value, steps):
    steps = steps % QUAD
    if steps == 0:
        return value
    return pltpu.roll(value, steps * CH, value.ndim - 1)


def group_sum(value, ones):
    high = value.astype(BF16)
    low = (value - high.astype(F32)).astype(BF16)
    both = jnp.concatenate([high, low], axis=1)
    return jnp.dot(both, ones, preferred_element_type=F32)


def group_ones():
    row = lax.broadcasted_iota(jnp.int32, (2 * LANES, LANES), 0) % LANES
    col = lax.broadcasted_iota(jnp.int32, (2 * LANES, LANES), 1)
    return jnp.where(row // CH == col // CH, 1.0, 0.0).astype(BF16)


def even(axis):
    return lax.rem(lax.axis_index(axis), 2) == 0


def one_row(plane, row):
    plane = plane.astype(F32)
    count = plane.shape[0] // QUAD
    return by_group(
        [roll_groups(plane[b * count : (b + 1) * count], b - row) for b in range(QUAD)]
    )


def pack_kernel(
    src_hbm, tgt_hbm, flow_hbm, own_ref, fl_ref, sa_ref, sb_ref,
    wide_ref, src_ref, tgt_ref, flow_ref, sem_ref,
):
    channels, rows, cols = src_ref.shape
    quads = rows // QUAD
    copies = [
        pltpu.make_async_copy(src, dst, sem_ref.at[index])
        for index, (src, dst) in enumerate(
            ((tgt_hbm, tgt_ref), (src_hbm, src_ref), (flow_hbm, flow_ref))
        )
    ]
    for copy in copies:
        copy.start()
    for base, ref in ((0, tgt_ref), (quads, src_ref)):
        copies[base // quads].wait()
        wide_ref[...] = ref[...].astype(F32).reshape(channels * rows, cols)
        for q in range(quads):
            part = jnp.concatenate(
                [wide_ref[pl.ds(q * QUAD + i, channels, stride=rows), :] for i in range(QUAD)],
                axis=0,
            )
            own_ref[base + q] = part.T.astype(BF16)
    copies[2].wait()
    pieces = []
    for f in range(2):
        value = flow_ref[f]
        high = value.astype(BF16).astype(F32)
        pieces += [high, value - high]
    fl_ref[...] = jnp.concatenate(pieces, axis=0).astype(BF16)
    is_even = even("row")
    last = quads - HALO // QUAD
    for dst, first in (
        (sa_ref, jnp.where(is_even, last, 0)),
        (sb_ref, jnp.where(is_even, 0, last)),
    ):
        for k in range(HALO // QUAD):
            dst[k * cols : (k + 1) * cols] = own_ref[first + k]
    top = [own_ref[quads].astype(F32), one_row(own_ref[quads + 1], 0)]
    low = [own_ref[2 * quads - 1].astype(F32), one_row(own_ref[2 * quads - 2], QUAD - 1)]
    top = jnp.concatenate(top + [p[:HALO] for p in pieces], axis=0)
    low = jnp.concatenate(low + [p[rows - HALO :] for p in pieces], axis=0)
    sa_ref[2 * cols :] = jnp.where(is_even, low, top).astype(BF16)
    sb_ref[2 * cols :] = jnp.where(is_even, top, low).astype(BF16)


def low_high(axis, near, far):
    index, size = lax.axis_index(axis), lax.axis_size(axis)
    near, far = near.astype(F32), far.astype(F32)
    flag = even(axis)
    outermost = jnp.logical_or(index == 0, index == size - 1)
    far = jnp.where(outermost, 0.0, far)
    return jnp.where(flag, far, near), jnp.where(flag, near, far)


def strip_kernel(own_ref, fl_ref, ra_ref, rb_ref, sc_ref, sd_ref, wide_ref):
    planes, cols, _ = own_ref.shape
    quads = planes // 2
    rows = quads * QUAD
    c_even = even("col")
    for kind in range(2):
        for q in range(quads + 4):
            left = halo_plane(kind, q, own_ref, ra_ref, rb_ref, slice(0, KEYS))[:HALO]
            right = halo_plane(kind, q, own_ref, ra_ref, rb_ref, slice(cols - KEYS, cols))[HALO:]
            row = (kind * (quads + 4) + q) * HALO
            wide_ref[0, row : row + HALO] = jnp.where(c_even, right, left)
            wide_ref[1, row : row + HALO] = jnp.where(c_even, left, right)
    count = 2 * (quads + 4) * HALO
    sc_ref[:count] = wide_ref[0].astype(BF16)
    sd_ref[:count] = wide_ref[1].astype(BF16)
    up, down = flow_up_down(ra_ref, rb_ref)
    own = fl_ref[...].astype(F32)
    left = right = jnp.zeros((rows + 2 * HALO, cols), F32)
    lane = lax.broadcasted_iota(jnp.int32, left.shape, 1)
    for v in range(4):
        flow = jnp.concatenate(
            [
                up[v * HALO : (v + 1) * HALO],
                own[v * rows : (v + 1) * rows],
                down[v * HALO : (v + 1) * HALO],
            ],
            axis=0,
        )
        here = lane // RADIUS == v
        left = jnp.where(here, roll(flow, v * RADIUS), left)
        right = jnp.where(here, roll(flow, (v + 1) * RADIUS), right)
    sc_ref[count:] = jnp.where(c_even, right, left).astype(BF16)
    sd_ref[count:] = jnp.where(c_even, left, right).astype(BF16)


def fill_taps(dst_ref, w_ref):
    zero = jnp.zeros((CH, CH), F32)
    for dx in range(3):
        for block in range(2 * QUAD):
            row = block if block < QUAD else {QUAD: QUAD, 2 * QUAD - 1: -1}.get(block)
            parts = []
            for out in range(QUAD):
                tap = None if row is None else row - out + 1
                ok = tap is not None and 0 <= tap < 3
                parts.append(w_ref[tap, dx].astype(F32) if ok else zero)
            dst_ref[dx, block * CH : (block + 1) * CH, :] = jnp.concatenate(parts, axis=1).astype(
                BF16
            )


def taps_of(ref, quad, start, count):
    main = ref[quad, pl.ds(start, count), :]
    after = ref[quad + 1, pl.ds(start, count), :]
    before = ref[quad - 1, pl.ds(start, count), :]
    lane = lax.broadcasted_iota(jnp.int32, main.shape, 1)
    beside = jnp.where(lane < 2 * CH, after, before)
    return jnp.concatenate([main, beside], axis=1).astype(BF16)


def conv(ref, quad, start, count, w_ref):
    total = jnp.zeros((count, LANES), F32)
    for dx in range(3):
        total += jnp.dot(
            taps_of(ref, quad, start + dx - 1, count), w_ref[dx], preferred_element_type=F32
        )
    return total


SPAN = 3 * QUAD
KEYS = 16
WIDE = 2


def halo_plane(kind, q, own_ref, ra_ref, rb_ref, part=None):
    planes, cols, _ = own_ref.shape
    quads = planes // 2
    part = part or slice(0, cols)
    if 2 <= q < quads + 2:
        return own_ref[kind * quads + q - 2, part].astype(F32)
    down = q >= quads + 2
    if kind == 1 and q in (0, quads + 3):
        row, count = (0 if down else QUAD - 1), cols // QUAD
        at = 3 * cols
        packed = low_high("row", ra_ref[at : at + count], rb_ref[at : at + count])[down]
        parts = []
        for b in range(part.start // count, (part.stop - 1) // count + 1):
            first, last = max(part.start - b * count, 0), min(part.stop - b * count, count)
            parts.append(roll_groups(packed, row - b)[first:last])
        return jnp.concatenate(parts, axis=0)
    at = 2 * cols if kind == 1 else (q - quads - 2 if down else q) * cols
    part = slice(at + part.start, at + part.stop)
    return low_high("row", ra_ref[part], rb_ref[part])[down]


def edge_plane(kind, q, side, own_ref, ra_ref, rb_ref, rc_ref, rd_ref):
    planes, cols, _ = own_ref.shape
    quads = planes // 2
    tile = slice(0, KEYS) if side == 0 else slice(cols - KEYS, cols)
    mine = halo_plane(kind, q, own_ref, ra_ref, rb_ref, tile)
    index = kind * (quads + 4) + q
    at = index // 2 * 2 * HALO
    fetched = low_high("col", rc_ref[at : at + 2 * HALO], rd_ref[at : at + 2 * HALO])[side]
    fetched = fetched[index % 2 * HALO : index % 2 * HALO + HALO]
    parts = [fetched, mine[:HALO]] if side == 0 else [mine[HALO:], fetched]
    return jnp.concatenate(parts, axis=0)


def flow_up_down(ra_ref, rb_ref):
    at = ra_ref.shape[0] - 4 * HALO
    return low_high("row", ra_ref[at:], rb_ref[at:])


def flow_part(f, ref_or_value, rows):
    parts = [ref_or_value[v * rows : (v + 1) * rows].astype(F32) for v in (2 * f, 2 * f + 1)]
    return parts[0] + parts[1]


def flow_mid(f, fl_ref, ra_ref, rb_ref):
    up, down = flow_up_down(ra_ref, rb_ref)
    return jnp.concatenate(
        [
            flow_part(f, up, HALO),
            flow_part(f, fl_ref, fl_ref.shape[0] // 4),
            flow_part(f, down, HALO),
        ],
        axis=0,
    )


def flow_inner(p_ref, values):
    groups = p_ref.shape[1]
    for f in range(2):
        mid = pltpu.roll(values[f], LANES - RADIUS, 1)
        lane = lax.broadcasted_iota(jnp.int32, mid.shape, 1)
        row = lax.broadcasted_iota(jnp.int32, mid.shape, 0)
        mid = jnp.where(lane < LANES - 8, mid, 0.0)
        turned = [roll_groups(mid, k) for k in range(QUAD)]
        for g in range(groups):
            total = jnp.zeros(mid.shape, F32)
            for i in range(QUAD):
                keep = jnp.logical_and(row % QUAD == i, lane // CH == i)
                total = jnp.where(keep, turned[(i - g) % QUAD], total)
            p_ref[f, g] = total


def flow_edge(e_ref, fl_ref, ra_ref, rb_ref, rc_ref, rd_ref):
    rows = fl_ref.shape[0] // 4
    ext = rows + 2 * HALO
    base = rc_ref.shape[0] - ext
    left, right = low_high("col", rc_ref[base:], rd_ref[base:])
    for f in range(2):
        mid = flow_mid(f, fl_ref, ra_ref, rb_ref)
        at = 2 * f * RADIUS
        lf = roll(left, -at) + roll(left, -at - RADIUS)
        rt = roll(right, 3 * RADIUS - at) + roll(right, 2 * RADIUS - at)
        lane = lax.broadcasted_iota(jnp.int32, mid.shape, 1)
        row = lax.broadcasted_iota(jnp.int32, mid.shape, 0)
        low = jnp.where(lane < RADIUS, lf, roll(mid, RADIUS))
        high = jnp.where(
            lane < 3 * RADIUS, roll(mid, 3 * RADIUS), rt
        )
        both = jnp.where(lane < 8, low, high)
        for h in range(2):
            total = jnp.zeros(mid.shape, F32)
            for i in range(QUAD):
                turn = i * CH + h * 16
                keep = jnp.logical_and(row % QUAD == i, lane // 16 == 2 * i + h)
                total = jnp.where(keep, pltpu.roll(both, turn, 1) if turn else both, total)
            e_ref[f, h] = total


def fill_mask(m_ref):
    key = lax.broadcasted_iota(jnp.int32, (SPAN, KEYS, LANES), 0)
    kx = lax.broadcasted_iota(jnp.int32, (SPAN, KEYS, LANES), 1)
    lane = lax.broadcasted_iota(jnp.int32, (SPAN, KEYS, LANES), 2)
    dy = key - lane // CH
    dx = kx - lane % 8
    ok = (dy >= 0) & (dy <= 2 * RADIUS) & (dx >= 0) & (dx <= 2 * RADIUS)
    m_ref[...] = jnp.where(ok, 1.0, 0.0)


def softmax_block(score_of, m_ref, f0, f1, scale):
    shape = (KEYS, f0.shape[1])
    lane = lax.broadcasted_iota(jnp.int32, shape, 1) % LANES
    at_y = (lane // CH + RADIUS).astype(F32)
    at_x = (lane % 8 + RADIUS).astype(F32)
    key_x = lax.broadcasted_iota(jnp.int32, shape, 0).astype(F32)
    f0 = jnp.broadcast_to(f0, shape)
    f1 = jnp.broadcast_to(f1, shape)
    side = f1 * (key_x - at_x) - f0 * at_y
    weights = []
    total = jnp.zeros(shape, F32)
    lean = jnp.zeros(shape, F32)
    for y in range(SPAN):
        mask = jnp.concatenate([m_ref[y]] * (shape[1] // LANES), axis=1)
        weight = jnp.exp2(score_of(y) * (scale * math.log2(math.e))) * mask
        weights.append(weight)
        total = total + weight
        lean = lean + weight * (f0 * float(y) + side)
    total = jnp.sum(total, axis=0, keepdims=True)
    lean = jnp.sum(lean, axis=0, keepdims=True)
    base = jnp.broadcast_to(lean / total, shape)
    factor = jnp.broadcast_to(scale / total, shape)
    step = f0 * factor
    side = (side - base) * factor
    return jnp.concatenate(
        [(weights[y] * (step * float(y) + side)).astype(BF16) for y in range(SPAN)], axis=0
    )


def unit_of(field, ones):
    recip = lax.rsqrt(group_sum(field * field, ones) * (1.0 / CH) + 1.0)
    return recip, (field * recip).astype(BF16).astype(F32)


def unit_grad(field, recip, grad, ones):
    inner = group_sum(grad * field, ones)
    return recip * grad - field * (recip * recip * recip) * inner * (1.0 / CH)


def key_rows(t4_ref, first, unit):
    turned = [roll_groups(unit, k) for k in range(QUAD)]
    for i in range(QUAD):
        for g in range(t4_ref.shape[0]):
            t4_ref[g, first + i] = by_group(
                [
                    turned[(j - i) % QUAD][g * GROUP + 8 * j : g * GROUP + 8 * j + KEYS]
                    for j in range(QUAD)
                ]
            ).astype(BF16)


def query_block(octs):
    group = lane_group((8, LANES))
    turned = [
        roll_groups(by_group([octs[(i + k) % QUAD] for i in range(QUAD)]), k)
        for k in range(QUAD)
    ]
    parts = [
        jnp.where(group == j, turned[(j - i) % QUAD], 0.0)
        for i in range(QUAD)
        for j in range(QUAD)
    ]
    return jnp.concatenate(parts, axis=0).astype(BF16)


def packed_rows(mine):
    def piece(i, j):
        at = i * GROUP + 8 * j
        return mine[at : at + 8]

    turned = [
        roll_groups(by_group([piece((j + k) % QUAD, j) for j in range(QUAD)]), k)
        for k in range(QUAD)
    ]
    return [by_group([turned[(i - j) % QUAD] for i in range(QUAD)]) for j in range(QUAD)]


def run_blocks(blocks, m_ref, sc_ref, d_ref, scale, wide=1):
    steps = [blocks[at : at + wide] for at in range(0, len(blocks), wide)]

    def lanes(index):
        return slice(index * LANES, (index + 1) * LANES)

    def score(b):
        for index, block in enumerate(steps[b]):
            sc_ref[b % 2, :, lanes(index)] = lax.dot_general(
                block[0](), block[1](), (((1,), (1,)), ((), ())), preferred_element_type=F32
            )

    def weigh(b):
        used = slice(0, len(steps[b]) * LANES)
        flows = [block[2]() for block in steps[b]]
        f0, f1 = (jnp.concatenate([x[f] for x in flows], axis=1) for f in range(2))
        d_ref[b % 2, :, used] = softmax_block(
            lambda y: sc_ref[b % 2, KEYS * y : KEYS * (y + 1), used], m_ref, f0, f1, scale
        )

    def collect(b):
        for index, block in enumerate(steps[b]):
            dscore = d_ref[b % 2, :, lanes(index)]
            keys, queries, _, wanted, put_keys, put_rows = block
            put_keys(jnp.dot(dscore[wanted], queries(), preferred_element_type=F32))
            mine = lax.dot_general(
                dscore, keys(), (((0,), (0,)), ((), ())), preferred_element_type=F32
            )
            put_rows(packed_rows(mine))

    score(0)
    for b in range(len(steps)):
        if b + 1 < len(steps):
            score(b + 1)
        weigh(b)
        if b > 0:
            collect(b - 1)
    collect(len(steps) - 1)


def conv_from(tap_list, w_ref):
    total = None
    for dx in range(3):
        term = jnp.dot(tap_list[dx], w_ref[dx], preferred_element_type=F32)
        total = term if total is None else total + term
    return total


def inner_block(n, g, keys, q_ref, p_ref, p_quad, ga_ref, gu_ref):
    rows = slice(p_quad * QUAD, (p_quad + 1) * QUAD)
    own = ga_ref.shape[1]
    first = n * QUAD - HALO
    low, high = max(first, 0), min(first + SPAN, own)
    wanted = slice((low - first) * KEYS, (high - first) * KEYS)

    def put_keys(value):
        ga_ref[g, low:high] = ga_ref[g, low:high] + value.reshape(high - low, KEYS, LANES)

    def put_rows(octs):
        for j in range(QUAD):
            gu_ref[n, g * GROUP + 8 * j : g * GROUP + 8 * j + 8] = octs[j]

    return (
        lambda: keys(n, g),
        lambda: q_ref[n, g],
        lambda: [jnp.sum(p_ref[f, g, rows, :], axis=0, keepdims=True) for f in range(2)],
        wanted,
        put_keys,
        put_rows,
    )


def inner_queries(n, es_ref, taps_ref, fe_ref, rf_ref, q_ref, ones, keep=None):
    cols = fe_ref.shape[1]
    tap_list = [taps_of(es_ref, n + 1, RADIUS + dx - 1, cols) for dx in range(3)]
    if keep is not None:
        for dx in range(3):
            keep[n, dx] = tap_list[dx]
    feat = conv_from(tap_list, taps_ref).astype(BF16).astype(F32)
    fe_ref[n] = feat
    recip, unit = unit_of(feat, ones)
    rf_ref[n] = recip
    for g in range(cols // GROUP):
        q_ref[n, g] = query_block(
            [unit[g * GROUP + 8 * j : g * GROUP + 8 * j + 8] for j in range(QUAD)]
        )


def fill_plane(dst_ref, q, value):
    cols = value.shape[0]
    dst_ref[q, :cols] = value
    dst_ref[q, cols:] = jnp.zeros((dst_ref.shape[1] - cols, LANES), F32)


def own_rows(
    quads_of, keys, es_ref, taps_ref, m_ref, p_ref, ga_ref, gf_out, gw_out,
    q_ref, fe_ref, rf_ref, gu_ref, tap_ref, sc_ref, d_ref, ones,
):
    cols = fe_ref.shape[1]
    for n in quads_of:
        inner_queries(n, es_ref, taps_ref, fe_ref, rf_ref, q_ref, ones, tap_ref)
    run_blocks(
        [
            inner_block(n, g, keys, q_ref, p_ref, n - 1, ga_ref, gu_ref)
            for n in quads_of
            for g in range(cols // GROUP)
        ],
        m_ref, sc_ref, d_ref, SHARPNESS / math.sqrt(CH), WIDE,
    )
    row = lax.broadcasted_iota(jnp.int32, (cols, LANES), 0)
    values = []
    for index, n in enumerate(quads_of):
        value = unit_grad(fe_ref[n], rf_ref[n], gu_ref[n], ones)
        value = jnp.where(row < cols - 8, value, 0.0).astype(BF16)
        gf_out[index] = value
        values.append(value)
    value = jnp.concatenate(values, axis=0)
    for dx in range(3):
        others = jnp.concatenate([tap_ref[n, dx] for n in quads_of], axis=0)
        gw_out[dx] = gw_out[dx] + lax.dot_general(
            value, others, (((0,), (0,)), ((), ())), preferred_element_type=F32
        )


def early_kernel(
    own_ref, fl_ref, w_ref, wt_ref,
    t4_out, taps_out, back_out, m_out, p_out, ga_out, gf_out, gw_out,
    es_ref, q_ref, fe_ref, rf_ref, gu_ref, tap_ref, sc_ref, d_ref,
):
    planes, cols, _ = own_ref.shape
    quads = planes // 2
    width = es_ref.shape[1]
    ones = group_ones()
    fill_taps(taps_out, w_ref)
    fill_taps(back_out, wt_ref)
    fill_mask(m_out)
    flow_inner(p_out, [flow_part(f, fl_ref, quads * QUAD) for f in range(2)])
    for q in range(quads):
        fill_plane(es_ref, q + 2, own_ref[quads + q].astype(F32))
        _, unit = unit_of(own_ref[q].astype(F32), ones)
        pad = jnp.zeros((width - cols, LANES), F32)
        key_rows(t4_out, q * QUAD, jnp.concatenate([unit, pad], axis=0))
    ga_out[...] = jnp.zeros_like(ga_out)
    gw_out[...] = jnp.zeros_like(gw_out)

    def keys(n, g):
        at = (n - 2) * QUAD
        return t4_out[g, at : at + SPAN].reshape(SPAN * KEYS, LANES)

    own_rows(
        range(2, quads), keys, es_ref, taps_out, m_out, p_out, ga_out, gf_out, gw_out,
        q_ref, fe_ref, rf_ref, gu_ref, tap_ref, sc_ref, d_ref, ones,
    )


def middle_kernel(
    own_ref, ra_ref, rb_ref, t4_ref, taps_ref, m_ref, p_ref, ga_in, gw_in,
    t4_out, ga_out, gf_out, gw_out,
    es_ref, q_ref, fe_ref, rf_ref, gu_ref, tap_ref, sc_ref, d_ref,
):
    planes, cols, _ = own_ref.shape
    quads = planes // 2
    width = es_ref.shape[1]
    ones = group_ones()
    for q in (1, 2, 3, quads, quads + 1, quads + 2):
        fill_plane(es_ref, q, halo_plane(1, q, own_ref, ra_ref, rb_ref))
    pad = jnp.zeros((width - cols, LANES), F32)
    for k, q in enumerate((1, quads + 2)):
        _, unit = unit_of(halo_plane(0, q, own_ref, ra_ref, rb_ref), ones)
        key_rows(t4_out, k * QUAD, jnp.concatenate([unit, pad], axis=0))

    def keys(n, g):
        if n == 1:
            parts = [t4_out[g, :QUAD], t4_ref[g, : 2 * QUAD]]
        else:
            parts = [t4_ref[g, (quads - 2) * QUAD :], t4_out[g, QUAD:]]
        return jnp.concatenate(parts, axis=0).reshape(SPAN * KEYS, LANES)

    own_rows(
        (1, quads), keys, es_ref, taps_ref, m_ref, p_ref, ga_out, gf_out, gw_out,
        q_ref, fe_ref, rf_ref, gu_ref, tap_ref, sc_ref, d_ref, ones,
    )


def edge_blocks(
    pairs, first, ee_ref, tu_ref, taps_ref, t4_ref, q_ref, ep_ref, ga_ref, ones, keep=None
):
    blocks, results = [], []
    slots = [(pair[j // 2], j % 2) for pair in pairs for j in range(QUAD)]
    tap_list = [
        jnp.concatenate(
            [taps_of(ee_ref.at[side], n + 1, RADIUS + dx - 1, 8).astype(F32) for n, side in slots],
            axis=0,
        ).astype(BF16)
        for dx in range(3)
    ]
    feat = conv_from(tap_list, taps_ref).astype(BF16).astype(F32)
    recip, unit = unit_of(feat, ones)
    for e, pair in enumerate(pairs):
        quad_of = [pair[j // 2] for j in range(QUAD)]
        at = e * GROUP
        q_ref[e] = query_block([unit[at + 8 * j : at + 8 * j + 8] for j in range(QUAD)])
        for y in range(SPAN):
            t4_ref[e, y] = by_group(
                [
                    tu_ref[(j - y) % QUAD, j % 2, quad_of[j] + y // QUAD]
                    for j in range(QUAD)
                ]
            ).astype(BF16)
        results.append([])

        def flows(pair=pair):
            total = []
            for f in range(2):
                parts = [
                    jnp.sum(
                        ep_ref[f, h, (pair[h] + 1) * QUAD : (pair[h] + 2) * QUAD, :],
                        axis=0,
                        keepdims=True,
                    )
                    for h in range(2)
                ]
                total.append(parts[0] + parts[1])
            return total

        def put_keys(value, e=e):
            ga_ref[first + e] = value.reshape(SPAN, KEYS, LANES)

        blocks.append(
            (
                lambda e=e: t4_ref[e].reshape(SPAN * KEYS, LANES),
                lambda e=e: q_ref[e],
                flows,
                slice(0, SPAN * KEYS),
                put_keys,
                results[-1].extend,
            )
        )
    return blocks, (tap_list, feat, recip, results)


def edge_planes(ee_ref, tu_ref, ones, quads_of, keys_of, refs):
    for side in range(2):
        for q in quads_of:
            ee_ref[side, q] = edge_plane(1, q, side, *refs)
        raw = jnp.concatenate([edge_plane(0, q, side, *refs) for q in keys_of], axis=0)
        _, unit = unit_of(raw, ones)
        for k in range(QUAD):
            turned = roll_groups(unit, k)
            for index, q in enumerate(keys_of):
                tu_ref[k, side, q] = turned[index * KEYS : (index + 1) * KEYS]


def edge_grads(stores, ones):
    _, feat, recip, results = stores
    grad = jnp.concatenate([x for result in results for x in result], axis=0)
    return unit_grad(feat, recip, grad, ones).astype(BF16)


def pairs_of(quads):
    return [(n, n + 1) for n in range(1, quads + 1, 2)]


def edge_kernel(
    own_ref, fl_ref, ra_ref, rb_ref, rc_ref, rd_ref, taps_ref, m_ref, gw_ref,
    ga_ref, gf_out, gw_out,
    ee_ref, tu_ref, t4_ref, q_ref, ep_ref, sc_ref, d_ref,
):
    planes, cols, _ = own_ref.shape
    quads = planes // 2
    ext = quads + 4
    scale = SHARPNESS / math.sqrt(CH)
    ones = group_ones()
    refs = (own_ref, ra_ref, rb_ref, rc_ref, rd_ref)
    edge_planes(ee_ref, tu_ref, ones, range(1, ext - 1), range(1, ext - 1), refs)
    flow_edge(ep_ref, fl_ref, ra_ref, rb_ref, rc_ref, rd_ref)
    blocks, stores = edge_blocks(
        pairs_of(quads), 0, ee_ref, tu_ref, taps_ref, t4_ref, q_ref, ep_ref, ga_ref, ones
    )
    run_blocks(blocks, m_ref, sc_ref, d_ref, scale, WIDE)
    grad = edge_grads(stores, ones)
    for e in range(gf_out.shape[0]):
        gf_out[e] = grad[e * GROUP : (e + 1) * GROUP]
    row = lax.broadcasted_iota(jnp.int32, grad.shape, 0)
    inside = jnp.logical_xor(row // 8 % 2 == 0, row % 8 < RADIUS)
    grad = jnp.where(inside, grad.astype(F32), 0.0).astype(BF16)
    totals = [
        gw_ref[dx]
        + lax.dot_general(
            grad, stores[0][dx], (((0,), (0,)), ((), ())), preferred_element_type=F32
        )
        for dx in range(3)
    ]
    lane = lax.broadcasted_iota(jnp.int32, (CH, LANES), 1)
    for dx, total in enumerate(totals):
        rows_of = [total[i * CH : (i + 1) * CH] for i in range(QUAD)]
        main = [x[:, :LANES] for x in rows_of]
        beside = [x[:, LANES:] for x in rows_of]
        start = jnp.where(lane < CH, roll_groups(beside[0], 1), roll_groups(main[0], 1))
        last = jnp.where(lane < 2 * CH, roll_groups(main[3], 2), roll_groups(beside[3], 2))
        totals[dx] = (start + main[1]) + (roll_groups(main[2], 3) + last)
    for dx in range(2):
        gw_out[dx * CH : (dx + 1) * CH] = jnp.where(
            lane < 3 * CH, totals[dx], roll_groups(totals[2], 3 - dx)
        )
    gw_out[2 * CH :] = one_row(totals[2], 2)


def spread(dst_ref, quad, value, channels, rows):
    flipped = value.T
    for i in range(QUAD):
        dst_ref[pl.ds(quad * QUAD + i, channels, stride=rows), :] = flipped[
            i * CH : (i + 1) * CH
        ]


def outer_kernel(
    lower, own_ref, ra_ref, rb_ref, taps_ref, m_ref, t4_own, t4_halo, ga_in,
    ga_out, gf_out,
    es_ref, t4_ref, q_ref, fe_ref, rf_ref, gu_ref, p_ref, sc_ref, d_ref,
):
    planes, cols, _ = own_ref.shape
    quads = planes // 2
    width = es_ref.shape[1]
    ones = group_ones()
    n = quads + 1 if lower else 0
    for q in (n, n + 1, n + 2):
        fill_plane(es_ref, q, halo_plane(1, q, own_ref, ra_ref, rb_ref))
    flow_inner(
        p_ref, [flow_part(f, flow_up_down(ra_ref, rb_ref)[lower], HALO) for f in range(2)]
    )
    _, unit = unit_of(halo_plane(0, quads + 3 if lower else 0, own_ref, ra_ref, rb_ref), ones)
    pad = jnp.zeros((width - cols, LANES), F32)
    key_rows(t4_ref, 0, jnp.concatenate([unit, pad], axis=0))

    def keys(n, g):
        if lower:
            parts = [t4_own[g, (quads - 1) * QUAD :], t4_halo[g, QUAD:], t4_ref[g]]
        else:
            parts = [t4_ref[g], t4_halo[g, :QUAD], t4_own[g, :QUAD]]
        return jnp.concatenate(parts, axis=0).reshape(SPAN * KEYS, LANES)

    inner_queries(n, es_ref, taps_ref, fe_ref, rf_ref, q_ref, ones)
    run_blocks(
        [
            inner_block(n, g, keys, q_ref, p_ref, 0 if lower else 1, ga_out, gu_ref)
            for g in range(cols // GROUP)
        ],
        m_ref, sc_ref, d_ref, SHARPNESS / math.sqrt(CH),
    )
    gf_out[...] = unit_grad(fe_ref[n], rf_ref[n], gu_ref[n], ones).astype(BF16)


def corner_kernel(
    own_ref, fl_ref, ra_ref, rb_ref, rc_ref, rd_ref, taps_ref, m_ref,
    ge_out, gf_out,
    ee_ref, tu_ref, t4_ref, q_ref, ep_ref, sc_ref, d_ref,
):
    quads = own_ref.shape[0] // 2
    ext = quads + 4
    ones = group_ones()
    refs = (own_ref, ra_ref, rb_ref, rc_ref, rd_ref)
    near = (0, 1, 2, ext - 3, ext - 2, ext - 1)
    edge_planes(ee_ref, tu_ref, ones, near, near, refs)
    flow_edge(ep_ref, fl_ref, ra_ref, rb_ref, rc_ref, rd_ref)
    blocks, stores = edge_blocks(
        [(0, quads + 1)], 0, ee_ref, tu_ref, taps_ref, t4_ref, q_ref, ep_ref, ge_out, ones
    )
    run_blocks(blocks, m_ref, sc_ref, d_ref, SHARPNESS / math.sqrt(CH))
    gf_out[...] = edge_grads(stores, ones)


def image_kernel(
    own_ref, back_ref, ga_ref, gem_ref, gec_ref,
    gf_early, gf_middle, gf_top, gf_low, gfe_ref, gfc_ref,
    gs_out, gt_out,
    full_ref, wide_ref,
):
    channels, rows, cols = gs_out.shape
    quads = rows // QUAD
    ones = group_ones()
    rows_of = {0: gf_top[...], quads + 1: gf_low[...], 1: gf_middle[0], quads: gf_middle[1]}
    for n in range(2, quads):
        rows_of[n] = gf_early[n - 2]
    for n, value in rows_of.items():
        full_ref[n, 8 : 8 + cols] = value.astype(F32)
    edges = [gfe_ref[e] for e in range(quads // 2)] + [gfc_ref[...]]
    where_is = {}
    for e, (pair, grad) in enumerate(zip(pairs_of(quads) + [(0, quads + 1)], edges)):
        grad = grad.astype(F32)
        for j in range(QUAD):
            at = 0 if j % 2 == 0 else cols
            full_ref[pair[j // 2], at : at + 8] = grad[8 * j : 8 * j + 8]
            where_is[pair[j // 2], j % 2] = (e, j)

    for q in range(quads):
        tap_list = [taps_of(full_ref, q + 1, RADIUS + dx - 1, cols) for dx in range(3)]
        spread(wide_ref, q, conv_from(tap_list, back_ref), channels, rows)
    gs_out[...] = wide_ref[...].astype(BF16).reshape(channels, rows, cols)

    group = lane_group((8, LANES))
    last = cols // 8
    for q in range(quads):
        parts = []
        for oct in range(1, last + 1):
            total = None
            for k in range(QUAD):
                both = jnp.zeros((8, LANES), F32)
                for half, which in ((0, oct), (1, oct - 1)):
                    if not 0 < which < last:
                        continue
                    g, j = divmod(which - 1, QUAD)
                    at = q * QUAD + (j + k) % QUAD
                    both = jnp.where(group == j, ga_ref[g, at, 8 * half : 8 * half + 8], both)
                both = roll_groups(both, k)
                total = both if total is None else total + both
            side = 0 if oct == 1 else 1 if oct == last else None
            if side is not None:
                half = 1 - side
                for n in range(q, q + 3):
                    e, j = where_is[n, side]
                    ref = gem_ref.at[e] if e < quads // 2 else gec_ref.at[0]
                    for i in range(QUAD):
                        part = ref[(q + 2 - n) * QUAD + i, 8 * half : 8 * half + 8]
                        total = total + roll_groups(jnp.where(group == j, part, 0.0), i - j)
            parts.append(total)
        grad = jnp.concatenate(parts, axis=0)
        field = own_ref[q].astype(F32)
        recip = lax.rsqrt(group_sum(field * field, ones) * (1.0 / CH) + 1.0)
        spread(wide_ref, q, unit_grad(field, recip, grad, ones), channels, rows)
    gt_out[...] = wide_ref[...].astype(BF16).reshape(channels, rows, cols)


def final_kernel(scale, one_ref, two_ref, out_ref):
    total = (one_ref[...].astype(F32) + two_ref[...].astype(F32)) * scale
    first, second, rest = total[:CH], total[CH : 2 * CH], total[2 * CH :]
    rest = jnp.concatenate([roll_groups(rest, 2 - b) for b in range(QUAD)], axis=0)
    third = by_group([roll_groups(first, 1), roll_groups(second, 2), rest, rest])
    for dx, value in enumerate((first, second, third)):
        value = value.T
        for tap in range(3):
            out_ref[tap, dx] = value[tap * CH : (tap + 1) * CH]


def pair_exchange(x, y, axis):
    rows, cols = lax.axis_size("row"), lax.axis_size("col")
    near, far = [], []
    for r in range(rows):
        for c in range(cols):
            index, size = (r, rows) if axis == "row" else (c, cols)
            other = index + 1 if index % 2 else index - 1
            for pairs, to in ((near, index ^ 1), (far, other)):
                if 0 <= to < size:
                    target = (to, c) if axis == "row" else (r, to)
                else:
                    target = (r, c ^ 1) if axis == "row" else (r ^ 1, c)
                pairs.append((r * cols + c, target[0] * cols + target[1]))
    both = ("row", "col")
    return lax.ppermute(x, both, near), lax.ppermute(y, both, far)


def swap(x, flips):
    rows, cols = lax.axis_size("row"), lax.axis_size("col")
    flip_r, flip_c = flips.get("row", 0), flips.get("col", 0)
    pairs = [
        (r * cols + c, (r ^ flip_r) * cols + (c ^ flip_c)) for r in range(rows) for c in range(cols)
    ]
    return lax.ppermute(x, ("row", "col"), pairs)


def after(value, *others):
    return lax.optimization_barrier((value, *others))[0]


def vmem(count):
    return [pl.BlockSpec(memory_space=pltpu.VMEM)] * count


def per_device(source, target, conv_weight, flow_cotangent):
    channels, rows, cols = source.shape
    quads = rows // QUAD
    ext = quads + 4
    groups = cols // GROUP
    width = cols + HALO
    asked = quads + 2
    flipped = jnp.transpose(conv_weight[::-1, ::-1], (0, 1, 3, 2))
    shape = jax.ShapeDtypeStruct

    def scratch(*dims, dtype=F32):
        return pltpu.VMEM(dims, dtype)

    def call(kernel, name, outs, scratches, *args, cycles=1000, alias=None, specs=None):
        return pl.pallas_call(
            kernel,
            out_shape=tuple(outs),
            in_specs=specs or vmem(len(args)),
            out_specs=tuple(vmem(len(outs))),
            scratch_shapes=scratches,
            input_output_aliases=alias or {},
            cost_estimate=pl.CostEstimate(
                flops=cycles * 250_000, bytes_accessed=cycles * 1000, transcendentals=0
            ),
            compiler_params=pltpu.CompilerParams(vmem_limit_bytes=16 << 20),
            name=name,
        )(*args)

    side = shape((3 * cols + cols // QUAD + 4 * HALO, LANES), BF16)
    own, flow, to_a, to_b = call(
        pack_kernel,
        "pack",
        [shape((2 * quads, cols, LANES), BF16), shape((4 * rows, cols), BF16), side, side],
        [
            scratch(channels * rows, cols),
            scratch(*source.shape, dtype=BF16),
            scratch(*target.shape, dtype=BF16),
            scratch(*flow_cotangent.shape),
            pltpu.SemaphoreType.DMA((3,)),
        ],
        *(
            pltpu.with_memory_space_constraint(x, pltpu.HBM)
            for x in (source, target, flow_cotangent)
        ),
        specs=[pl.BlockSpec(memory_space=pltpu.HBM)] * 3,
    )
    ra, rb = pair_exchange(to_a, to_b, "row")
    taps = shape((3, 2 * LANES, LANES), BF16)
    stages = [
        scratch(2, SPAN * KEYS, WIDE * LANES),
        scratch(2, SPAN * KEYS, WIDE * LANES, dtype=BF16),
    ]
    inner = [
        scratch(asked, groups, LANES, LANES, dtype=BF16),
        scratch(asked, cols, LANES),
        scratch(asked, cols, LANES),
        scratch(asked, cols, LANES),
    ]
    planes = scratch(ext, width, LANES)
    tap_lists = scratch(asked, 3, cols, 2 * LANES, dtype=BF16)
    for_keys = shape((groups, rows, KEYS, LANES), F32)
    for_kernel = shape((3, LANES, 2 * LANES), F32)
    for_feat = shape((2, cols, LANES), BF16)
    keys, forward, back, mask, cotangents, grad_keys, feat_early, terms = call(
        early_kernel,
        "early",
        [
            shape((groups, rows, KEYS, LANES), BF16),
            taps,
            taps,
            shape((SPAN, KEYS, LANES), F32),
            shape((2, groups, rows, LANES), F32),
            for_keys,
            shape((quads - 2, cols, LANES), BF16),
            for_kernel,
        ],
        [planes] + inner + [tap_lists] + stages,
        own,
        flow,
        conv_weight,
        flipped,
        cycles=3000,
    )
    strip = shape((2 * ext * HALO + ext * QUAD, LANES), BF16)
    to_c, to_d = call(
        strip_kernel,
        "strip",
        [strip, strip],
        [scratch(2, 2 * ext * HALO, LANES)],
        own,
        flow,
        ra,
        rb,
    )
    rc, rd = pair_exchange(to_c, to_d, "col")
    halo_keys, grad_keys, feat_middle, terms = call(
        middle_kernel,
        "middle",
        [shape((groups, 2 * QUAD, KEYS, LANES), BF16), for_keys, for_feat, for_kernel],
        [planes] + inner + [tap_lists] + stages,
        own,
        ra,
        rb,
        keys,
        forward,
        mask,
        cotangents,
        grad_keys,
        terms,
        cycles=3000,
        alias={7: 1, 8: 3},
    )
    pairs = quads // 2
    outer = [scratch(2, ext, KEYS, LANES), scratch(QUAD, 2, ext, KEYS, LANES)]
    fetched = (own, flow, ra, rb, rc, rd, forward, mask)

    def edge_scratch(count):
        return outer + [
            scratch(count, SPAN, KEYS, LANES, dtype=BF16),
            scratch(count, LANES, LANES, dtype=BF16),
            scratch(2, 2, ext * QUAD, LANES),
        ] + stages

    edge_keys, edge_feat, terms = call(
        edge_kernel,
        "edge",
        [
            shape((pairs, SPAN, KEYS, LANES), F32),
            shape((pairs, GROUP, LANES), BF16),
            shape((2 * CH + CH // QUAD, LANES), F32),
        ],
        edge_scratch(pairs),
        *fetched,
        terms,
    )

    def outer_rows(lower, sums):
        return call(
            functools.partial(outer_kernel, lower),
            "lower" if lower else "upper",
            [for_keys, shape((cols, LANES), BF16)],
            [planes, scratch(groups, QUAD, KEYS, LANES, dtype=BF16)]
            + inner
            + [scratch(2, groups, HALO, LANES)]
            + stages,
            after(own, sums),
            ra,
            rb,
            forward,
            mask,
            keys,
            halo_keys,
            grad_keys,
            alias={7: 0},
            cycles=1500,
        )

    bits = {axis: [] for axis in ("row", "col")}
    for axis, found in bits.items():
        step = 1
        while step < lax.axis_size(axis):
            found.append({axis: step})
            step *= 2
    steps = [[bits["row"][0]]]
    down, along = bits["row"][1:], bits["col"]
    while down or along:
        if True and down and along and len(down) + len(along) > 2:
            one, two = down.pop(0), along.pop(0)
            steps.append([one, two, {**one, **two}])
        else:
            steps.append([(down or along).pop(0)])

    def exchange(value, step):
        value = value.astype(BF16) if step is not steps[0] else value
        return [value] + [swap(value, flips) for flips in step]

    def total_of(parts):
        parts = [x.astype(F32) for x in parts]
        return parts[0] + parts[1] if len(parts) == 2 else (parts[0] + parts[1]) + (parts[2] + parts[3])

    for index, step in enumerate(steps[:-1]):
        parts = exchange(terms, step)
        done = ()
        if index == 0:
            corner_keys, corner_feat = call(
                corner_kernel,
                "corner",
                [shape((1, SPAN, KEYS, LANES), F32), shape((GROUP, LANES), BF16)],
                edge_scratch(1),
                after(own, terms),
                *fetched[1:],
            )
            done = (corner_feat,)
        if index == len(steps) - 2:
            grad_keys, feat_low = outer_rows(1, terms)
            done = (*done, feat_low)
            if len(step) > 1:
                grad_keys, feat_top = outer_rows(0, terms)
                done = (*done, feat_top)
        elif index == len(steps) - 3 and len(steps[-2]) == 1:
            grad_keys, feat_top = outer_rows(0, terms)
            done = (*done, feat_top)
        terms = total_of(parts)
        if done:
            terms = after(terms, done)
    own_terms, arriving = exchange(terms, steps[-1])
    grad_source, grad_target = call(
        image_kernel,
        "image",
        [shape(source.shape, BF16), shape(target.shape, BF16)],
        [scratch(asked, 8 + cols, LANES), scratch(channels * rows, cols)],
        after(own, terms),
        back,
        grad_keys,
        edge_keys,
        corner_keys,
        feat_early,
        feat_middle,
        feat_top,
        feat_low,
        edge_feat,
        corner_feat,
        cycles=2000,
    )
    pixels = rows * cols * lax.axis_size("row") * lax.axis_size("col")
    (grad_weight,) = call(
        functools.partial(final_kernel, 1.0 / math.sqrt(pixels)),
        "final",
        [shape((3, 3, CH, CH), F32)],
        [],
        own_terms,
        arriving,
        cycles=10,
    )
    return (grad_source, grad_target, grad_weight)


def solution(mesh):
    placed = (
        P(None, ("sec", "row"), "col"),
        P(None, ("sec", "row"), "col"),
        P(),
        P(None, ("sec", "row"), "col"),
    )
    return jax.shard_map(
        per_device,
        mesh=mesh,
        in_specs=placed,
        out_specs=(
            P(None, ("sec", "row"), "col"),
            P(None, ("sec", "row"), "col"),
            P("sec", None, None, None),
        ),
        check_vma=False,
    )
```
